512 devices in a mesh: seq: 32 (over x, y), row: 4 (over z_lo), col: 4 (over z_hi, core).
Axes of the slice: x: 4, y: 8, z: 8 (z_hi: 2, z_lo: 4; z = z_hi * 4 + z_lo), core: 2. Of those that a mesh axis runs over, the one named last changes fastest.
Arguments:
- hidden_in: bfloat16 [4096, 2048], P('seq', ('row', 'col')), may hold values from -6 to 6
- seg_ids: int32 [4096], replicated, may hold values from 0 to 7, never falling along the last dimension, each value on 1 to 2048 neighbouring positions
- norm_gain: float32 [2048], replicated, may hold values from 0.25 to 1.75
- w_query: bfloat16 [2048, 1024], P(None, 'row'), may hold values from -0.125 to 0.125
- w_key: bfloat16 [2048, 1024], P(None, 'row'), may hold values from -0.125 to 0.125
- w_value: bfloat16 [2048, 2048], P(None, ('row', 'col')), may hold values from -0.125 to 0.125
- w_gate: bfloat16 [2048, 2048], P(None, ('row', 'col')), may hold values from -0.125 to 0.125
- w_decay_down: bfloat16 [2048, 16], replicated, may hold values from -0.125 to 0.125
- w_decay_up: bfloat16 [16, 1024], P(None, 'row'), may hold values from -1.5 to 1.5
- decay_bias: float32 [1024], P('row'), may hold values from -2 to 12
- conv_query: float32 [4, 1024], P(None, 'row'), may hold values from -3 to 3
- conv_key: float32 [4, 1024], P(None, 'row'), may hold values from -3 to 3
- conv_value: float32 [4, 2048], P(None, ('row', 'col')), may hold values from -3 to 3
- head_gain: float32 [512], P('col'), may hold values from 0.25 to 1.75
- w_out: bfloat16 [2048, 2048], P(('row', 'col')), may hold values from -0.1875 to 0.1875
Outputs:
- mixed: bfloat16 [4096, 2048], P('seq', ('row', 'col'))
The draws below stay inside these ranges and needn't reach their ends.
Inputs may be any that keep to these rules, and one draw needn't show every extreme that they name: seg_ids never fall along the tokens; each of the 8 prompts holds 1 to 2048 consecutive tokens, and one holds exactly 2048.
All inputs are finite; a program needn't handle non-finite values.
Results may differ from the reference program's by a relative error of at most 0.014.
Values may be sent and summed in bfloat16 or wider, within the bound.
No kernel may reach another device: no remote copies, remote signals or barrier semaphores. Data moves between devices by JAX's collectives and lax.ppermute only.
A program may use at most 64 MiB of HBM per device.

```python
import math
import jax
import jax.numpy as jnp
import numpy as np
from jax import lax

D = 2048
HEADS = 4
HEAD_K = 256
HEAD_V = 512
RANK = 16
KERNEL = 4
SPAN = 64
TOKENS = 4096
KEYS = 1024
VALUES = 2048
PROMPTS = 8
LONGEST = 2048


def raised(drawn, stream_key, source, target, shards_of, factor):
    owner, partner = [(jnp.arange(drawn.shape[axis_at]) // (drawn.shape[axis_at] // shards_of)).reshape([-1 if axis == axis_at else 1 for axis in range(drawn.ndim)]) for axis_at in (source, target)]
    chosen = jax.random.permutation(stream_key, shards_of)[partner]
    strong = (owner == chosen) | (owner == (partner + shards_of // 2) % shards_of)
    return jnp.where(strong, factor * drawn, drawn)


def block_scale(stream_key, shape, cuts, low, largest):
    level = 1.0
    for dim, blocks in cuts:
        draws = jax.random.uniform(jax.random.fold_in(jax.random.fold_in(stream_key, 6), dim), (blocks,), jnp.float32, low / len(cuts), largest / len(cuts))
        level = level * jnp.repeat(jnp.exp(draws), shape[dim] // blocks).reshape((-1,) + (1,) * (len(shape) - 1 - dim))
    return level


def split_up(count, total, most, skew):
    loads = [(1 << 20) // math.isqrt(standing ** skew) + 1 for standing in range(2, count + 1)]
    surplus, given = total - most - (count - 1), [1] * (count - 1)
    while surplus > 0:
        free = [i for i in range(count - 1) if given[i] < most]
        mass, budget = sum([loads[i] for i in free]), surplus
        for i in free:
            extra = min(most - given[i], max(1, budget * loads[i] // mass), surplus)
            given[i] = given[i] + extra
            surplus = surplus - extra
    return np.array([most] + given)


def ragged_sizes(rng, number_of, total, limit, slope):
    if number_of == 2:
        one = jax.random.randint(rng, (), max(1, total - limit), min(limit, total - 1) + 1)
        return jnp.stack([one, total - one])
    tallies = jnp.asarray(split_up(number_of, total, limit, slope), jnp.int32)
    twos = (number_of - 1) // 2
    source_of, receiver = tallies[1:1 + 2 * twos:2], tallies[2:2 + 2 * twos:2]
    margin = jnp.minimum(source_of - 1, limit - receiver)
    shifted = jax.random.randint(jax.random.fold_in(rng, 1), (twos,), 0, 1 << 20) % (margin + 1)
    tallies = tallies.at[1:1 + 2 * twos:2].set(source_of - shifted).at[2:2 + 2 * twos:2].set(receiver + shifted)
    return tallies[jax.random.permutation(jax.random.fold_in(rng, 2), number_of)]


def noise(key, dims, deviation, bound, split=(), kind=jnp.bfloat16):
    gain = block_scale(key, dims, split, -0.22, 0.18) if split else 1.0
    drawn = jax.random.normal(key, dims, jnp.float32) * deviation * gain
    return jnp.minimum(jnp.maximum(drawn, -bound), bound).astype(kind)


def bell_draw_with(rng, shape, scale, limit, shards, heavy, kind=jnp.bfloat16):
    result = scale * jax.random.normal(rng, shape, jnp.float32)
    if shards:
        result = result * block_scale(rng, shape, shards, -0.22, 0.18)
    return jnp.clip(raised(result, jax.random.fold_in(rng, 3), *heavy), -limit, limit).astype(kind)


def setup_inputs(seed: int = 0) -> dict:
    arg_keys = jax.random.split(jax.random.key(seed), 16)
    return {
        "hidden_in": noise(arg_keys[0], (TOKENS, D), 1.0, 6.0, ((0, 32), (1, 16))),
        "seg_ids": jnp.searchsorted(jnp.cumsum(ragged_sizes(arg_keys[1], PROMPTS, TOKENS, LONGEST, 2)), jnp.arange(TOKENS), side="right").astype(jnp.int32),
        "norm_gain": jnp.clip(1.0 + 0.15 * jax.random.normal(arg_keys[2], (D,), jnp.float32), 0.25, 1.75),
        "w_query": noise(arg_keys[3], (D, KEYS), D ** -0.5, 0.125, ((1, 4),)),
        "w_key": noise(arg_keys[4], (D, KEYS), D ** -0.5, 0.125, ((1, 4),)),
        "w_value": noise(arg_keys[5], (D, VALUES), D ** -0.5, 0.125, ((1, 16),)),
        "w_gate": noise(arg_keys[6], (D, VALUES), D ** -0.5, 0.125, ((1, 16),)),
        "w_decay_down": noise(arg_keys[7], (D, RANK), D ** -0.5, 0.125),
        "w_decay_up": noise(arg_keys[8], (RANK, KEYS), RANK ** -0.5, 1.5, ((1, 4),)),
        "decay_bias": jnp.clip(-2.0 + 14.0 * jax.random.uniform(arg_keys[9], (KEYS,), jnp.float32) ** block_scale(arg_keys[9], (KEYS,), ((0, 4),), -0.2, 0.2), -2.0, 12.0),
        "conv_query": noise(arg_keys[10], (KERNEL, KEYS), KERNEL ** -0.5, 3.0, ((1, 4),), jnp.float32),
        "conv_key": noise(arg_keys[11], (KERNEL, KEYS), KERNEL ** -0.5, 3.0, ((1, 4),), jnp.float32),
        "conv_value": noise(arg_keys[12], (KERNEL, VALUES), KERNEL ** -0.5, 3.0, ((1, 16),), jnp.float32),
        "head_gain": jnp.clip(1.0 + 0.15 * jax.random.normal(arg_keys[13], (HEAD_V,), jnp.float32), 0.25, 1.75),
        "w_out": bell_draw_with(arg_keys[14], (VALUES, D), VALUES ** -0.5, 0.1875, ((0, 16),), (0, 1, 16, 2.0)),
    }


highest = lax.Precision.HIGHEST

def span_step(state, queries, keys_c, values_c, log_decay, segments, seg_before):
    width = segments.shape[0]
    cumulated = jnp.cumsum(log_decay, axis=0)
    row_iota = lax.broadcasted_iota(jnp.int32, (width, width), 0)
    col_iota = lax.broadcasted_iota(jnp.int32, (width, width), 1)
    visible = (segments[:, None] == segments[None, :]) & (row_iota >= col_iota)
    spread = jnp.minimum(cumulated[:, None, :] - cumulated[None, :, :], 0.0)
    weights = lax.optimization_barrier(jnp.sum(queries[:, None, :] * keys_c[None, :, :] * jnp.exp(spread), axis=2))
    weights = jnp.where(visible, weights, 0.0)
    carried = (segments == seg_before)[:, None]
    reach = jnp.where(carried, queries * jnp.exp(cumulated), 0.0)
    outputs = jnp.dot(weights, values_c, precision=highest) + jnp.dot(reach, state, precision=highest)
    final = cumulated[-1]
    tail = (segments == segments[-1])[:, None]
    pushed = jnp.where(tail, keys_c * jnp.exp(final[None, :] - cumulated), 0.0)
    keep = jnp.where(segments[-1] == seg_before, jnp.exp(final), 0.0)
    state_new = state * keep[:, None] + jnp.einsum('ck,cv->kv', pushed, values_c, precision=highest)
    return (state_new, outputs, cumulated)

def short_conv(extended, kernel, seg_ext, segments):
    length = segments.shape[0]
    taps = kernel.shape[0]
    total = jnp.zeros((length, extended.shape[1]), jnp.float32)
    for j in range(taps):
        offset = taps - 1 - j
        same = (seg_ext[offset:offset + length] == segments)[:, None]
        total = total + jnp.where(same, kernel[j][None, :] * extended[offset:offset + length], 0.0)
    return total

def reference(hidden_in, seg_ids, norm_gain, w_query, w_key, w_value, w_gate, w_decay_down, w_decay_up, decay_bias, conv_query, conv_key, conv_value, head_gain, w_out):
    activ = hidden_in.astype(jnp.float32)
    normed = (activ * lax.rsqrt(lax.optimization_barrier(jnp.mean(activ * activ, axis=1, keepdims=True)) + 1e-06) * norm_gain).astype(jnp.bfloat16)
    query_pre = jnp.dot(normed, w_query, preferred_element_type=jnp.float32)
    key_pre = jnp.dot(normed, w_key, preferred_element_type=jnp.float32)
    value_pre = jnp.dot(normed, w_value, preferred_element_type=jnp.float32)
    gate_pre = jnp.dot(normed, w_gate, preferred_element_type=jnp.float32)
    rank_part = jnp.dot(normed, w_decay_down, preferred_element_type=jnp.float32)
    log_decay = jax.nn.log_sigmoid(jnp.dot(rank_part, w_decay_up.astype(jnp.float32), precision=highest) + decay_bias) / 16.0
    padding = jnp.full((KERNEL - 1,), -1, jnp.int32)
    seg_ext = jnp.concatenate([padding, seg_ids.astype(jnp.int32)])
    stacked = jnp.concatenate([query_pre, key_pre, value_pre], axis=1)
    extended = jnp.concatenate([jnp.zeros((KERNEL - 1, stacked.shape[1]), jnp.float32), stacked], axis=0)
    kernel = jnp.concatenate([conv_query, conv_key, conv_value], axis=1)
    mixed_in = jax.nn.silu(short_conv(extended, kernel, seg_ext, seg_ids))
    queries = mixed_in[:, :KEYS] * HEAD_K ** (-0.5)
    keys_all = mixed_in[:, KEYS:2 * KEYS]
    values_all = mixed_in[:, 2 * KEYS:]
    blocks = TOKENS // SPAN
    seg_blocks = seg_ids.reshape(blocks, SPAN)
    befores = seg_ext[KERNEL - 2:KERNEL - 2 + TOKENS:SPAN]

    def per_head(head):
        q_head = lax.dynamic_slice_in_dim(queries, head * HEAD_K, HEAD_K, 1).reshape(blocks, SPAN, HEAD_K)
        k_head = lax.dynamic_slice_in_dim(keys_all, head * HEAD_K, HEAD_K, 1).reshape(blocks, SPAN, HEAD_K)
        g_head = lax.dynamic_slice_in_dim(log_decay, head * HEAD_K, HEAD_K, 1).reshape(blocks, SPAN, HEAD_K)
        v_head = lax.dynamic_slice_in_dim(values_all, head * HEAD_V, HEAD_V, 1).reshape(blocks, SPAN, HEAD_V)

        def advance(state, pieces):
            state_new, outputs, cumulated = span_step(state, pieces[0], pieces[1], pieces[2], pieces[3], pieces[4], pieces[5])
            return (state_new, outputs)
        start_state = jnp.zeros((HEAD_K, HEAD_V), jnp.float32)
        final_state, outputs = lax.scan(advance, start_state, (q_head, k_head, v_head, g_head, seg_blocks, befores))
        return outputs.reshape(TOKENS, HEAD_V)
    per_heads = lax.map(per_head, jnp.arange(HEADS, dtype=jnp.int32))
    stat = lax.optimization_barrier(jnp.mean(per_heads * per_heads, axis=2, keepdims=True))
    normalized = per_heads * lax.rsqrt(stat + 1e-05) * head_gain
    normalized = jnp.transpose(normalized, (1, 0, 2)).reshape(TOKENS, VALUES)
    gated = (normalized * jax.nn.silu(gate_pre)).astype(jnp.bfloat16)
    attn = jnp.dot(gated, w_out, preferred_element_type=jnp.float32)
    return (activ + attn).astype(jnp.bfloat16)
```

```python
import jax
import jax.numpy as jnp
from jax import lax
from jax.experimental import pallas as pl
from jax.experimental.pallas import tpu as pltpu
from jax.sharding import Mesh, PartitionSpec as P

F32 = jnp.float32
BF16 = jnp.bfloat16
HIGHEST = lax.Precision.HIGHEST
HEAD_V = 512
WIDTH = 2048
BLOCK = 128
HEAD_K = 256
CHUNK = 128
LAST = (((1,), (1,)), ((), ()))
FIRST = (((0,), (0,)), ((), ()))

SEQ = ("x", "y")
CHIPS = ("row", "zhi")
ROWS_X, ROWS_Y = 4, 8
PIECE = BLOCK // ROWS_Y


def local_call(kernel, outs, *args, scratch=(), scalars=0):
    vmem = pl.BlockSpec(memory_space=pltpu.VMEM)
    smem = pl.BlockSpec(memory_space=pltpu.SMEM)
    return pl.pallas_call(
        kernel,
        out_shape=[jax.ShapeDtypeStruct(s, t) for s, t in outs],
        in_specs=[smem] * scalars + [vmem] * (len(args) - scalars),
        out_specs=[vmem] * len(outs),
        scratch_shapes=list(scratch),
        name=kernel.__name__,
    )(*args)


def dot(a, b, dims=(((1,), (0,)), ((), ())), precision=None):
    return lax.dot_general(a, b, dims, precision=precision, preferred_element_type=F32)


def halves(value):
    high = value.astype(BF16)
    return high, (value - high.astype(F32)).astype(BF16)


def pair_rows(value):
    high, low = halves(value)
    shape = (8, value.shape[1])
    index = lax.broadcasted_iota(jnp.int32, shape, 0)
    both = jnp.where(
        index == 0,
        jnp.broadcast_to(high.astype(F32), shape),
        jnp.where(index == 1, jnp.broadcast_to(low.astype(F32), shape), 0.0),
    )
    return both.astype(BF16)


def silu(value):
    return value * jax.nn.sigmoid(value)


def project(
    whole, gain, w_query, w_key, w_value, w_gate, w_down, pre, gate_pre, rank_part, normed
):
    chunks = WIDTH // CHUNK
    squares = jnp.zeros((BLOCK, CHUNK), F32)
    for f in range(chunks):
        activ = whole[f % 2, f // 2].astype(F32)
        squares = squares + activ * activ
    scale = lax.rsqrt(jnp.sum(squares, axis=1, keepdims=True) / WIDTH + 1e-06)
    for f in range(chunks):
        span = slice(f * CHUNK, (f + 1) * CHUNK)
        activ = whole[f % 2, f // 2].astype(F32)
        normed[:, span] = (activ * scale * gain[:, span]).astype(BF16)
    rows = normed[...]
    pre[:, :HEAD_K] = dot(rows, w_query[...])
    pre[:, HEAD_K : 2 * HEAD_K] = dot(rows, w_key[...])
    pre[:, 2 * HEAD_K :] = dot(rows, w_value[...])
    gate_pre[...] = dot(rows, w_gate[...])
    rank_part[...] = dot(rows, w_down[...])


def gates(
    index, rank_part, w_up, bias, gate_pre, head_gain, seg_ids, cumulated, gate, columns, own_rows
):
    logits = dot(rank_part[...], w_up[...].astype(F32), precision=HIGHEST) + bias[...]
    log_decay = (jnp.minimum(logits, 0.0) - jnp.log(1.0 + jnp.exp(-jnp.abs(logits)))) / 16.0
    row_iota = lax.broadcasted_iota(jnp.int32, (BLOCK, BLOCK), 0)
    col_iota = lax.broadcasted_iota(jnp.int32, (BLOCK, BLOCK), 1)
    lower = jnp.where(row_iota >= col_iota, 1.0, 0.0).astype(F32)
    cumulated[...] = dot(lower, log_decay, precision=HIGHEST)
    gate[...] = silu(gate_pre[...]) * head_gain[...]
    at = index[0]
    own = seg_ids[pl.ds(at, 1), :].astype(F32)
    before = seg_ids[pl.ds(jnp.maximum(at - 1, 0), 1), :].astype(F32)
    before = jnp.where(at > 0, before, -1.0)
    own = jnp.broadcast_to(own, (8, BLOCK))
    before = jnp.broadcast_to(before, (8, BLOCK))
    lane = lax.broadcasted_iota(jnp.int32, (8, BLOCK), 1)
    parts = [own]
    for j in range(1, 4):
        parts.append(jnp.where(lane < j, pltpu.roll(before, j, 1), pltpu.roll(own, j, 1)))
    parts.append(jnp.broadcast_to(before[:, BLOCK - 1 :], (8, BLOCK)))
    parts.append(jnp.broadcast_to(own[:, BLOCK - 1 :], (8, BLOCK)))
    parts.append(jnp.zeros((BLOCK - 8 * len(parts), BLOCK), F32))
    columns[...] = jnp.transpose(jnp.concatenate(parts, axis=0))
    own_rows[...] = own


def span(
    pre, edge, taps_q, taps_k, taps_v, cumulated, columns, own_rows, intra, reach, pieces, extended
):
    extended[0:8, :] = edge[...]
    extended[8:, :] = pre[...]
    seg = columns[:, 0:1]

    def conv(lanes, taps):
        total = taps[0:1, :] * extended[8:, lanes]
        for j in range(1, 4):
            same = columns[:, 8 * j : 8 * j + 1] == seg
            total = total + jnp.where(
                same, taps[j : j + 1, :] * extended[8 - j : 8 - j + BLOCK, lanes], 0.0
            )
        return silu(total)

    queries = conv(slice(0, HEAD_K), taps_q) * HEAD_K ** (-0.5)
    keys = conv(slice(HEAD_K, 2 * HEAD_K), taps_k)
    values = conv(slice(2 * HEAD_K, 2 * HEAD_K + CHUNK), taps_v)
    cum = cumulated[...]
    row_iota = lax.broadcasted_iota(jnp.int32, (BLOCK, BLOCK), 0)
    col_iota = lax.broadcasted_iota(jnp.int32, (BLOCK, BLOCK), 1)
    weights = jnp.zeros((BLOCK, BLOCK), F32)
    for half in (8, 16, 32, 64):
        anchors = [
            jnp.broadcast_to(cum[b + half - 1 : b + half, :], (2 * half, HEAD_K))
            for b in range(0, BLOCK, 2 * half)
        ]
        anchor = jnp.concatenate(anchors, axis=0) if len(anchors) > 1 else anchors[0]
        factor = jnp.exp(-jnp.abs(cum - anchor))
        part = dot((queries * factor).astype(BF16), (keys * factor).astype(BF16), LAST)
        inside = (
            (row_iota // (2 * half) == col_iota // (2 * half))
            & (row_iota % (2 * half) >= half)
            & (col_iota % (2 * half) < half)
        )
        weights = jnp.where(inside, part, weights)
    groups = (BLOCK // 8, 8, HEAD_K)
    cum_g, keys_g = cum.reshape(groups), keys.reshape(groups)
    queries_g = queries.reshape(groups)
    for by in range(8):
        if by:
            spread = jnp.minimum(cum_g - pltpu.roll(cum_g, by, 1), 0.0)
            product = queries_g * pltpu.roll(keys_g, by, 1) * jnp.exp(spread)
        else:
            product = queries_g * keys_g
        sums = jnp.sum(product.reshape(BLOCK, HEAD_K), axis=1, keepdims=True)
        inside = (row_iota - col_iota == by) & (row_iota % 8 >= by)
        weights = jnp.where(inside, sums, weights)
    visible = (seg == own_rows[0:1, :]) & (row_iota >= col_iota)
    weights = jnp.where(visible, weights, 0.0)
    values_b = values.astype(BF16)
    intra[...] = dot(weights.astype(BF16), values_b)
    before, last = columns[:, 32:33], columns[:, 40:41]
    reach[...] = jnp.where(seg == before, queries * jnp.exp(cum), 0.0)
    final = cum[BLOCK - 1 :, :]
    pushed = jnp.where(seg == last, keys * jnp.exp(final - cum), 0.0)
    state = dot(values_b, pushed.astype(BF16), FIRST)
    keep = jnp.where(before[0:1, :] == last[0:1, :], jnp.exp(final), 0.0)
    keep_rows = pair_rows(keep)
    for j in range(ROWS_Y):
        pieces[j, 0:PIECE, :] = state[j * PIECE : (j + 1) * PIECE, :].astype(BF16)
        pieces[j, PIECE:, :] = keep_rows


def row_scan(pieces, entering, kept, totals):
    state = jnp.zeros((PIECE, HEAD_K), F32)
    keep = jnp.ones((1, HEAD_K), F32)
    for j in range(ROWS_Y):
        entering[j] = state
        kept[j] = jnp.broadcast_to(keep, (8, HEAD_K))
        pair = pieces[j, PIECE:, :].astype(F32)
        decay = pair[0:1, :] + pair[1:2, :]
        state = state * decay + pieces[j, 0:PIECE, :].astype(F32)
        keep = keep * decay
    totals[0:PIECE, :] = state
    totals[PIECE:, :] = jnp.broadcast_to(keep, (8, HEAD_K))


def carry(entering, kept, one_back, two_back, states):
    arriving = one_back[0:PIECE, :] + one_back[PIECE : PIECE + 1, :] * two_back[0:PIECE, :]
    for j in range(ROWS_Y):
        states[j] = (entering[j] + kept[j, 0:1, :] * arriving).astype(BF16)


def attend(index, intra, reach, incoming, gate, w_out, kept, kept_squares, sent):
    high, low = halves(reach[...])
    state = incoming[...]
    attended = intra[...] + dot(high, state, LAST) + dot(low, state, LAST)
    squares = dot(jnp.ones((8, CHUNK), F32), attended * attended, LAST, precision=HIGHEST)
    terms = dot((attended * gate[...]).astype(BF16), w_out[...])
    first = index[0] == 0
    for j in range(8):
        even = terms[:, (2 * j) * CHUNK : (2 * j + 1) * CHUNK]
        odd = terms[:, (2 * j + 1) * CHUNK : (2 * j + 2) * CHUNK]
        kept[j] = jnp.where(first, even, odd)
        sent[j * BLOCK : (j + 1) * BLOCK, :] = jnp.where(first, odd, even).astype(BF16)
    kept_squares[...] = squares
    sent[8 * BLOCK :, :] = pair_rows(squares[0:1, :])


def pair_sum(kept, kept_squares, received, sent):
    other = received[8 * BLOCK :, :].astype(F32)
    squares = pair_rows(kept_squares[0:1, :] + other[0:1, :] + other[1:2, :])
    for j in range(8):
        terms = kept[j] + received[j * BLOCK : (j + 1) * BLOCK, :].astype(F32)
        sent[j, 0:BLOCK, :] = terms.astype(BF16)
        sent[j, BLOCK:, :] = squares


def finish(received, hidden, mixed):
    parts = []
    for r in range(4):
        pair = received[2 * r, BLOCK:, :].astype(F32) + received[2 * r + 1, BLOCK:, :].astype(F32)
        squares = pair[0:1, :] + pair[1:2, :]
        scale = lax.rsqrt(squares / HEAD_V + 1e-05)
        parts.append(jnp.broadcast_to(scale, (8, BLOCK)))
    parts.append(jnp.zeros((BLOCK - 8 * len(parts), BLOCK), F32))
    columns = jnp.transpose(jnp.concatenate(parts, axis=0))
    total = hidden[...].astype(F32)
    for r in range(4):
        terms = received[2 * r, 0:BLOCK, :].astype(F32)
        terms = terms + received[2 * r + 1, 0:BLOCK, :].astype(F32)
        total = total + columns[:, 8 * r : 8 * r + 1] * terms
    mixed[...] = total.astype(BF16)


def shards(
    hidden_in,
    seg_ids,
    norm_gain,
    w_query,
    w_key,
    w_value,
    w_gate,
    w_decay_down,
    w_decay_up,
    decay_bias,
    conv_query,
    conv_key,
    conv_value,
    head_gain,
    w_out,
):
    block = lax.axis_index("x") * ROWS_Y + lax.axis_index("y")
    block_at = jnp.reshape(block, (1,)).astype(jnp.int32)
    core_at = jnp.reshape(lax.axis_index("core"), (1,)).astype(jnp.int32)
    blocks = ROWS_X * ROWS_Y

    copies = jnp.broadcast_to(hidden_in[None], (8, BLOCK, CHUNK))
    of_core = lax.all_to_all(copies, CHIPS, 0, 0)
    whole = lax.all_gather(of_core, "core", axis=0)

    pre, gate_pre, rank_part = local_call(
        project,
        [((BLOCK, 2 * HEAD_K + CHUNK), F32), ((BLOCK, CHUNK), F32), ((BLOCK, 16), F32)],
        whole,
        norm_gain.reshape(1, WIDTH),
        w_query,
        w_key,
        w_value,
        w_gate,
        w_decay_down,
        scratch=[pltpu.VMEM((BLOCK, WIDTH), BF16)],
    )
    edge = lax.ppermute(pre[BLOCK - 8 :], SEQ, [(i, i + 1) for i in range(blocks - 1)])
    cumulated, gate, columns, own_rows = local_call(
        gates,
        [
            ((BLOCK, HEAD_K), F32),
            ((BLOCK, CHUNK), F32),
            ((BLOCK, BLOCK), F32),
            ((8, BLOCK), F32),
        ],
        block_at,
        rank_part,
        w_decay_up,
        decay_bias.reshape(1, HEAD_K),
        gate_pre,
        head_gain.reshape(1, CHUNK),
        seg_ids.reshape(blocks, BLOCK),
        scalars=1,
    )
    intra, reach, pieces = local_call(
        span,
        [
            ((BLOCK, CHUNK), F32),
            ((BLOCK, HEAD_K), F32),
            ((ROWS_Y, PIECE + 8, HEAD_K), BF16),
        ],
        pre,
        edge,
        conv_query,
        conv_key,
        conv_value,
        cumulated,
        columns,
        own_rows,
        scratch=[pltpu.VMEM((BLOCK + 8, 2 * HEAD_K + CHUNK), F32)],
    )
    entering, kept, totals = local_call(
        row_scan,
        [
            ((ROWS_Y, PIECE, HEAD_K), F32),
            ((ROWS_Y, 8, HEAD_K), F32),
            ((PIECE + 8, HEAD_K), F32),
        ],
        lax.all_to_all(pieces, "y", 0, 0),
    )
    one_back = lax.ppermute(totals, "x", [(i, i + 1) for i in range(ROWS_X - 1)])
    two_back = lax.ppermute(totals, "x", [(i, i + 2) for i in range(ROWS_X - 2)])
    (states,) = local_call(
        carry, [((ROWS_Y, PIECE, HEAD_K), BF16)], entering, kept, one_back, two_back
    )
    incoming = lax.all_to_all(states, "y", 0, 0).reshape(CHUNK, HEAD_K)
    mine, my_squares, sent = local_call(
        attend,
        [((8, BLOCK, CHUNK), F32), ((8, BLOCK), F32), ((8 * BLOCK + 8, CHUNK), BF16)],
        core_at,
        intra,
        reach,
        incoming,
        gate,
        w_out,
        scalars=1,
    )
    theirs = lax.ppermute(sent, "core", [(0, 1), (1, 0)])
    (pairs,) = local_call(
        pair_sum, [((8, BLOCK + 8, CHUNK), BF16)], mine, my_squares, theirs
    )
    arrived = lax.all_to_all(pairs, CHIPS, 0, 0)
    (mixed,) = local_call(finish, [((BLOCK, CHUNK), BF16)], arrived, hidden_in)
    return mixed


def solution(mesh):
    finer = Mesh(mesh.devices.reshape(ROWS_X, ROWS_Y, 4, 2, 2), ("x", "y", "row", "zhi", "core"))
    part = ("row", "zhi", "core")
    return jax.shard_map(
        shards,
        mesh=finer,
        in_specs=(
            P(SEQ, part),
            P(),
            P(),
            P(None, "row"),
            P(None, "row"),
            P(None, part),
            P(None, part),
            P(),
            P(None, "row"),
            P("row"),
            P(None, "row"),
            P(None, "row"),
            P(None, part),
            P(("zhi", "core")),
            P(part, None),
        ),
        out_specs=P(SEQ, part),
        check_vma=False,
    )
```

```python
import jax
import jax.numpy as jnp
from jax import lax
from jax.experimental import pallas as pl
from jax.experimental.pallas import tpu as pltpu
from jax.sharding import Mesh, PartitionSpec as P

F32 = jnp.float32
BF16 = jnp.bfloat16
HIGHEST = lax.Precision.HIGHEST
HEAD_V = 512
WIDTH = 2048
BLOCK = 128
HEAD_K = 256
CHUNK = 128
LAST = (((1,), (1,)), ((), ()))
FIRST = (((0,), (0,)), ((), ()))

SEQ = ("x", "y")
CHIPS = ("row", "zhi")
ROWS_X, ROWS_Y = 4, 8
PIECE = BLOCK // ROWS_Y


def local_call(kernel, outs, *args, scratch=(), scalars=0, plain=(), last=False):
    vmem = pl.BlockSpec(memory_space=pltpu.VMEM)
    smem = pl.BlockSpec(memory_space=pltpu.SMEM)
    args = [
        a if i < scalars or i in plain else pltpu.with_memory_space_constraint(a, pltpu.VMEM)
        for i, a in enumerate(args)
    ]
    return pl.pallas_call(
        kernel,
        out_shape=[jax.ShapeDtypeStruct(s, t) if last else pltpu.VMEM(s, t) for s, t in outs],
        in_specs=[smem] * scalars + [vmem] * (len(args) - scalars),
        out_specs=[vmem] * len(outs),
        scratch_shapes=list(scratch),
        name=kernel.__name__,
        compiler_params=pltpu.CompilerParams(vmem_limit_bytes=16 << 20),
    )(*args)


def dot(a, b, dims=(((1,), (0,)), ((), ())), precision=None):
    return lax.dot_general(a, b, dims, precision=precision, preferred_element_type=F32)


def halves(value):
    high = value.astype(BF16)
    return high, (value - high.astype(F32)).astype(BF16)


def pair_rows(value):
    high, low = halves(value)
    shape = (8, value.shape[1])
    index = lax.broadcasted_iota(jnp.int32, shape, 0)
    both = jnp.where(
        index == 0,
        jnp.broadcast_to(high.astype(F32), shape),
        jnp.where(index == 1, jnp.broadcast_to(low.astype(F32), shape), 0.0),
    )
    return both.astype(BF16)


def silu(value):
    return value * jax.nn.sigmoid(value)


def spread_out(hidden, copies):
    for j in range(8):
        copies[j] = hidden[...]


def project(
    whole, gain, w_query, w_key, w_value, w_gate, w_down, pre, tail, gate_pre, rank_part, normed
):
    chunks = WIDTH // CHUNK
    squares = jnp.zeros((BLOCK, CHUNK), F32)
    for f in range(chunks):
        activ = whole[f % 2, f // 2].astype(F32)
        squares = squares + activ * activ
    scale = lax.rsqrt(jnp.sum(squares, axis=1, keepdims=True) / WIDTH + 1e-06)
    for f in range(chunks):
        span = slice(f * CHUNK, (f + 1) * CHUNK)
        activ = whole[f % 2, f // 2].astype(F32)
        normed[:, span] = (activ * scale * gain[:, span]).astype(BF16)
    rows = normed[...]
    pre[:, :HEAD_K] = dot(rows, w_query[...])
    pre[:, HEAD_K : 2 * HEAD_K] = dot(rows, w_key[...])
    pre[:, 2 * HEAD_K :] = dot(rows, w_value[...])
    tail[...] = pre[BLOCK - 8 :, :]
    gate_pre[...] = dot(rows, w_gate[...])
    rank_part[...] = dot(rows, w_down[...], LAST)


def gates(
    index, rank_part, w_up, bias, gate_pre, head_gain, seg_ids, cumulated, gate, columns, own_rows
):
    logits = dot(rank_part[...], w_up[...].astype(F32), precision=HIGHEST) + bias[...]
    log_decay = (jnp.minimum(logits, 0.0) - jnp.log(1.0 + jnp.exp(-jnp.abs(logits)))) / 16.0
    row_iota = lax.broadcasted_iota(jnp.int32, (BLOCK, BLOCK), 0)
    col_iota = lax.broadcasted_iota(jnp.int32, (BLOCK, BLOCK), 1)
    lower = jnp.where(row_iota >= col_iota, 1.0, 0.0).astype(F32)
    cumulated[...] = dot(lower, log_decay, precision=HIGHEST)
    gate[...] = silu(gate_pre[...]) * head_gain[...]
    at = index[0]
    own = seg_ids[pl.ds(at, 1), :].astype(F32)
    before = seg_ids[pl.ds(jnp.maximum(at - 1, 0), 1), :].astype(F32)
    before = jnp.where(at > 0, before, -1.0)
    own = jnp.broadcast_to(own, (8, BLOCK))
    before = jnp.broadcast_to(before, (8, BLOCK))
    lane = lax.broadcasted_iota(jnp.int32, (8, BLOCK), 1)
    parts = [own]
    for j in range(1, 4):
        parts.append(jnp.where(lane < j, pltpu.roll(before, j, 1), pltpu.roll(own, j, 1)))
    parts.append(jnp.broadcast_to(before[:, BLOCK - 1 :], (8, BLOCK)))
    parts.append(jnp.broadcast_to(own[:, BLOCK - 1 :], (8, BLOCK)))
    parts.append(jnp.zeros((BLOCK - 8 * len(parts), BLOCK), F32))
    columns[...] = jnp.transpose(jnp.concatenate(parts, axis=0))
    own_rows[...] = own


def span(
    pre, edge, taps_q, taps_k, taps_v, cumulated, columns, own_rows, intra, reach, pieces, extended
):
    extended[0:8, :] = edge[...]
    extended[8:, :] = pre[...]
    seg = columns[:, 0:1]

    def conv(lanes, taps):
        total = taps[0:1, :] * extended[8:, lanes]
        for j in range(1, 4):
            same = columns[:, 8 * j : 8 * j + 1] == seg
            total = total + jnp.where(
                same, taps[j : j + 1, :] * extended[8 - j : 8 - j + BLOCK, lanes], 0.0
            )
        return silu(total)

    queries = conv(slice(0, HEAD_K), taps_q) * HEAD_K ** (-0.5)
    keys = conv(slice(HEAD_K, 2 * HEAD_K), taps_k)
    values = conv(slice(2 * HEAD_K, 2 * HEAD_K + CHUNK), taps_v)
    cum = cumulated[...]
    row_iota = lax.broadcasted_iota(jnp.int32, (BLOCK, BLOCK), 0)
    col_iota = lax.broadcasted_iota(jnp.int32, (BLOCK, BLOCK), 1)
    weights = jnp.zeros((BLOCK, BLOCK), F32)
    for half in (8, 16, 32, 64):
        anchors = [
            jnp.broadcast_to(cum[b + half - 1 : b + half, :], (2 * half, HEAD_K))
            for b in range(0, BLOCK, 2 * half)
        ]
        anchor = jnp.concatenate(anchors, axis=0) if len(anchors) > 1 else anchors[0]
        factor = jnp.exp(-jnp.abs(cum - anchor))
        part = dot((queries * factor).astype(BF16), (keys * factor).astype(BF16), LAST)
        inside = (
            (row_iota // (2 * half) == col_iota // (2 * half))
            & (row_iota % (2 * half) >= half)
            & (col_iota % (2 * half) < half)
        )
        weights = jnp.where(inside, part, weights)
    groups = (BLOCK // 8, 8, HEAD_K)
    cum_g, keys_g = cum.reshape(groups), keys.reshape(groups)
    queries_g = queries.reshape(groups)
    for by in range(8):
        if by:
            spread = jnp.minimum(cum_g - pltpu.roll(cum_g, by, 1), 0.0)
            product = queries_g * pltpu.roll(keys_g, by, 1) * jnp.exp(spread)
        else:
            product = queries_g * keys_g
        sums = jnp.sum(product.reshape(BLOCK, HEAD_K), axis=1, keepdims=True)
        inside = (row_iota - col_iota == by) & (row_iota % 8 >= by)
        weights = jnp.where(inside, sums, weights)
    visible = (seg == own_rows[0:1, :]) & (row_iota >= col_iota)
    weights = jnp.where(visible, weights, 0.0)
    values_b = values.astype(BF16)
    intra[...] = dot(weights.astype(BF16), values_b)
    before, last = columns[:, 32:33], columns[:, 40:41]
    reach[...] = jnp.where(seg == before, queries * jnp.exp(cum), 0.0)
    final = cum[BLOCK - 1 :, :]
    pushed = jnp.where(seg == last, keys * jnp.exp(final - cum), 0.0)
    state = dot(values_b, pushed.astype(BF16), FIRST)
    keep = jnp.where(before[0:1, :] == last[0:1, :], jnp.exp(final), 0.0)
    keep_rows = pair_rows(keep)
    for j in range(ROWS_Y):
        pieces[j, 0:PIECE, :] = state[j * PIECE : (j + 1) * PIECE, :].astype(BF16)
        pieces[j, PIECE:, :] = keep_rows


def row_scan(pieces, entering, kept, totals):
    state = jnp.zeros((PIECE, HEAD_K), F32)
    keep = jnp.ones((1, HEAD_K), F32)
    for j in range(ROWS_Y):
        entering[j] = state
        kept[j] = jnp.broadcast_to(keep, (8, HEAD_K))
        pair = pieces[j, PIECE:, :].astype(F32)
        decay = pair[0:1, :] + pair[1:2, :]
        state = state * decay + pieces[j, 0:PIECE, :].astype(F32)
        keep = keep * decay
    totals[0:PIECE, :] = state
    totals[PIECE:, :] = jnp.broadcast_to(keep, (8, HEAD_K))


def carry(entering, kept, one_back, two_back, states):
    arriving = one_back[0:PIECE, :] + one_back[PIECE : PIECE + 1, :] * two_back[0:PIECE, :]
    for j in range(ROWS_Y):
        states[j] = (entering[j] + kept[j, 0:1, :] * arriving).astype(BF16)


def attend(index, intra, reach, incoming, gate, w_out, kept, kept_squares, sent):
    high, low = halves(reach[...])
    state = incoming[...]
    attended = intra[...] + dot(high, state, LAST) + dot(low, state, LAST)
    squares = dot(jnp.ones((8, CHUNK), F32), attended * attended, LAST, precision=HIGHEST)
    terms = dot((attended * gate[...]).astype(BF16), w_out[...])
    first = index[0] == 0
    for j in range(8):
        even = terms[:, (2 * j) * CHUNK : (2 * j + 1) * CHUNK]
        odd = terms[:, (2 * j + 1) * CHUNK : (2 * j + 2) * CHUNK]
        kept[j] = jnp.where(first, even, odd)
        sent[j * BLOCK : (j + 1) * BLOCK, :] = jnp.where(first, odd, even).astype(BF16)
    kept_squares[...] = squares
    sent[8 * BLOCK :, :] = pair_rows(squares[0:1, :])


def pair_sum(index, kept, kept_squares, both, sent):
    received = both.at[1 - index[0]]
    other = received[8 * BLOCK :, :].astype(F32)
    squares = pair_rows(kept_squares[0:1, :] + other[0:1, :] + other[1:2, :])
    for j in range(8):
        terms = kept[j] + received[j * BLOCK : (j + 1) * BLOCK, :].astype(F32)
        sent[j, 0:BLOCK, :] = terms.astype(BF16)
        sent[j, BLOCK:, :] = squares


def finish(received, hidden, mixed):
    parts = []
    for r in range(4):
        pair = received[2 * r, BLOCK:, :].astype(F32) + received[2 * r + 1, BLOCK:, :].astype(F32)
        squares = pair[0:1, :] + pair[1:2, :]
        scale = lax.rsqrt(squares / HEAD_V + 1e-05)
        parts.append(jnp.broadcast_to(scale, (8, BLOCK)))
    parts.append(jnp.zeros((BLOCK - 8 * len(parts), BLOCK), F32))
    columns = jnp.transpose(jnp.concatenate(parts, axis=0))
    total = hidden[...].astype(F32)
    for r in range(4):
        terms = received[2 * r, 0:BLOCK, :].astype(F32)
        terms = terms + received[2 * r + 1, 0:BLOCK, :].astype(F32)
        total = total + columns[:, 8 * r : 8 * r + 1] * terms
    mixed[...] = total.astype(BF16)


def shards(
    hidden_in,
    seg_ids,
    norm_gain,
    w_query,
    w_key,
    w_value,
    w_gate,
    w_decay_down,
    w_decay_up,
    decay_bias,
    conv_query,
    conv_key,
    conv_value,
    head_gain,
    w_out,
):
    block = lax.axis_index("x") * ROWS_Y + lax.axis_index("y")
    block_at = jnp.reshape(block, (1,)).astype(jnp.int32)
    core_at = jnp.reshape(lax.axis_index("core"), (1,)).astype(jnp.int32)
    blocks = ROWS_X * ROWS_Y

    (copies,) = local_call(spread_out, [((8, BLOCK, CHUNK), BF16)], hidden_in, plain=(0,))
    of_core = lax.all_to_all(copies, CHIPS, 0, 0)
    whole = lax.all_gather(of_core, "core", axis=0)

    pre, tail, gate_pre, rank_part = local_call(
        project,
        [
            ((BLOCK, 2 * HEAD_K + CHUNK), F32),
            ((8, 2 * HEAD_K + CHUNK), F32),
            ((BLOCK, CHUNK), F32),
            ((BLOCK, 16), F32),
        ],
        whole,
        norm_gain.reshape(1, WIDTH),
        w_query,
        w_key,
        w_value,
        w_gate,
        w_decay_down.T,
        scratch=[pltpu.VMEM((BLOCK, WIDTH), BF16)],
    )
    edge = lax.ppermute(tail, SEQ, [(i, i + 1) for i in range(blocks - 1)])
    cumulated, gate, columns, own_rows = local_call(
        gates,
        [
            ((BLOCK, HEAD_K), F32),
            ((BLOCK, CHUNK), F32),
            ((BLOCK, BLOCK), F32),
            ((8, BLOCK), F32),
        ],
        block_at,
        rank_part,
        w_decay_up,
        decay_bias.reshape(1, HEAD_K),
        gate_pre,
        head_gain.reshape(1, CHUNK),
        seg_ids.reshape(blocks, BLOCK),
        scalars=1,
    )
    intra, reach, pieces = local_call(
        span,
        [
            ((BLOCK, CHUNK), F32),
            ((BLOCK, HEAD_K), F32),
            ((ROWS_Y, PIECE + 8, HEAD_K), BF16),
        ],
        pre,
        edge,
        conv_query,
        conv_key,
        conv_value,
        cumulated,
        columns,
        own_rows,
        scratch=[pltpu.VMEM((BLOCK + 8, 2 * HEAD_K + CHUNK), F32)],
    )
    entering, kept, totals = local_call(
        row_scan,
        [
            ((ROWS_Y, PIECE, HEAD_K), F32),
            ((ROWS_Y, 8, HEAD_K), F32),
            ((PIECE + 8, HEAD_K), F32),
        ],
        lax.all_to_all(pieces, "y", 0, 0),
    )
    one_back = lax.ppermute(totals, "x", [(i, i + 1) for i in range(ROWS_X - 1)])
    two_back = lax.ppermute(totals, "x", [(i, i + 2) for i in range(ROWS_X - 2)])
    (states,) = local_call(
        carry, [((ROWS_Y, PIECE, HEAD_K), BF16)], entering, kept, one_back, two_back
    )
    incoming = lax.all_to_all(states, "y", 0, 0).reshape(CHUNK, HEAD_K)
    mine, my_squares, sent = local_call(
        attend,
        [((8, BLOCK, CHUNK), F32), ((8, BLOCK), F32), ((8 * BLOCK + 8, CHUNK), BF16)],
        core_at,
        intra,
        reach,
        incoming,
        gate,
        w_out,
        scalars=1,
    )
    both = lax.all_gather(sent, "core", axis=0)
    (pairs,) = local_call(
        pair_sum, [((8, BLOCK + 8, CHUNK), BF16)], core_at, mine, my_squares, both, scalars=1
    )
    arrived = lax.all_to_all(pairs, CHIPS, 0, 0)
    (mixed,) = local_call(
        finish, [((BLOCK, CHUNK), BF16)], arrived, hidden_in, plain=(1,), last=True
    )
    return mixed


def solution(mesh):
    finer = Mesh(mesh.devices.reshape(ROWS_X, ROWS_Y, 4, 2, 2), ("x", "y", "row", "zhi", "core"))
    part = ("row", "zhi", "core")
    return jax.shard_map(
        shards,
        mesh=finer,
        in_specs=(
            P(SEQ, part),
            P(),
            P(),
            P(None, "row"),
            P(None, "row"),
            P(None, part),
            P(None, part),
            P(),
            P(None, "row"),
            P("row"),
            P(None, "row"),
            P(None, "row"),
            P(None, part),
            P(("zhi", "core")),
            P(part, None),
        ),
        out_specs=P(SEQ, part),
        check_vma=False,
    )
```

```python
import jax
import jax.numpy as jnp
from jax import lax
from jax.experimental import pallas as pl
from jax.experimental.pallas import tpu as pltpu
from jax.sharding import Mesh, PartitionSpec as P

F32 = jnp.float32
BF16 = jnp.bfloat16
HIGHEST = lax.Precision.HIGHEST
HEAD_V = 512
WIDTH = 2048
BLOCK = 128
HEAD_K = 256
CHUNK = 128
LAST = (((1,), (1,)), ((), ()))
FIRST = (((0,), (0,)), ((), ()))

SEQ = ("x", "y")
CHIPS = ("row", "zhi")
ROWS_X, ROWS_Y = 4, 8
PIECE = BLOCK // ROWS_Y


def local_call(kernel, outs, *args, scratch=(), scalars=0, plain=(), anywhere=(), last=False):
    elsewhere = (*range(scalars), *plain, *anywhere)
    vmem = pl.BlockSpec(memory_space=pltpu.VMEM)
    smem = pl.BlockSpec(memory_space=pltpu.SMEM)
    args = [
        pltpu.with_memory_space_constraint(a, pltpu.HBM if i in anywhere else pltpu.VMEM)
        if i in anywhere or i not in elsewhere
        else a
        for i, a in enumerate(args)
    ]
    return pl.pallas_call(
        kernel,
        out_shape=[jax.ShapeDtypeStruct(s, t) if last else pltpu.VMEM(s, t) for s, t in outs],
        in_specs=[
            smem if i < scalars else pl.BlockSpec(memory_space=pltpu.HBM) if i in anywhere else vmem
            for i in range(len(args))
        ],
        out_specs=[vmem] * len(outs),
        scratch_shapes=list(scratch),
        name=kernel.__name__,
        compiler_params=pltpu.CompilerParams(vmem_limit_bytes=16 << 20),
    )(*args)


def dot(a, b, dims=(((1,), (0,)), ((), ())), precision=None):
    return lax.dot_general(a, b, dims, precision=precision, preferred_element_type=F32)


def halves(value):
    high = value.astype(BF16)
    return high, (value - high.astype(F32)).astype(BF16)


def pair_rows(value):
    high, low = halves(value)
    shape = (8, value.shape[1])
    index = lax.broadcasted_iota(jnp.int32, shape, 0)
    both = jnp.where(
        index == 0,
        jnp.broadcast_to(high.astype(F32), shape),
        jnp.where(index == 1, jnp.broadcast_to(low.astype(F32), shape), 0.0),
    )
    return both.astype(BF16)


def silu(value):
    return value * jax.nn.sigmoid(value)


def spread_out(hidden, copies):
    for j in range(8):
        copies[j] = hidden[...]


def project(
    whole,
    gain,
    w_query,
    w_value,
    key_hbm,
    gate_hbm,
    down_hbm,
    pre,
    tail,
    gate_pre,
    rank_part,
    normed,
    w_key,
    w_gate,
    w_down,
    arrived,
):
    copies = [
        pltpu.make_async_copy(source, target, arrived.at[i])
        for i, (source, target) in enumerate(
            ((key_hbm, w_key), (gate_hbm, w_gate), (down_hbm, w_down))
        )
    ]
    for copy in copies:
        copy.start()
    chunks = WIDTH // CHUNK
    squares = jnp.zeros((BLOCK, CHUNK), F32)
    for f in range(chunks):
        activ = whole[f % 2, f // 2].astype(F32)
        squares = squares + activ * activ
    scale = lax.rsqrt(jnp.sum(squares, axis=1, keepdims=True) / WIDTH + 1e-06)
    for f in range(chunks):
        span = slice(f * CHUNK, (f + 1) * CHUNK)
        activ = whole[f % 2, f // 2].astype(F32)
        normed[:, span] = (activ * scale * gain[:, span]).astype(BF16)
    rows = normed[...]
    pre[:, :HEAD_K] = dot(rows, w_query[...])
    pre[:, 2 * HEAD_K :] = dot(rows, w_value[...])
    copies[0].wait()
    pre[:, HEAD_K : 2 * HEAD_K] = dot(rows, w_key[...])
    tail[...] = pre[BLOCK - 8 :, :]
    copies[1].wait()
    gate_pre[...] = dot(rows, w_gate[...])
    copies[2].wait()
    rank_part[...] = dot(rows, w_down[...], LAST)


def gates(
    index,
    core,
    rank_part,
    w_up,
    bias,
    gate_pre,
    head_gain,
    seg_ids,
    taps_q,
    taps_k,
    taps_v,
    cumulated,
    gate,
    columns,
    own_rows,
    taps,
):
    del core
    taps[:, :HEAD_K] = taps_q[...]
    taps[:, HEAD_K : 2 * HEAD_K] = taps_k[...]
    taps[:, 2 * HEAD_K :] = taps_v[...]
    logits = dot(rank_part[...], w_up[...].astype(F32), precision=HIGHEST) + bias[...]
    log_decay = (jnp.minimum(logits, 0.0) - jnp.log(1.0 + jnp.exp(-jnp.abs(logits)))) / 16.0
    row_iota = lax.broadcasted_iota(jnp.int32, (BLOCK, BLOCK), 0)
    col_iota = lax.broadcasted_iota(jnp.int32, (BLOCK, BLOCK), 1)
    lower = jnp.where(row_iota >= col_iota, 1.0, 0.0).astype(F32)
    cumulated[...] = dot(lower, log_decay, precision=HIGHEST)
    gate[...] = silu(gate_pre[...]) * head_gain[...]
    at = index[0]
    own = seg_ids[pl.ds(at, 1), :].astype(F32)
    before = seg_ids[pl.ds(jnp.maximum(at - 1, 0), 1), :].astype(F32)
    before = jnp.where(at > 0, before, -1.0)
    own = jnp.broadcast_to(own, (8, BLOCK))
    before = jnp.broadcast_to(before, (8, BLOCK))
    lane = lax.broadcasted_iota(jnp.int32, (8, BLOCK), 1)
    parts = [own]
    for j in range(1, 4):
        parts.append(jnp.where(lane < j, pltpu.roll(before, j, 1), pltpu.roll(own, j, 1)))
    parts.append(jnp.broadcast_to(before[:, BLOCK - 1 :], (8, BLOCK)))
    parts.append(jnp.broadcast_to(own[:, BLOCK - 1 :], (8, BLOCK)))
    parts.append(jnp.zeros((BLOCK - 8 * len(parts), BLOCK), F32))
    columns[...] = jnp.transpose(jnp.concatenate(parts, axis=0))
    own_rows[...] = own


def span(
    pre, edge, taps, cumulated, columns, own_rows, intra, reach, pieces, extended
):
    extended[0:8, :] = edge[...]
    extended[8:, :] = pre[...]
    seg = columns[:, 0:1]

    def conv(lanes):
        total = taps[0:1, lanes] * extended[8:, lanes]
        for j in range(1, 4):
            same = columns[:, 8 * j : 8 * j + 1] == seg
            total = total + jnp.where(
                same, taps[j : j + 1, lanes] * extended[8 - j : 8 - j + BLOCK, lanes], 0.0
            )
        return silu(total)

    queries = conv(slice(0, HEAD_K)) * HEAD_K ** (-0.5)
    keys = conv(slice(HEAD_K, 2 * HEAD_K))
    values = conv(slice(2 * HEAD_K, 2 * HEAD_K + CHUNK))
    cum = cumulated[...]
    row_iota = lax.broadcasted_iota(jnp.int32, (BLOCK, BLOCK), 0)
    col_iota = lax.broadcasted_iota(jnp.int32, (BLOCK, BLOCK), 1)
    weights = jnp.zeros((BLOCK, BLOCK), F32)
    for half in (8, 16, 32, 64):
        anchors = [
            jnp.broadcast_to(cum[b + half - 1 : b + half, :], (2 * half, HEAD_K))
            for b in range(0, BLOCK, 2 * half)
        ]
        anchor = jnp.concatenate(anchors, axis=0) if len(anchors) > 1 else anchors[0]
        factor = jnp.exp(-jnp.abs(cum - anchor))
        part = dot((queries * factor).astype(BF16), (keys * factor).astype(BF16), LAST)
        inside = (
            (row_iota // (2 * half) == col_iota // (2 * half))
            & (row_iota % (2 * half) >= half)
            & (col_iota % (2 * half) < half)
        )
        weights = jnp.where(inside, part, weights)
    groups = (BLOCK // 8, 8, HEAD_K)
    cum_g, keys_g = cum.reshape(groups), keys.reshape(groups)
    queries_g = queries.reshape(groups)
    for by in range(8):
        if by:
            spread = jnp.minimum(cum_g - pltpu.roll(cum_g, by, 1), 0.0)
            product = queries_g * pltpu.roll(keys_g, by, 1) * jnp.exp(spread)
        else:
            product = queries_g * keys_g
        sums = jnp.sum(product.reshape(BLOCK, HEAD_K), axis=1, keepdims=True)
        inside = (row_iota - col_iota == by) & (row_iota % 8 >= by)
        weights = jnp.where(inside, sums, weights)
    visible = (seg == own_rows[0:1, :]) & (row_iota >= col_iota)
    weights = jnp.where(visible, weights, 0.0)
    values_b = values.astype(BF16)
    intra[...] = dot(weights.astype(BF16), values_b)
    before, last = columns[:, 32:33], columns[:, 40:41]
    reach[...] = jnp.where(seg == before, queries * jnp.exp(cum), 0.0)
    final = cum[BLOCK - 1 :, :]
    pushed = jnp.where(seg == last, keys * jnp.exp(final - cum), 0.0)
    state = dot(values_b, pushed.astype(BF16), FIRST)
    keep = jnp.where(before[0:1, :] == last[0:1, :], jnp.exp(final), 0.0)
    keep_rows = pair_rows(keep)
    for j in range(ROWS_Y):
        pieces[j, 0:PIECE, :] = state[j * PIECE : (j + 1) * PIECE, :].astype(BF16)
        pieces[j, PIECE:, :] = keep_rows


def row_scan(pieces, entering, kept, totals):
    state = jnp.zeros((PIECE, HEAD_K), F32)
    keep = jnp.ones((1, HEAD_K), F32)
    for j in range(ROWS_Y):
        entering[j] = state
        kept[j] = jnp.broadcast_to(keep, (8, HEAD_K))
        pair = pieces[j, PIECE:, :].astype(F32)
        decay = pair[0:1, :] + pair[1:2, :]
        state = state * decay + pieces[j, 0:PIECE, :].astype(F32)
        keep = keep * decay
    totals[0:PIECE, :] = state
    totals[PIECE:, :] = jnp.broadcast_to(keep, (8, HEAD_K))


def carry(entering, kept, one_back, two_back, states):
    arriving = one_back[0:PIECE, :] + one_back[PIECE : PIECE + 1, :] * two_back[0:PIECE, :]
    for j in range(ROWS_Y):
        states[j] = (entering[j] + kept[j, 0:1, :] * arriving).astype(BF16)


def attend(index, intra, reach, incoming, gate, w_out, kept, kept_squares, sent):
    high, low = halves(reach[...])
    state = incoming[...]
    attended = intra[...] + dot(high, state, LAST) + dot(low, state, LAST)
    squares = dot(jnp.ones((8, CHUNK), F32), attended * attended, LAST, precision=HIGHEST)
    terms = dot((attended * gate[...]).astype(BF16), w_out[...])
    first = index[0] == 0
    for j in range(8):
        even = terms[:, (2 * j) * CHUNK : (2 * j + 1) * CHUNK]
        odd = terms[:, (2 * j + 1) * CHUNK : (2 * j + 2) * CHUNK]
        kept[j] = jnp.where(first, even, odd)
        sent[j * BLOCK : (j + 1) * BLOCK, :] = jnp.where(first, odd, even).astype(BF16)
    kept_squares[...] = squares
    sent[8 * BLOCK :, :] = pair_rows(squares[0:1, :])


def pair_sum(index, kept, kept_squares, both, sent):
    received = both.at[1 - index[0]]
    other = received[8 * BLOCK :, :].astype(F32)
    squares = pair_rows(kept_squares[0:1, :] + other[0:1, :] + other[1:2, :])
    for j in range(8):
        terms = kept[j] + received[j * BLOCK : (j + 1) * BLOCK, :].astype(F32)
        sent[j, 0:BLOCK, :] = terms.astype(BF16)
        sent[j, BLOCK:, :] = squares


def finish(received, hidden, mixed):
    parts = []
    for r in range(4):
        pair = received[2 * r, BLOCK:, :].astype(F32) + received[2 * r + 1, BLOCK:, :].astype(F32)
        squares = pair[0:1, :] + pair[1:2, :]
        scale = lax.rsqrt(squares / HEAD_V + 1e-05)
        parts.append(jnp.broadcast_to(scale, (8, BLOCK)))
    parts.append(jnp.zeros((BLOCK - 8 * len(parts), BLOCK), F32))
    columns = jnp.transpose(jnp.concatenate(parts, axis=0))
    total = hidden[...].astype(F32)
    for r in range(4):
        terms = received[2 * r, 0:BLOCK, :].astype(F32)
        terms = terms + received[2 * r + 1, 0:BLOCK, :].astype(F32)
        total = total + columns[:, 8 * r : 8 * r + 1] * terms
    mixed[...] = total.astype(BF16)


def shards(
    hidden_in,
    seg_ids,
    norm_gain,
    w_query,
    w_key,
    w_value,
    w_gate,
    w_decay_down,
    w_decay_up,
    decay_bias,
    conv_query,
    conv_key,
    conv_value,
    head_gain,
    w_out,
):
    block = lax.axis_index("x") * ROWS_Y + lax.axis_index("y")
    block_at = jnp.reshape(block, (1,)).astype(jnp.int32)
    core_at = jnp.reshape(lax.axis_index("core"), (1,)).astype(jnp.int32)
    blocks = ROWS_X * ROWS_Y

    (copies,) = local_call(spread_out, [((8, BLOCK, CHUNK), BF16)], hidden_in, plain=(0,))
    of_core = lax.all_to_all(copies, CHIPS, 0, 0)
    whole = lax.all_gather(of_core, "core", axis=0)

    pre, tail, gate_pre, rank_part = local_call(
        project,
        [
            ((BLOCK, 2 * HEAD_K + CHUNK), F32),
            ((8, 2 * HEAD_K + CHUNK), F32),
            ((BLOCK, CHUNK), F32),
            ((BLOCK, 16), F32),
        ],
        whole,
        norm_gain.reshape(1, WIDTH),
        w_query,
        w_value,
        w_key,
        w_gate,
        w_decay_down.T,
        scratch=[
            pltpu.VMEM((BLOCK, WIDTH), BF16),
            pltpu.VMEM((WIDTH, HEAD_K), BF16),
            pltpu.VMEM((WIDTH, CHUNK), BF16),
            pltpu.VMEM((16, WIDTH), BF16),
            pltpu.SemaphoreType.DMA((3,)),
        ],
        anywhere=(4, 5, 6),
    )
    edge = lax.ppermute(tail, SEQ, [(i, i + 1) for i in range(blocks - 1)])
    cumulated, gate, columns, own_rows, taps = local_call(
        gates,
        [
            ((BLOCK, HEAD_K), F32),
            ((BLOCK, CHUNK), F32),
            ((BLOCK, BLOCK), F32),
            ((8, BLOCK), F32),
            ((4, 2 * HEAD_K + CHUNK), F32),
        ],
        block_at,
        core_at,
        rank_part,
        w_decay_up,
        decay_bias.reshape(1, HEAD_K),
        gate_pre,
        head_gain.reshape(1, CHUNK),
        seg_ids.reshape(blocks, BLOCK),
        conv_query,
        conv_key,
        conv_value,
        scalars=2,
        plain=(3, 4, 6, 7, 8, 9, 10),
    )
    intra, reach, pieces = local_call(
        span,
        [
            ((BLOCK, CHUNK), F32),
            ((BLOCK, HEAD_K), F32),
            ((ROWS_Y, PIECE + 8, HEAD_K), BF16),
        ],
        pre,
        edge,
        taps,
        cumulated,
        columns,
        own_rows,
        scratch=[pltpu.VMEM((BLOCK + 8, 2 * HEAD_K + CHUNK), F32)],
    )
    entering, kept, totals = local_call(
        row_scan,
        [
            ((ROWS_Y, PIECE, HEAD_K), F32),
            ((ROWS_Y, 8, HEAD_K), F32),
            ((PIECE + 8, HEAD_K), F32),
        ],
        lax.all_to_all(pieces, "y", 0, 0),
    )
    one_back = lax.ppermute(totals, "x", [(i, i + 1) for i in range(ROWS_X - 1)])
    two_back = lax.ppermute(totals, "x", [(i, i + 2) for i in range(ROWS_X - 2)])
    (states,) = local_call(
        carry, [((ROWS_Y, PIECE, HEAD_K), BF16)], entering, kept, one_back, two_back
    )
    incoming = lax.all_to_all(states, "y", 0, 0).reshape(CHUNK, HEAD_K)
    mine, my_squares, sent = local_call(
        attend,
        [((8, BLOCK, CHUNK), F32), ((8, BLOCK), F32), ((8 * BLOCK + 8, CHUNK), BF16)],
        core_at,
        intra,
        reach,
        incoming,
        gate,
        w_out,
        scalars=1,
    )
    both = lax.all_gather(sent, "core", axis=0)
    (pairs,) = local_call(
        pair_sum, [((8, BLOCK + 8, CHUNK), BF16)], core_at, mine, my_squares, both, scalars=1
    )
    arrived = lax.all_to_all(pairs, CHIPS, 0, 0)
    (mixed,) = local_call(
        finish, [((BLOCK, CHUNK), BF16)], arrived, hidden_in, plain=(1,), last=True
    )
    return mixed


def solution(mesh):
    finer = Mesh(mesh.devices.reshape(ROWS_X, ROWS_Y, 4, 2, 2), ("x", "y", "row", "zhi", "core"))
    part = ("row", "zhi", "core")
    return jax.shard_map(
        shards,
        mesh=finer,
        in_specs=(
            P(SEQ, part),
            P(),
            P(),
            P(None, "row"),
            P(None, "row"),
            P(None, part),
            P(None, part),
            P(),
            P(None, "row"),
            P("row"),
            P(None, "row"),
            P(None, "row"),
            P(None, part),
            P(("zhi", "core")),
            P(part, None),
        ),
        out_specs=P(SEQ, part),
        check_vma=False,
    )
```

```python
import jax
import jax.numpy as jnp
from jax import lax
from jax.experimental import pallas as pl
from jax.experimental.pallas import tpu as pltpu
from jax.sharding import Mesh, PartitionSpec as P

F32 = jnp.float32
BF16 = jnp.bfloat16
HIGHEST = lax.Precision.HIGHEST
HEAD_V = 512
WIDTH = 2048
BLOCK = 128
HEAD_K = 256
CHUNK = 128
LAST = (((1,), (1,)), ((), ()))
FIRST = (((0,), (0,)), ((), ()))

SEQ = ("x", "y")
CHIPS = ("row", "zhi")
ROWS_X, ROWS_Y = 4, 8
PIECE = BLOCK // ROWS_Y


def local_call(kernel, outs, *args, scratch=(), scalars=0, plain=(), anywhere=(), last=False):
    elsewhere = (*range(scalars), *plain, *anywhere)
    vmem = pl.BlockSpec(memory_space=pltpu.VMEM)
    smem = pl.BlockSpec(memory_space=pltpu.SMEM)
    args = [
        pltpu.with_memory_space_constraint(a, pltpu.HBM if i in anywhere else pltpu.VMEM)
        if i in anywhere or i not in elsewhere
        else a
        for i, a in enumerate(args)
    ]
    return pl.pallas_call(
        kernel,
        out_shape=[jax.ShapeDtypeStruct(s, t) if last else pltpu.VMEM(s, t) for s, t in outs],
        in_specs=[
            smem if i < scalars else pl.BlockSpec(memory_space=pltpu.HBM) if i in anywhere else vmem
            for i in range(len(args))
        ],
        out_specs=[vmem] * len(outs),
        scratch_shapes=list(scratch),
        name=kernel.__name__,
        compiler_params=pltpu.CompilerParams(vmem_limit_bytes=16 << 20),
    )(*args)


def dot(a, b, dims=(((1,), (0,)), ((), ())), precision=None):
    return lax.dot_general(a, b, dims, precision=precision, preferred_element_type=F32)


def halves(value):
    high = value.astype(BF16)
    return high, (value - high.astype(F32)).astype(BF16)


def pair_rows(value):
    high, low = halves(value)
    shape = (8, value.shape[1])
    index = lax.broadcasted_iota(jnp.int32, shape, 0)
    both = jnp.where(
        index == 0,
        jnp.broadcast_to(high.astype(F32), shape),
        jnp.where(index == 1, jnp.broadcast_to(low.astype(F32), shape), 0.0),
    )
    return both.astype(BF16)


def silu(value):
    return value * jax.nn.sigmoid(value)


def take(index, core, hidden, kept, tail):
    del index, core
    kept[...] = hidden[...]
    tail[...] = hidden[BLOCK - 8 :, :]


def fetch(tail, key_hbm, gate_hbm, w_key, w_gate, arrived):
    del tail
    copies = [
        pltpu.make_async_copy(key_hbm, w_key, arrived.at[0]),
        pltpu.make_async_copy(gate_hbm, w_gate, arrived.at[1]),
    ]
    for copy in copies:
        copy.start()
    for copy in copies:
        copy.wait()


def spread_out(hidden, edge, w_key, copies):
    del w_key
    for j in range(8):
        copies[j, 0:BLOCK, :] = hidden[...]
        copies[j, BLOCK:, :] = edge[...]


def local_work(
    index,
    core,
    whole,
    gain,
    w_query,
    w_key,
    w_value,
    w_gate,
    w_down,
    w_up,
    bias,
    head_gain,
    seg_ids,
    taps_q,
    taps_k,
    taps_v,
    intra,
    reach,
    pieces,
    gate,
    normed,
    extended,
):
    del core
    chunks = WIDTH // CHUNK
    squares = jnp.zeros((BLOCK + 8, CHUNK), F32)
    for f in range(chunks):
        activ = whole[f % 2, f // 2].astype(F32)
        squares = squares + activ * activ
    scale = lax.rsqrt(jnp.sum(squares, axis=1, keepdims=True) / WIDTH + 1e-06)
    for f in range(chunks):
        lanes = slice(f * CHUNK, (f + 1) * CHUNK)
        activ = whole[f % 2, f // 2].astype(F32)
        normed[:, lanes] = (activ * scale * gain[:, lanes]).astype(BF16)
    rows = normed[...]
    rank_part = dot(rows, w_down[...], LAST)[0:BLOCK, :]
    gate_pre = dot(rows, w_gate[...])[0:BLOCK, :]

    def conv(weight, taps, lanes):
        pre = dot(rows, weight[...])
        extended[0:8, lanes] = pre[BLOCK:, :]
        extended[8:, lanes] = pre[0:BLOCK, :]
        total = taps[0:1, :] * pre[0:BLOCK, :]
        for j in range(1, 4):
            same = columns[:, 8 * j : 8 * j + 1] == seg
            total = total + jnp.where(
                same, taps[j : j + 1, :] * extended[8 - j : 8 - j + BLOCK, lanes], 0.0
            )
        return silu(total)

    at = index[0]
    own = seg_ids[pl.ds(at, 1), :].astype(F32)
    before = seg_ids[pl.ds(jnp.maximum(at - 1, 0), 1), :].astype(F32)
    before = jnp.where(at > 0, before, -1.0)
    own = jnp.broadcast_to(own, (8, BLOCK))
    before = jnp.broadcast_to(before, (8, BLOCK))
    lane = lax.broadcasted_iota(jnp.int32, (8, BLOCK), 1)
    parts = [own]
    for j in range(1, 4):
        parts.append(jnp.where(lane < j, pltpu.roll(before, j, 1), pltpu.roll(own, j, 1)))
    before = jnp.broadcast_to(before[:, BLOCK - 1 :], (8, BLOCK))
    last = jnp.broadcast_to(own[:, BLOCK - 1 :], (8, BLOCK))
    parts += [before, last]
    parts.append(jnp.zeros((BLOCK - 8 * len(parts), BLOCK), F32))
    columns = jnp.transpose(jnp.concatenate(parts, axis=0))
    seg = columns[:, 0:1]

    logits = dot(rank_part, w_up[...].astype(F32), precision=HIGHEST) + bias[...]
    log_decay = (jnp.minimum(logits, 0.0) - jnp.log(1.0 + jnp.exp(-jnp.abs(logits)))) / 16.0
    row_iota = lax.broadcasted_iota(jnp.int32, (BLOCK, BLOCK), 0)
    col_iota = lax.broadcasted_iota(jnp.int32, (BLOCK, BLOCK), 1)
    lower = jnp.where(row_iota >= col_iota, 1.0, 0.0).astype(F32)
    cum = dot(lower, log_decay, precision=HIGHEST)

    keys = conv(w_key, taps_k, slice(HEAD_K, 2 * HEAD_K))
    values = conv(w_value, taps_v, slice(2 * HEAD_K, 2 * HEAD_K + CHUNK)).astype(BF16)
    final = cum[BLOCK - 1 :, :]
    pushed = jnp.where(seg == columns[:, 40:41], keys * jnp.exp(final - cum), 0.0)
    state = dot(values, pushed.astype(BF16), FIRST)
    keep = jnp.where(before[0:1, 0:1] == last[0:1, 0:1], jnp.exp(final), 0.0)
    keep_rows = pair_rows(keep)
    for j in range(ROWS_Y):
        pieces[j, 0:PIECE, :] = state[j * PIECE : (j + 1) * PIECE, :].astype(BF16)
        pieces[j, PIECE:, :] = keep_rows

    gate[...] = silu(gate_pre) * head_gain[...]
    queries = conv(w_query, taps_q, slice(0, HEAD_K)) * HEAD_K ** (-0.5)
    reach[...] = jnp.where(seg == columns[:, 32:33], queries * jnp.exp(cum), 0.0)
    weights = jnp.zeros((BLOCK, BLOCK), F32)
    for half in (8, 16, 32, 64):
        anchors = [
            jnp.broadcast_to(cum[b + half - 1 : b + half, :], (2 * half, HEAD_K))
            for b in range(0, BLOCK, 2 * half)
        ]
        anchor = jnp.concatenate(anchors, axis=0) if len(anchors) > 1 else anchors[0]
        factor = jnp.exp(-jnp.abs(cum - anchor))
        part = dot((queries * factor).astype(BF16), (keys * factor).astype(BF16), LAST)
        inside = (
            (row_iota // (2 * half) == col_iota // (2 * half))
            & (row_iota % (2 * half) >= half)
            & (col_iota % (2 * half) < half)
        )
        weights = jnp.where(inside, part, weights)
    groups = (BLOCK // 8, 8, HEAD_K)
    cum_g, keys_g = cum.reshape(groups), keys.reshape(groups)
    queries_g = queries.reshape(groups)
    for by in range(8):
        if by:
            spread = jnp.minimum(cum_g - pltpu.roll(cum_g, by, 1), 0.0)
            product = queries_g * pltpu.roll(keys_g, by, 1) * jnp.exp(spread)
        else:
            product = queries_g * keys_g
        sums = jnp.sum(product.reshape(BLOCK, HEAD_K), axis=1, keepdims=True)
        inside = (row_iota - col_iota == by) & (row_iota % 8 >= by)
        weights = jnp.where(inside, sums, weights)
    visible = (seg == own[0:1, :]) & (row_iota >= col_iota)
    weights = jnp.where(visible, weights, 0.0)
    intra[...] = dot(weights.astype(BF16), values)


def row_scan(pieces, entering, kept, totals):
    state = jnp.zeros((PIECE, HEAD_K), F32)
    keep = jnp.ones((1, HEAD_K), F32)
    for j in range(ROWS_Y):
        entering[j] = state
        kept[j] = jnp.broadcast_to(keep, (8, HEAD_K))
        pair = pieces[j, PIECE:, :].astype(F32)
        decay = pair[0:1, :] + pair[1:2, :]
        state = state * decay + pieces[j, 0:PIECE, :].astype(F32)
        keep = keep * decay
    totals[0:PIECE, :] = state
    totals[PIECE:, :] = jnp.broadcast_to(keep, (8, HEAD_K))


def carry(entering, kept, one_back, two_back, states):
    arriving = one_back[0:PIECE, :] + one_back[PIECE : PIECE + 1, :] * two_back[0:PIECE, :]
    for j in range(ROWS_Y):
        states[j] = (entering[j] + kept[j, 0:1, :] * arriving).astype(BF16)


def attend(index, intra, reach, incoming, gate, w_out, kept, kept_squares, sent):
    high, low = halves(reach[...])
    state = incoming[...]
    attended = intra[...] + dot(high, state, LAST) + dot(low, state, LAST)
    squares = dot(jnp.ones((8, CHUNK), F32), attended * attended, LAST, precision=HIGHEST)
    terms = dot((attended * gate[...]).astype(BF16), w_out[...])
    first = index[0] == 0
    for j in range(8):
        even = terms[:, (2 * j) * CHUNK : (2 * j + 1) * CHUNK]
        odd = terms[:, (2 * j + 1) * CHUNK : (2 * j + 2) * CHUNK]
        kept[j] = jnp.where(first, even, odd)
        sent[j * BLOCK : (j + 1) * BLOCK, :] = jnp.where(first, odd, even).astype(BF16)
    kept_squares[...] = squares
    sent[8 * BLOCK :, :] = pair_rows(squares[0:1, :])


def pair_sum(index, kept, kept_squares, both, sent):
    received = both.at[1 - index[0]]
    other = received[8 * BLOCK :, :].astype(F32)
    squares = pair_rows(kept_squares[0:1, :] + other[0:1, :] + other[1:2, :])
    for j in range(8):
        terms = kept[j] + received[j * BLOCK : (j + 1) * BLOCK, :].astype(F32)
        sent[j, 0:BLOCK, :] = terms.astype(BF16)
        sent[j, BLOCK:, :] = squares


def finish(received, hidden, mixed):
    parts = []
    for r in range(4):
        pair = received[2 * r, BLOCK:, :].astype(F32) + received[2 * r + 1, BLOCK:, :].astype(F32)
        squares = pair[0:1, :] + pair[1:2, :]
        scale = lax.rsqrt(squares / HEAD_V + 1e-05)
        parts.append(jnp.broadcast_to(scale, (8, BLOCK)))
    parts.append(jnp.zeros((BLOCK - 8 * len(parts), BLOCK), F32))
    columns = jnp.transpose(jnp.concatenate(parts, axis=0))
    total = hidden[...].astype(F32)
    for r in range(4):
        terms = received[2 * r, 0:BLOCK, :].astype(F32)
        terms = terms + received[2 * r + 1, 0:BLOCK, :].astype(F32)
        total = total + columns[:, 8 * r : 8 * r + 1] * terms
    mixed[...] = total.astype(BF16)


def shards(
    hidden_in,
    seg_ids,
    norm_gain,
    w_query,
    w_key,
    w_value,
    w_gate,
    w_decay_down,
    w_decay_up,
    decay_bias,
    conv_query,
    conv_key,
    conv_value,
    head_gain,
    w_out,
):
    block = lax.axis_index("x") * ROWS_Y + lax.axis_index("y")
    block_at = jnp.reshape(block, (1,)).astype(jnp.int32)
    core_at = jnp.reshape(lax.axis_index("core"), (1,)).astype(jnp.int32)
    blocks = ROWS_X * ROWS_Y

    onward = [(i, i + 1) for i in range(blocks - 1)]
    hidden, tail = local_call(
        take,
        [((BLOCK, CHUNK), BF16), ((8, CHUNK), BF16)],
        block_at,
        core_at,
        hidden_in,
        scalars=2,
        plain=(2,),
    )
    edge = lax.ppermute(tail, SEQ, onward)
    key_here, gate_here = local_call(
        fetch,
        [((WIDTH, HEAD_K), BF16), ((WIDTH, CHUNK), BF16)],
        tail,
        w_key,
        w_gate,
        scratch=[pltpu.SemaphoreType.DMA((2,))],
        anywhere=(1, 2),
    )
    (copies,) = local_call(
        spread_out,
        [((8, BLOCK + 8, CHUNK), BF16)],
        hidden,
        edge,
        key_here,
    )
    of_core = lax.all_to_all(copies, CHIPS, 0, 0)
    whole = lax.all_gather(of_core, "core", axis=0)
    intra, reach, pieces, gate = local_call(
        local_work,
        [
            ((BLOCK, CHUNK), F32),
            ((BLOCK, HEAD_K), F32),
            ((ROWS_Y, PIECE + 8, HEAD_K), BF16),
            ((BLOCK, CHUNK), F32),
        ],
        block_at,
        core_at,
        whole,
        norm_gain.reshape(1, WIDTH),
        w_query,
        key_here,
        w_value,
        gate_here,
        w_decay_down.T,
        w_decay_up,
        decay_bias.reshape(1, HEAD_K),
        head_gain.reshape(1, CHUNK),
        seg_ids.reshape(blocks, BLOCK),
        conv_query,
        conv_key,
        conv_value,
        scratch=[
            pltpu.VMEM((BLOCK + 8, WIDTH), BF16),
            pltpu.VMEM((BLOCK + 8, 2 * HEAD_K + CHUNK), F32),
        ],
        scalars=2,
    )
    entering, kept, totals = local_call(
        row_scan,
        [
            ((ROWS_Y, PIECE, HEAD_K), F32),
            ((ROWS_Y, 8, HEAD_K), F32),
            ((PIECE + 8, HEAD_K), F32),
        ],
        lax.all_to_all(pieces, "y", 0, 0),
    )
    one_back = lax.ppermute(totals, "x", [(i, i + 1) for i in range(ROWS_X - 1)])
    two_back = lax.ppermute(totals, "x", [(i, i + 2) for i in range(ROWS_X - 2)])
    (states,) = local_call(
        carry, [((ROWS_Y, PIECE, HEAD_K), BF16)], entering, kept, one_back, two_back
    )
    incoming = lax.all_to_all(states, "y", 0, 0).reshape(CHUNK, HEAD_K)
    mine, my_squares, sent = local_call(
        attend,
        [((8, BLOCK, CHUNK), F32), ((8, BLOCK), F32), ((8 * BLOCK + 8, CHUNK), BF16)],
        core_at,
        intra,
        reach,
        incoming,
        gate,
        w_out,
        scalars=1,
    )
    both = lax.all_gather(sent, "core", axis=0)
    (pairs,) = local_call(
        pair_sum, [((8, BLOCK + 8, CHUNK), BF16)], core_at, mine, my_squares, both, scalars=1
    )
    arrived = lax.all_to_all(pairs, CHIPS, 0, 0)
    (mixed,) = local_call(
        finish, [((BLOCK, CHUNK), BF16)], arrived, hidden, last=True
    )
    return mixed


def solution(mesh):
    finer = Mesh(mesh.devices.reshape(ROWS_X, ROWS_Y, 4, 2, 2), ("x", "y", "row", "zhi", "core"))
    part = ("row", "zhi", "core")
    return jax.shard_map(
        shards,
        mesh=finer,
        in_specs=(
            P(SEQ, part),
            P(),
            P(),
            P(None, "row"),
            P(None, "row"),
            P(None, part),
            P(None, part),
            P(),
            P(None, "row"),
            P("row"),
            P(None, "row"),
            P(None, "row"),
            P(None, part),
            P(("zhi", "core")),
            P(part, None),
        ),
        out_specs=P(SEQ, part),
        check_vma=False,
    )
```

```python
import jax
import jax.numpy as jnp
from jax import lax
from jax.experimental import pallas as pl
from jax.experimental.pallas import tpu as pltpu
from jax.sharding import Mesh, PartitionSpec as P

F32 = jnp.float32
BF16 = jnp.bfloat16
HIGHEST = lax.Precision.HIGHEST
HEAD_V = 512
WIDTH = 2048
BLOCK = 128
HEAD_K = 256
CHUNK = 128
LAST = (((1,), (1,)), ((), ()))
FIRST = (((0,), (0,)), ((), ()))

SEQ = ("x", "y")
CHIPS = ("row", "zhi")
ROWS_X, ROWS_Y = 4, 8
PIECE = BLOCK // ROWS_Y


def local_call(kernel, outs, *args, scratch=(), scalars=0, plain=(), anywhere=(), last=False):
    elsewhere = (*range(scalars), *plain, *anywhere)
    vmem = pl.BlockSpec(memory_space=pltpu.VMEM)
    smem = pl.BlockSpec(memory_space=pltpu.SMEM)
    args = [
        pltpu.with_memory_space_constraint(a, pltpu.HBM if i in anywhere else pltpu.VMEM)
        if i in anywhere or i not in elsewhere
        else a
        for i, a in enumerate(args)
    ]
    return pl.pallas_call(
        kernel,
        out_shape=[jax.ShapeDtypeStruct(s, t) if last else pltpu.VMEM(s, t) for s, t in outs],
        in_specs=[
            smem if i < scalars else pl.BlockSpec(memory_space=pltpu.HBM) if i in anywhere else vmem
            for i in range(len(args))
        ],
        out_specs=[vmem] * len(outs),
        scratch_shapes=list(scratch),
        name=kernel.__name__,
        compiler_params=pltpu.CompilerParams(vmem_limit_bytes=16 << 20),
    )(*args)


def dot(a, b, dims=(((1,), (0,)), ((), ())), precision=None):
    return lax.dot_general(a, b, dims, precision=precision, preferred_element_type=F32)


def halves(value):
    high = value.astype(BF16)
    return high, (value - high.astype(F32)).astype(BF16)


def pair_rows(value):
    high, low = halves(value)
    shape = (8, value.shape[1])
    index = lax.broadcasted_iota(jnp.int32, shape, 0)
    both = jnp.where(
        index == 0,
        jnp.broadcast_to(high.astype(F32), shape),
        jnp.where(index == 1, jnp.broadcast_to(low.astype(F32), shape), 0.0),
    )
    return both.astype(BF16)


def silu(value):
    return value * jax.nn.sigmoid(value)


def fetch(index, core, *refs):
    del index, core
    count = (len(refs) - 1) // 2
    arrived = refs[-1]
    copies = [
        pltpu.make_async_copy(refs[i], refs[count + i], arrived.at[i]) for i in range(count)
    ]
    for copy in copies:
        copy.start()
    for copy in copies:
        copy.wait()


def spread_out(hidden, neighbour, w_key, copies):
    del w_key
    edge = neighbour[BLOCK - 8 :, :]
    for j in range(8):
        copies[j, 0:BLOCK, :] = hidden[...]
        copies[j, BLOCK:, :] = edge


def conv(pre, taps, extended, columns):
    extended[0:8, :] = pre[BLOCK:, :]
    extended[8:, :] = pre[0:BLOCK, :]
    seg = columns[:, 0:1]
    total = taps[0:1, :] * pre[0:BLOCK, :]
    for j in range(1, 4):
        same = columns[:, 8 * j : 8 * j + 1] == seg
        total = total + jnp.where(
            same, taps[j : j + 1, :] * extended[8 - j : 8 - j + BLOCK, :], 0.0
        )
    return silu(total)


def block_state(
    index,
    whole,
    gain,
    w_key,
    w_value,
    w_down,
    w_up,
    bias,
    seg_ids,
    taps_k,
    taps_v,
    pieces,
    normed,
    keys_out,
    values_out,
    cumulated,
    columns_out,
    own_rows,
    extended_k,
    extended_v,
):
    chunks = WIDTH // CHUNK
    squares = jnp.zeros((BLOCK + 8, CHUNK), F32)
    for f in range(chunks):
        activ = whole[f % 2, f // 2].astype(F32)
        squares = squares + activ * activ
    scale = lax.rsqrt(jnp.sum(squares, axis=1, keepdims=True) / WIDTH + 1e-06)
    for f in range(chunks):
        lanes = slice(f * CHUNK, (f + 1) * CHUNK)
        activ = whole[f % 2, f // 2].astype(F32)
        normed[:, lanes] = (activ * scale * gain[:, lanes]).astype(BF16)
    rows = normed[...]
    rank_part = dot(rows, w_down[...], LAST)[0:BLOCK, :]

    at = index[0]
    own = seg_ids[pl.ds(at, 1), :].astype(F32)
    before = seg_ids[pl.ds(jnp.maximum(at - 1, 0), 1), :].astype(F32)
    before = jnp.where(at > 0, before, -1.0)
    own = jnp.broadcast_to(own, (8, BLOCK))
    before = jnp.broadcast_to(before, (8, BLOCK))
    lane = lax.broadcasted_iota(jnp.int32, (8, BLOCK), 1)
    parts = [own]
    for j in range(1, 4):
        parts.append(jnp.where(lane < j, pltpu.roll(before, j, 1), pltpu.roll(own, j, 1)))
    before = jnp.broadcast_to(before[:, BLOCK - 1 :], (8, BLOCK))
    last = jnp.broadcast_to(own[:, BLOCK - 1 :], (8, BLOCK))
    parts += [before, last]
    parts.append(jnp.zeros((BLOCK - 8 * len(parts), BLOCK), F32))
    columns = jnp.transpose(jnp.concatenate(parts, axis=0))
    columns_out[...] = columns
    own_rows[...] = own

    logits = dot(rank_part, w_up[...].astype(F32), precision=HIGHEST) + bias[...]
    log_decay = (jnp.minimum(logits, 0.0) - jnp.log(1.0 + jnp.exp(-jnp.abs(logits)))) / 16.0
    row_iota = lax.broadcasted_iota(jnp.int32, (BLOCK, BLOCK), 0)
    col_iota = lax.broadcasted_iota(jnp.int32, (BLOCK, BLOCK), 1)
    lower = jnp.where(row_iota >= col_iota, 1.0, 0.0).astype(F32)
    cum = dot(lower, log_decay, precision=HIGHEST)
    cumulated[...] = cum

    keys = conv(dot(rows, w_key[...]), taps_k, extended_k, columns)
    values = conv(dot(rows, w_value[...]), taps_v, extended_v, columns).astype(BF16)
    keys_out[...] = keys
    values_out[...] = values
    final = cum[BLOCK - 1 :, :]
    pushed = jnp.where(columns[:, 0:1] == columns[:, 40:41], keys * jnp.exp(final - cum), 0.0)
    state = dot(values, pushed.astype(BF16), FIRST)
    keep = jnp.where(before[0:1, 0:1] == last[0:1, 0:1], jnp.exp(final), 0.0)
    keep_rows = pair_rows(keep)
    for j in range(ROWS_Y):
        pieces[j, 0:PIECE, :] = state[j * PIECE : (j + 1) * PIECE, :].astype(BF16)
        pieces[j, PIECE:, :] = keep_rows


def block_attention(
    normed,
    w_query,
    w_gate,
    taps_q,
    head_gain,
    keys_in,
    values,
    cumulated,
    columns,
    own_rows,
    totals,
    intra,
    reach,
    gate,
    extended,
):
    del totals
    rows = normed[...]
    gate[...] = silu(dot(rows, w_gate[...])[0:BLOCK, :]) * head_gain[...]
    queries = conv(dot(rows, w_query[...]), taps_q, extended, columns) * HEAD_K ** (-0.5)
    keys, cum, seg = keys_in[...], cumulated[...], columns[:, 0:1]
    row_iota = lax.broadcasted_iota(jnp.int32, (BLOCK, BLOCK), 0)
    col_iota = lax.broadcasted_iota(jnp.int32, (BLOCK, BLOCK), 1)
    reach[...] = jnp.where(seg == columns[:, 32:33], queries * jnp.exp(cum), 0.0)
    weights = jnp.zeros((BLOCK, BLOCK), F32)
    for half in (8, 16, 32, 64):
        anchors = [
            jnp.broadcast_to(cum[b + half - 1 : b + half, :], (2 * half, HEAD_K))
            for b in range(0, BLOCK, 2 * half)
        ]
        anchor = jnp.concatenate(anchors, axis=0) if len(anchors) > 1 else anchors[0]
        factor = jnp.exp(-jnp.abs(cum - anchor))
        part = dot((queries * factor).astype(BF16), (keys * factor).astype(BF16), LAST)
        inside = (
            (row_iota // (2 * half) == col_iota // (2 * half))
            & (row_iota % (2 * half) >= half)
            & (col_iota % (2 * half) < half)
        )
        weights = jnp.where(inside, part, weights)
    groups = (BLOCK // 8, 8, HEAD_K)
    cum_g, keys_g = cum.reshape(groups), keys.reshape(groups)
    queries_g = queries.reshape(groups)
    for by in range(8):
        if by:
            spread = jnp.minimum(cum_g - pltpu.roll(cum_g, by, 1), 0.0)
            product = queries_g * pltpu.roll(keys_g, by, 1) * jnp.exp(spread)
        else:
            product = queries_g * keys_g
        sums = jnp.sum(product.reshape(BLOCK, HEAD_K), axis=1, keepdims=True)
        inside = (row_iota - col_iota == by) & (row_iota % 8 >= by)
        weights = jnp.where(inside, sums, weights)
    visible = (seg == own_rows[0:1, :]) & (row_iota >= col_iota)
    weights = jnp.where(visible, weights, 0.0)
    intra[...] = dot(weights.astype(BF16), values[...])


def row_scan(pieces, entering, kept, totals):
    state = jnp.zeros((PIECE, HEAD_K), F32)
    keep = jnp.ones((1, HEAD_K), F32)
    for j in range(ROWS_Y):
        entering[j] = state
        kept[j] = jnp.broadcast_to(keep, (8, HEAD_K))
        pair = pieces[j, PIECE:, :].astype(F32)
        decay = pair[0:1, :] + pair[1:2, :]
        state = state * decay + pieces[j, 0:PIECE, :].astype(F32)
        keep = keep * decay
    totals[0:PIECE, :] = state.astype(BF16)
    totals[PIECE:, :] = pair_rows(keep)


def carry(entering, kept, one_back, two_back, reach, states):
    del reach
    pair = one_back[PIECE:, :].astype(F32)
    decay = pair[0:1, :] + pair[1:2, :]
    arriving = one_back[0:PIECE, :].astype(F32) + decay * two_back[0:PIECE, :].astype(F32)
    for j in range(ROWS_Y):
        states[j] = (entering[j] + kept[j, 0:1, :] * arriving).astype(BF16)


def attend(index, intra, reach, incoming, gate, w_out, kept, kept_squares, sent):
    high, low = halves(reach[...])
    state = incoming[...]
    attended = intra[...] + dot(high, state, LAST) + dot(low, state, LAST)
    squares = dot(jnp.ones((8, CHUNK), F32), attended * attended, LAST, precision=HIGHEST)
    terms = dot((attended * gate[...]).astype(BF16), w_out[...])
    first = index[0] == 0
    for j in range(8):
        even = terms[:, (2 * j) * CHUNK : (2 * j + 1) * CHUNK]
        odd = terms[:, (2 * j + 1) * CHUNK : (2 * j + 2) * CHUNK]
        kept[j] = jnp.where(first, even, odd)
        sent[j * BLOCK : (j + 1) * BLOCK, :] = jnp.where(first, odd, even).astype(BF16)
    kept_squares[...] = squares
    sent[8 * BLOCK :, :] = pair_rows(squares[0:1, :])


def pair_sum(index, kept, kept_squares, both, sent):
    received = both.at[1 - index[0]]
    other = received[8 * BLOCK :, :].astype(F32)
    squares = pair_rows(kept_squares[0:1, :] + other[0:1, :] + other[1:2, :])
    for j in range(8):
        terms = kept[j] + received[j * BLOCK : (j + 1) * BLOCK, :].astype(F32)
        sent[j, 0:BLOCK, :] = terms.astype(BF16)
        sent[j, BLOCK:, :] = squares


def finish(received, hidden, mixed):
    parts = []
    for r in range(4):
        pair = received[2 * r, BLOCK:, :].astype(F32) + received[2 * r + 1, BLOCK:, :].astype(F32)
        squares = pair[0:1, :] + pair[1:2, :]
        scale = lax.rsqrt(squares / HEAD_V + 1e-05)
        parts.append(jnp.broadcast_to(scale, (8, BLOCK)))
    parts.append(jnp.zeros((BLOCK - 8 * len(parts), BLOCK), F32))
    columns = jnp.transpose(jnp.concatenate(parts, axis=0))
    total = hidden[...].astype(F32)
    for r in range(4):
        terms = received[2 * r, 0:BLOCK, :].astype(F32)
        terms = terms + received[2 * r + 1, 0:BLOCK, :].astype(F32)
        total = total + columns[:, 8 * r : 8 * r + 1] * terms
    mixed[...] = total.astype(BF16)


def shards(
    hidden_in,
    seg_ids,
    norm_gain,
    w_query,
    w_key,
    w_value,
    w_gate,
    w_decay_down,
    w_decay_up,
    decay_bias,
    conv_query,
    conv_key,
    conv_value,
    head_gain,
    w_out,
):
    block = lax.axis_index("x") * ROWS_Y + lax.axis_index("y")
    block_at = jnp.reshape(block, (1,)).astype(jnp.int32)
    core_at = jnp.reshape(lax.axis_index("core"), (1,)).astype(jnp.int32)
    blocks = ROWS_X * ROWS_Y

    onward = [(i, i + 1) for i in range(blocks - 1)]
    neighbour = lax.ppermute(hidden_in, SEQ, onward)
    needed = (
        w_key,
        norm_gain.reshape(1, WIDTH),
        w_decay_down.T,
        w_decay_up,
        decay_bias.reshape(1, HEAD_K),
        seg_ids.reshape(blocks, BLOCK),
        conv_key,
        conv_value,
        hidden_in,
    )
    key_here, gain, down, up, bias, segs, taps_k, taps_v, hidden = local_call(
        fetch,
        [(a.shape, a.dtype) for a in needed],
        block_at,
        core_at,
        *needed,
        scratch=[pltpu.SemaphoreType.DMA((len(needed),))],
        scalars=2,
        anywhere=range(2, 2 + len(needed)),
    )
    (copies,) = local_call(
        spread_out, [((8, BLOCK + 8, CHUNK), BF16)], hidden, neighbour, key_here
    )
    of_core = lax.all_to_all(copies, CHIPS, 0, 0)
    whole = lax.all_gather(of_core, "core", axis=0)
    pieces, normed, keys, values, cumulated, columns, own_rows = local_call(
        block_state,
        [
            ((ROWS_Y, PIECE + 8, HEAD_K), BF16),
            ((BLOCK + 8, WIDTH), BF16),
            ((BLOCK, HEAD_K), F32),
            ((BLOCK, CHUNK), BF16),
            ((BLOCK, HEAD_K), F32),
            ((BLOCK, BLOCK), F32),
            ((8, BLOCK), F32),
        ],
        block_at,
        whole,
        gain,
        key_here,
        w_value,
        down,
        up,
        bias,
        segs,
        taps_k,
        taps_v,
        scratch=[pltpu.VMEM((BLOCK + 8, HEAD_K), F32), pltpu.VMEM((BLOCK + 8, CHUNK), F32)],
        scalars=1,
    )
    entering, kept, totals = local_call(
        row_scan,
        [
            ((ROWS_Y, PIECE, HEAD_K), F32),
            ((ROWS_Y, 8, HEAD_K), F32),
            ((PIECE + 8, HEAD_K), BF16),
        ],
        lax.all_to_all(pieces, "y", 0, 0),
    )
    one_back = lax.ppermute(totals, "x", [(i, i + 1) for i in range(ROWS_X - 1)])
    two_back = lax.ppermute(totals, "x", [(i, i + 2) for i in range(ROWS_X - 2)])
    intra, reach, gate = local_call(
        block_attention,
        [((BLOCK, CHUNK), F32), ((BLOCK, HEAD_K), F32), ((BLOCK, CHUNK), F32)],
        normed,
        w_query,
        w_gate,
        conv_query,
        head_gain.reshape(1, CHUNK),
        keys,
        values,
        cumulated,
        columns,
        own_rows,
        totals,
        scratch=[pltpu.VMEM((BLOCK + 8, HEAD_K), F32)],
    )
    (states,) = local_call(
        carry, [((ROWS_Y, PIECE, HEAD_K), BF16)], entering, kept, one_back, two_back, reach
    )
    incoming = lax.all_to_all(states, "y", 0, 0).reshape(CHUNK, HEAD_K)
    mine, my_squares, sent = local_call(
        attend,
        [((8, BLOCK, CHUNK), F32), ((8, BLOCK), F32), ((8 * BLOCK + 8, CHUNK), BF16)],
        core_at,
        intra,
        reach,
        incoming,
        gate,
        w_out,
        scalars=1,
    )
    both = lax.all_gather(sent, "core", axis=0)
    (pairs,) = local_call(
        pair_sum, [((8, BLOCK + 8, CHUNK), BF16)], core_at, mine, my_squares, both, scalars=1
    )
    arrived = lax.all_to_all(pairs, CHIPS, 0, 0)
    (mixed,) = local_call(
        finish, [((BLOCK, CHUNK), BF16)], arrived, hidden, last=True
    )
    return mixed


def solution(mesh):
    finer = Mesh(mesh.devices.reshape(ROWS_X, ROWS_Y, 4, 2, 2), ("x", "y", "row", "zhi", "core"))
    part = ("row", "zhi", "core")
    return jax.shard_map(
        shards,
        mesh=finer,
        in_specs=(
            P(SEQ, part),
            P(),
            P(),
            P(None, "row"),
            P(None, "row"),
            P(None, part),
            P(None, part),
            P(),
            P(None, "row"),
            P("row"),
            P(None, "row"),
            P(None, "row"),
            P(None, part),
            P(("zhi", "core")),
            P(part, None),
        ),
        out_specs=P(SEQ, part),
        check_vma=False,
    )
```

```python
import jax
import jax.numpy as jnp
from jax import lax
from jax.experimental import pallas as pl
from jax.experimental.pallas import tpu as pltpu
from jax.sharding import Mesh, PartitionSpec as P

F32 = jnp.float32
BF16 = jnp.bfloat16
HIGHEST = lax.Precision.HIGHEST
HEAD_V = 512
WIDTH = 2048
BLOCK = 128
HEAD_K = 256
CHUNK = 128
LAST = (((1,), (1,)), ((), ()))
FIRST = (((0,), (0,)), ((), ()))

SEQ = ("x", "y")
CHIPS = ("row", "zhi")
ROWS_X, ROWS_Y = 4, 8
LANES = 128
PIECE = BLOCK // ROWS_Y


def local_call(kernel, outs, *args, scratch=(), scalars=0, plain=(), anywhere=(), last=False):
    elsewhere = (*range(scalars), *plain, *anywhere)
    vmem = pl.BlockSpec(memory_space=pltpu.VMEM)
    smem = pl.BlockSpec(memory_space=pltpu.SMEM)
    args = [
        pltpu.with_memory_space_constraint(a, pltpu.HBM if i in anywhere else pltpu.VMEM)
        if i in anywhere or i not in elsewhere
        else a
        for i, a in enumerate(args)
    ]
    return pl.pallas_call(
        kernel,
        out_shape=[jax.ShapeDtypeStruct(s, t) if last else pltpu.VMEM(s, t) for s, t in outs],
        in_specs=[
            smem if i < scalars else pl.BlockSpec(memory_space=pltpu.HBM) if i in anywhere else vmem
            for i in range(len(args))
        ],
        out_specs=[vmem] * len(outs),
        scratch_shapes=list(scratch),
        name=kernel.__name__,
        compiler_params=pltpu.CompilerParams(vmem_limit_bytes=16 << 20),
    )(*args)


def dot(a, b, dims=(((1,), (0,)), ((), ())), precision=None):
    return lax.dot_general(a, b, dims, precision=precision, preferred_element_type=F32)


def halves(value):
    high = value.astype(BF16)
    return high, (value - high.astype(F32)).astype(BF16)


def pair_rows(value):
    high, low = halves(value)
    shape = (8, value.shape[1])
    index = lax.broadcasted_iota(jnp.int32, shape, 0)
    both = jnp.where(
        index == 0,
        jnp.broadcast_to(high.astype(F32), shape),
        jnp.where(index == 1, jnp.broadcast_to(low.astype(F32), shape), 0.0),
    )
    return both.astype(BF16)


def pair_lanes(value):
    shape = (8, LANES)
    index = lax.broadcasted_iota(jnp.int32, shape, 0)
    out = jnp.zeros(shape, F32)
    for i, part in enumerate(halves(value)):
        for j in range(2):
            row = part.astype(F32)[:, j * LANES : (j + 1) * LANES]
            out = jnp.where(index == 2 * i + j, jnp.broadcast_to(row, shape), out)
    return out.astype(BF16)


def unpaired(piece):
    wide = piece.astype(F32)
    state = jnp.concatenate([wide[0:PIECE], wide[PIECE : 2 * PIECE]], axis=1)
    rows = wide[2 * PIECE :]
    decay = jnp.concatenate([rows[0:1] + rows[2:3], rows[1:2] + rows[3:4]], axis=1)
    return state, decay


def silu(value):
    return value * jax.nn.sigmoid(value)


def fetch(index, core, *refs):
    del index, core
    count = (len(refs) - 1) // 2
    arrived = refs[-1]
    copies = [
        pltpu.make_async_copy(refs[i], refs[count + i], arrived.at[i]) for i in range(count)
    ]
    for copy in copies:
        copy.start()
    for copy in copies:
        copy.wait()


def spread_out(hidden, neighbour, w_key, copies):
    del w_key
    edge = neighbour[BLOCK - 8 :, :]
    for j in range(8):
        copies[j, 0:BLOCK, :] = hidden[...]
        copies[j, BLOCK:, :] = edge


def conv(pre, taps, extended, columns):
    extended[0:8, :] = pre[BLOCK:, :]
    extended[8:, :] = pre[0:BLOCK, :]
    seg = columns[:, 0:1]
    total = taps[0:1, :] * pre[0:BLOCK, :]
    for j in range(1, 4):
        same = columns[:, 8 * j : 8 * j + 1] == seg
        total = total + jnp.where(
            same, taps[j : j + 1, :] * extended[8 - j : 8 - j + BLOCK, :], 0.0
        )
    return silu(total)


def block_state(
    index,
    whole,
    gain,
    w_key,
    w_value,
    w_down,
    w_up,
    bias,
    seg_ids,
    taps_k,
    taps_v,
    pieces,
    normed,
    keys_out,
    values_out,
    cumulated,
    columns_out,
    own_rows,
    extended_k,
    extended_v,
):
    chunks = WIDTH // CHUNK
    squares = jnp.zeros((BLOCK + 8, CHUNK), F32)
    for f in range(chunks):
        activ = whole[f % 2, f // 2].astype(F32)
        squares = squares + activ * activ
    scale = lax.rsqrt(jnp.sum(squares, axis=1, keepdims=True) / WIDTH + 1e-06)
    for f in range(chunks):
        lanes = slice(f * CHUNK, (f + 1) * CHUNK)
        activ = whole[f % 2, f // 2].astype(F32)
        normed[:, lanes] = (activ * scale * gain[:, lanes]).astype(BF16)
    rows = normed[...]
    rank_part = dot(rows, w_down[...], LAST)[0:BLOCK, :]

    at = index[0]
    own = seg_ids[pl.ds(at, 1), :].astype(F32)
    before = seg_ids[pl.ds(jnp.maximum(at - 1, 0), 1), :].astype(F32)
    before = jnp.where(at > 0, before, -1.0)
    own = jnp.broadcast_to(own, (8, BLOCK))
    before = jnp.broadcast_to(before, (8, BLOCK))
    lane = lax.broadcasted_iota(jnp.int32, (8, BLOCK), 1)
    parts = [own]
    for j in range(1, 4):
        parts.append(jnp.where(lane < j, pltpu.roll(before, j, 1), pltpu.roll(own, j, 1)))
    before = jnp.broadcast_to(before[:, BLOCK - 1 :], (8, BLOCK))
    last = jnp.broadcast_to(own[:, BLOCK - 1 :], (8, BLOCK))
    parts += [before, last]
    parts.append(jnp.zeros((BLOCK - 8 * len(parts), BLOCK), F32))
    columns = jnp.transpose(jnp.concatenate(parts, axis=0))
    columns_out[...] = columns
    own_rows[...] = own

    logits = dot(rank_part, w_up[...].astype(F32), precision=HIGHEST) + bias[...]
    log_decay = (jnp.minimum(logits, 0.0) - jnp.log(1.0 + jnp.exp(-jnp.abs(logits)))) / 16.0
    row_iota = lax.broadcasted_iota(jnp.int32, (BLOCK, BLOCK), 0)
    col_iota = lax.broadcasted_iota(jnp.int32, (BLOCK, BLOCK), 1)
    lower = jnp.where(row_iota >= col_iota, 1.0, 0.0).astype(F32)
    cum = dot(lower, log_decay, precision=HIGHEST)
    cumulated[...] = cum

    keys = conv(dot(rows, w_key[...]), taps_k, extended_k, columns)
    values = conv(dot(rows, w_value[...]), taps_v, extended_v, columns).astype(BF16)
    keys_out[...] = keys
    values_out[...] = values
    final = cum[BLOCK - 1 :, :]
    pushed = jnp.where(columns[:, 0:1] == columns[:, 40:41], keys * jnp.exp(final - cum), 0.0)
    state = dot(values, pushed.astype(BF16), FIRST)
    keep = jnp.where(before[0:1, 0:1] == last[0:1, 0:1], jnp.exp(final), 0.0)
    keep_rows = pair_lanes(keep)
    for j in range(ROWS_Y):
        piece = state[j * PIECE : (j + 1) * PIECE, :].astype(BF16)
        pieces[j, 0:PIECE, :] = piece[:, :LANES]
        pieces[j, PIECE : 2 * PIECE, :] = piece[:, LANES:]
        pieces[j, 2 * PIECE :, :] = keep_rows


def block_attention(
    normed,
    w_query,
    w_gate,
    taps_q,
    head_gain,
    keys_in,
    values,
    cumulated,
    columns,
    own_rows,
    totals,
    intra,
    reach,
    gate,
    extended,
):
    del totals
    rows = normed[...]
    gate[...] = silu(dot(rows, w_gate[...])[0:BLOCK, :]) * head_gain[...]
    queries = conv(dot(rows, w_query[...]), taps_q, extended, columns) * HEAD_K ** (-0.5)
    keys, cum, seg = keys_in[...], cumulated[...], columns[:, 0:1]
    row_iota = lax.broadcasted_iota(jnp.int32, (BLOCK, BLOCK), 0)
    col_iota = lax.broadcasted_iota(jnp.int32, (BLOCK, BLOCK), 1)
    reach[...] = jnp.where(seg == columns[:, 32:33], queries * jnp.exp(cum), 0.0)
    weights = jnp.zeros((BLOCK, BLOCK), F32)
    for half in (8, 16, 32, 64):
        anchors = [
            jnp.broadcast_to(cum[b + half - 1 : b + half, :], (2 * half, HEAD_K))
            for b in range(0, BLOCK, 2 * half)
        ]
        anchor = jnp.concatenate(anchors, axis=0) if len(anchors) > 1 else anchors[0]
        factor = jnp.exp(-jnp.abs(cum - anchor))
        part = dot((queries * factor).astype(BF16), (keys * factor).astype(BF16), LAST)
        inside = (
            (row_iota // (2 * half) == col_iota // (2 * half))
            & (row_iota % (2 * half) >= half)
            & (col_iota % (2 * half) < half)
        )
        weights = jnp.where(inside, part, weights)
    groups = (BLOCK // 8, 8, HEAD_K)
    cum_g, keys_g = cum.reshape(groups), keys.reshape(groups)
    queries_g = queries.reshape(groups)
    for by in range(8):
        if by:
            spread = jnp.minimum(cum_g - pltpu.roll(cum_g, by, 1), 0.0)
            product = queries_g * pltpu.roll(keys_g, by, 1) * jnp.exp(spread)
        else:
            product = queries_g * keys_g
        sums = jnp.sum(product.reshape(BLOCK, HEAD_K), axis=1, keepdims=True)
        inside = (row_iota - col_iota == by) & (row_iota % 8 >= by)
        weights = jnp.where(inside, sums, weights)
    visible = (seg == own_rows[0:1, :]) & (row_iota >= col_iota)
    weights = jnp.where(visible, weights, 0.0)
    intra[...] = dot(weights.astype(BF16), values[...])


def row_scan(pieces, entering, kept, totals):
    state = jnp.zeros((PIECE, HEAD_K), F32)
    keep = jnp.ones((1, HEAD_K), F32)
    for j in range(ROWS_Y):
        entering[j] = state
        kept[j] = jnp.broadcast_to(keep, (8, HEAD_K))
        both, decay = unpaired(pieces[j])
        state = state * decay + both
        keep = keep * decay
    totals[0:PIECE, :] = state[:, :LANES].astype(BF16)
    totals[PIECE : 2 * PIECE, :] = state[:, LANES:].astype(BF16)
    totals[2 * PIECE :, :] = pair_lanes(keep)


def carry(entering, kept, two_back, one_back, reach, states):
    del reach
    near, decay = unpaired(one_back[...])
    arriving = near + decay * unpaired(two_back[...])[0]
    for j in range(ROWS_Y):
        states[j] = (entering[j] + kept[j, 0:1, :] * arriving).astype(BF16)


def attend(index, intra, reach, incoming, gate, w_out, kept, kept_squares, sent):
    high, low = halves(reach[...])
    state = incoming[...]
    attended = intra[...] + dot(high, state, LAST) + dot(low, state, LAST)
    squares = dot(jnp.ones((8, CHUNK), F32), attended * attended, LAST, precision=HIGHEST)
    terms = dot((attended * gate[...]).astype(BF16), w_out[...])
    first = index[0] == 0
    for j in range(8):
        even = terms[:, (2 * j) * CHUNK : (2 * j + 1) * CHUNK]
        odd = terms[:, (2 * j + 1) * CHUNK : (2 * j + 2) * CHUNK]
        kept[j] = jnp.where(first, even, odd)
        sent[j * BLOCK : (j + 1) * BLOCK, :] = jnp.where(first, odd, even).astype(BF16)
    kept_squares[...] = squares
    sent[8 * BLOCK :, :] = pair_rows(squares[0:1, :])


def pair_sum(index, kept, kept_squares, both, sent):
    received = both.at[1 - index[0]]
    other = received[8 * BLOCK :, :].astype(F32)
    squares = pair_rows(kept_squares[0:1, :] + other[0:1, :] + other[1:2, :])
    for j in range(8):
        terms = kept[j] + received[j * BLOCK : (j + 1) * BLOCK, :].astype(F32)
        sent[j, 0:BLOCK, :] = terms.astype(BF16)
        sent[j, BLOCK:, :] = squares


def finish(received, hidden, mixed):
    parts = []
    for r in range(4):
        pair = received[2 * r, BLOCK:, :].astype(F32) + received[2 * r + 1, BLOCK:, :].astype(F32)
        squares = pair[0:1, :] + pair[1:2, :]
        scale = lax.rsqrt(squares / HEAD_V + 1e-05)
        parts.append(jnp.broadcast_to(scale, (8, BLOCK)))
    parts.append(jnp.zeros((BLOCK - 8 * len(parts), BLOCK), F32))
    columns = jnp.transpose(jnp.concatenate(parts, axis=0))
    total = hidden[...].astype(F32)
    for r in range(4):
        terms = received[2 * r, 0:BLOCK, :].astype(F32)
        terms = terms + received[2 * r + 1, 0:BLOCK, :].astype(F32)
        total = total + columns[:, 8 * r : 8 * r + 1] * terms
    mixed[...] = total.astype(BF16)


def shards(
    hidden_in,
    seg_ids,
    norm_gain,
    w_query,
    w_key,
    w_value,
    w_gate,
    w_decay_down,
    w_decay_up,
    decay_bias,
    conv_query,
    conv_key,
    conv_value,
    head_gain,
    w_out,
):
    block = lax.axis_index("x") * ROWS_Y + lax.axis_index("y")
    block_at = jnp.reshape(block, (1,)).astype(jnp.int32)
    core_at = jnp.reshape(lax.axis_index("core"), (1,)).astype(jnp.int32)
    blocks = ROWS_X * ROWS_Y

    onward = [(i, i + 1) for i in range(blocks - 1)]
    neighbour = lax.ppermute(hidden_in, SEQ, onward)
    needed = (
        w_key,
        norm_gain.reshape(1, WIDTH),
        w_decay_down.T,
        w_decay_up,
        decay_bias.reshape(1, HEAD_K),
        seg_ids.reshape(blocks, BLOCK),
        conv_key,
        conv_value,
        hidden_in,
    )
    key_here, gain, down, up, bias, segs, taps_k, taps_v, hidden = local_call(
        fetch,
        [(a.shape, a.dtype) for a in needed],
        block_at,
        core_at,
        *needed,
        scratch=[pltpu.SemaphoreType.DMA((len(needed),))],
        scalars=2,
        anywhere=range(2, 2 + len(needed)),
    )
    (copies,) = local_call(
        spread_out, [((8, BLOCK + 8, CHUNK), BF16)], hidden, neighbour, key_here
    )
    of_core = lax.all_to_all(copies, CHIPS, 0, 0)
    whole = lax.all_gather(of_core, "core", axis=0)
    pieces, normed, keys, values, cumulated, columns, own_rows = local_call(
        block_state,
        [
            ((ROWS_Y, 2 * PIECE + 8, LANES), BF16),
            ((BLOCK + 8, WIDTH), BF16),
            ((BLOCK, HEAD_K), F32),
            ((BLOCK, CHUNK), BF16),
            ((BLOCK, HEAD_K), F32),
            ((BLOCK, BLOCK), F32),
            ((8, BLOCK), F32),
        ],
        block_at,
        whole,
        gain,
        key_here,
        w_value,
        down,
        up,
        bias,
        segs,
        taps_k,
        taps_v,
        scratch=[pltpu.VMEM((BLOCK + 8, HEAD_K), F32), pltpu.VMEM((BLOCK + 8, CHUNK), F32)],
        scalars=1,
    )
    entering, kept, totals = local_call(
        row_scan,
        [
            ((ROWS_Y, PIECE, HEAD_K), F32),
            ((ROWS_Y, 8, HEAD_K), F32),
            ((2 * PIECE + 8, LANES), BF16),
        ],
        lax.all_to_all(pieces, "y", 0, 0),
    )
    one_back = lax.ppermute(totals, "x", [(i, i + 1) for i in range(ROWS_X - 1)])
    two_back = lax.ppermute(totals, "x", [(i, i + 2) for i in range(ROWS_X - 2)])
    intra, reach, gate = local_call(
        block_attention,
        [((BLOCK, CHUNK), F32), ((BLOCK, HEAD_K), F32), ((BLOCK, CHUNK), F32)],
        normed,
        w_query,
        w_gate,
        conv_query,
        head_gain.reshape(1, CHUNK),
        keys,
        values,
        cumulated,
        columns,
        own_rows,
        totals,
        scratch=[pltpu.VMEM((BLOCK + 8, HEAD_K), F32)],
    )
    (states,) = local_call(
        carry, [((ROWS_Y, PIECE, HEAD_K), BF16)], entering, kept, two_back, one_back, reach
    )
    incoming = lax.all_to_all(states, "y", 0, 0).reshape(CHUNK, HEAD_K)
    mine, my_squares, sent = local_call(
        attend,
        [((8, BLOCK, CHUNK), F32), ((8, BLOCK), F32), ((8 * BLOCK + 8, CHUNK), BF16)],
        core_at,
        intra,
        reach,
        incoming,
        gate,
        w_out,
        scalars=1,
    )
    both = lax.all_gather(sent, "core", axis=0)
    (pairs,) = local_call(
        pair_sum, [((8, BLOCK + 8, CHUNK), BF16)], core_at, mine, my_squares, both, scalars=1
    )
    arrived = lax.all_to_all(pairs, CHIPS, 0, 0)
    (mixed,) = local_call(
        finish, [((BLOCK, CHUNK), BF16)], arrived, hidden, last=True
    )
    return mixed


def solution(mesh):
    finer = Mesh(mesh.devices.reshape(ROWS_X, ROWS_Y, 4, 2, 2), ("x", "y", "row", "zhi", "core"))
    part = ("row", "zhi", "core")
    return jax.shard_map(
        shards,
        mesh=finer,
        in_specs=(
            P(SEQ, part),
            P(),
            P(),
            P(None, "row"),
            P(None, "row"),
            P(None, part),
            P(None, part),
            P(),
            P(None, "row"),
            P("row"),
            P(None, "row"),
            P(None, "row"),
            P(None, part),
            P(("zhi", "core")),
            P(part, None),
        ),
        out_specs=P(SEQ, part),
        check_vma=False,
    )
```

```python
import jax
import jax.numpy as jnp
from jax import lax
from jax.experimental import pallas as pl
from jax.experimental.pallas import tpu as pltpu
from jax.sharding import Mesh, PartitionSpec as P

F32 = jnp.float32
BF16 = jnp.bfloat16
HIGHEST = lax.Precision.HIGHEST
HEAD_V = 512
WIDTH = 2048
BLOCK = 128
HEAD_K = 256
CHUNK = 128
LAST = (((1,), (1,)), ((), ()))
FIRST = (((0,), (0,)), ((), ()))

SEQ = ("x", "y")
CHIPS = ("row", "zhi")
ROWS_X, ROWS_Y = 4, 8
LANES = 128
PIECE = BLOCK // ROWS_Y


def local_call(kernel, outs, *args, scratch=(), scalars=0, plain=(), anywhere=(), last=False):
    elsewhere = (*range(scalars), *plain, *anywhere)
    vmem = pl.BlockSpec(memory_space=pltpu.VMEM)
    smem = pl.BlockSpec(memory_space=pltpu.SMEM)
    args = [
        pltpu.with_memory_space_constraint(a, pltpu.HBM if i in anywhere else pltpu.VMEM)
        if i in anywhere or i not in elsewhere
        else a
        for i, a in enumerate(args)
    ]
    return pl.pallas_call(
        kernel,
        out_shape=[jax.ShapeDtypeStruct(s, t) if last else pltpu.VMEM(s, t) for s, t in outs],
        in_specs=[
            smem if i < scalars else pl.BlockSpec(memory_space=pltpu.HBM) if i in anywhere else vmem
            for i in range(len(args))
        ],
        out_specs=[vmem] * len(outs),
        scratch_shapes=list(scratch),
        name=kernel.__name__,
        compiler_params=pltpu.CompilerParams(vmem_limit_bytes=16 << 20),
    )(*args)


def dot(a, b, dims=(((1,), (0,)), ((), ())), precision=None):
    return lax.dot_general(a, b, dims, precision=precision, preferred_element_type=F32)


def halves(value):
    high = value.astype(BF16)
    return high, (value - high.astype(F32)).astype(BF16)


def pair_rows(value):
    high, low = halves(value)
    shape = (8, value.shape[1])
    index = lax.broadcasted_iota(jnp.int32, shape, 0)
    both = jnp.where(
        index == 0,
        jnp.broadcast_to(high.astype(F32), shape),
        jnp.where(index == 1, jnp.broadcast_to(low.astype(F32), shape), 0.0),
    )
    return both.astype(BF16)


def pair_lanes(value):
    shape = (8, LANES)
    index = lax.broadcasted_iota(jnp.int32, shape, 0)
    out = jnp.zeros(shape, F32)
    for i, part in enumerate(halves(value)):
        for j in range(2):
            row = part.astype(F32)[:, j * LANES : (j + 1) * LANES]
            out = jnp.where(index == 2 * i + j, jnp.broadcast_to(row, shape), out)
    return out.astype(BF16)


def unpaired(piece):
    wide = piece.astype(F32)
    state = jnp.concatenate([wide[0:PIECE], wide[PIECE : 2 * PIECE]], axis=1)
    rows = wide[2 * PIECE :]
    decay = jnp.concatenate([rows[0:1] + rows[2:3], rows[1:2] + rows[3:4]], axis=1)
    return state, decay


def silu(value):
    return value * jax.nn.sigmoid(value)


def fetch(index, core, *refs):
    del index, core
    count = (len(refs) - 1) // 2
    arrived = refs[-1]
    copies = [
        pltpu.make_async_copy(refs[i], refs[count + i], arrived.at[i]) for i in range(count)
    ]
    for copy in copies:
        copy.start()
    for copy in copies:
        copy.wait()


def spread_out(hidden, neighbour, w_key, copies):
    del w_key
    edge = neighbour[BLOCK - 8 :, :]
    for j in range(8):
        copies[j, 0:BLOCK, :] = hidden[...]
        copies[j, BLOCK:, :] = edge


def conv(pre, taps, extended, columns):
    extended[0:8, :] = pre[BLOCK:, :]
    extended[8:, :] = pre[0:BLOCK, :]
    seg = columns[:, 0:1]
    total = taps[0:1, :] * pre[0:BLOCK, :]
    for j in range(1, 4):
        same = columns[:, 8 * j : 8 * j + 1] == seg
        total = total + jnp.where(
            same, taps[j : j + 1, :] * extended[8 - j : 8 - j + BLOCK, :], 0.0
        )
    return silu(total)


def block_state(
    index,
    whole,
    gain,
    w_key,
    w_value,
    w_down,
    w_up,
    bias,
    seg_ids,
    taps_k,
    taps_v,
    pieces,
    normed,
    keys_out,
    values_out,
    cumulated,
    columns_out,
    own_rows,
    extended_k,
    extended_v,
):
    chunks = WIDTH // CHUNK
    squares = jnp.zeros((BLOCK + 8, CHUNK), F32)
    for f in range(chunks):
        activ = whole[f % 2, f // 2].astype(F32)
        squares = squares + activ * activ
    scale = lax.rsqrt(jnp.sum(squares, axis=1, keepdims=True) / WIDTH + 1e-06)
    for f in range(chunks):
        lanes = slice(f * CHUNK, (f + 1) * CHUNK)
        activ = whole[f % 2, f // 2].astype(F32)
        normed[:, lanes] = (activ * scale * gain[:, lanes]).astype(BF16)
    rows = normed[...]
    rank_part = dot(rows, w_down[...], LAST)[0:BLOCK, :]

    at = index[0]
    own = seg_ids[pl.ds(at, 1), :].astype(F32)
    before = seg_ids[pl.ds(jnp.maximum(at - 1, 0), 1), :].astype(F32)
    before = jnp.where(at > 0, before, -1.0)
    own = jnp.broadcast_to(own, (8, BLOCK))
    before = jnp.broadcast_to(before, (8, BLOCK))
    lane = lax.broadcasted_iota(jnp.int32, (8, BLOCK), 1)
    parts = [own]
    for j in range(1, 4):
        parts.append(jnp.where(lane < j, pltpu.roll(before, j, 1), pltpu.roll(own, j, 1)))
    before = jnp.broadcast_to(before[:, BLOCK - 1 :], (8, BLOCK))
    last = jnp.broadcast_to(own[:, BLOCK - 1 :], (8, BLOCK))
    parts += [before, last]
    parts.append(jnp.zeros((BLOCK - 8 * len(parts), BLOCK), F32))
    columns = jnp.transpose(jnp.concatenate(parts, axis=0))
    columns_out[...] = columns
    own_rows[...] = own

    logits = dot(rank_part, w_up[...].astype(F32), precision=HIGHEST) + bias[...]
    log_decay = (jnp.minimum(logits, 0.0) - jnp.log(1.0 + jnp.exp(-jnp.abs(logits)))) / 16.0
    row_iota = lax.broadcasted_iota(jnp.int32, (BLOCK, BLOCK), 0)
    col_iota = lax.broadcasted_iota(jnp.int32, (BLOCK, BLOCK), 1)
    lower = jnp.where(row_iota >= col_iota, 1.0, 0.0).astype(F32)
    cum = dot(lower, log_decay, precision=HIGHEST)
    cumulated[...] = cum

    keys = conv(dot(rows, w_key[...]), taps_k, extended_k, columns)
    values = conv(dot(rows, w_value[...]), taps_v, extended_v, columns).astype(BF16)
    keys_out[...] = keys
    values_out[...] = values
    final = cum[BLOCK - 1 :, :]
    pushed = jnp.where(columns[:, 0:1] == columns[:, 40:41], keys * jnp.exp(final - cum), 0.0)
    state = dot(values, pushed.astype(BF16), FIRST)
    keep = jnp.where(before[0:1, 0:1] == last[0:1, 0:1], jnp.exp(final), 0.0)
    keep_rows = pair_lanes(keep)
    for j in range(ROWS_Y):
        piece = state[j * PIECE : (j + 1) * PIECE, :].astype(BF16)
        pieces[j, 0:PIECE, :] = piece[:, :LANES]
        pieces[j, PIECE : 2 * PIECE, :] = piece[:, LANES:]
        pieces[j, 2 * PIECE :, :] = keep_rows


def block_attention(
    normed,
    w_query,
    w_gate,
    taps_q,
    head_gain,
    keys_in,
    values,
    cumulated,
    columns,
    own_rows,
    totals,
    intra,
    reach,
    gate,
    extended,
):
    del totals
    rows = normed[...]
    gate[...] = silu(dot(rows, w_gate[...])[0:BLOCK, :]) * head_gain[...]
    queries = conv(dot(rows, w_query[...]), taps_q, extended, columns) * HEAD_K ** (-0.5)
    keys, cum, seg = keys_in[...], cumulated[...], columns[:, 0:1]
    row_iota = lax.broadcasted_iota(jnp.int32, (BLOCK, BLOCK), 0)
    col_iota = lax.broadcasted_iota(jnp.int32, (BLOCK, BLOCK), 1)
    reach[...] = jnp.where(seg == columns[:, 32:33], queries * jnp.exp(cum), 0.0)
    weights = jnp.zeros((BLOCK, BLOCK), F32)
    for half in (8, 16, 32, 64):
        anchors = [
            jnp.broadcast_to(cum[b + half - 1 : b + half, :], (2 * half, HEAD_K))
            for b in range(0, BLOCK, 2 * half)
        ]
        anchor = jnp.concatenate(anchors, axis=0) if len(anchors) > 1 else anchors[0]
        factor = jnp.exp(-jnp.abs(cum - anchor))
        part = dot((queries * factor).astype(BF16), (keys * factor).astype(BF16), LAST)
        inside = (
            (row_iota // (2 * half) == col_iota // (2 * half))
            & (row_iota % (2 * half) >= half)
            & (col_iota % (2 * half) < half)
        )
        weights = jnp.where(inside, part, weights)
    groups = (BLOCK // 8, 8, HEAD_K)
    cum_g, keys_g = cum.reshape(groups), keys.reshape(groups)
    queries_g = queries.reshape(groups)
    for by in range(8):
        if by:
            spread = jnp.minimum(cum_g - pltpu.roll(cum_g, by, 1), 0.0)
            product = queries_g * pltpu.roll(keys_g, by, 1) * jnp.exp(spread)
        else:
            product = queries_g * keys_g
        sums = jnp.sum(product.reshape(BLOCK, HEAD_K), axis=1, keepdims=True)
        inside = (row_iota - col_iota == by) & (row_iota % 8 >= by)
        weights = jnp.where(inside, sums, weights)
    visible = (seg == own_rows[0:1, :]) & (row_iota >= col_iota)
    weights = jnp.where(visible, weights, 0.0)
    intra[...] = dot(weights.astype(BF16), values[...])


def row_scan(pieces, entering, kept, totals):
    state = jnp.zeros((PIECE, HEAD_K), F32)
    keep = jnp.ones((1, HEAD_K), F32)
    for j in range(ROWS_Y):
        entering[j] = state
        kept[j] = jnp.broadcast_to(keep, (8, HEAD_K))
        both, decay = unpaired(pieces[j])
        state = state * decay + both
        keep = keep * decay
    last = pair_lanes(keep)
    for x in range(ROWS_X):
        totals[x, 0:PIECE, :] = state[:, :LANES].astype(BF16)
        totals[x, PIECE : 2 * PIECE, :] = state[:, LANES:].astype(BF16)
        totals[x, 2 * PIECE :, :] = last


def carry(index, rows, entering, kept, reach, states):
    del reach
    row = index[0] // ROWS_Y

    def back(by):
        state, decay = unpaired(rows[jnp.maximum(row - by, 0)])
        return jnp.where(row >= by, state, 0.0), decay

    near, decay = back(1)
    arriving = near + decay * back(2)[0]
    for j in range(ROWS_Y):
        states[j] = (entering[j] + kept[j, 0:1, :] * arriving).astype(BF16)


def attend(index, intra, reach, incoming, gate, w_out, kept, kept_squares, sent):
    high, low = halves(reach[...])
    state = incoming[...]
    attended = intra[...] + dot(high, state, LAST) + dot(low, state, LAST)
    squares = dot(jnp.ones((8, CHUNK), F32), attended * attended, LAST, precision=HIGHEST)
    terms = dot((attended * gate[...]).astype(BF16), w_out[...])
    first = index[0] == 0
    for j in range(8):
        even = terms[:, (2 * j) * CHUNK : (2 * j + 1) * CHUNK]
        odd = terms[:, (2 * j + 1) * CHUNK : (2 * j + 2) * CHUNK]
        kept[j] = jnp.where(first, even, odd)
        sent[j * BLOCK : (j + 1) * BLOCK, :] = jnp.where(first, odd, even).astype(BF16)
    kept_squares[...] = squares
    sent[8 * BLOCK :, :] = pair_rows(squares[0:1, :])


def pair_sum(index, kept, kept_squares, both, sent):
    received = both.at[1 - index[0]]
    other = received[8 * BLOCK :, :].astype(F32)
    squares = pair_rows(kept_squares[0:1, :] + other[0:1, :] + other[1:2, :])
    for j in range(8):
        terms = kept[j] + received[j * BLOCK : (j + 1) * BLOCK, :].astype(F32)
        sent[j, 0:BLOCK, :] = terms.astype(BF16)
        sent[j, BLOCK:, :] = squares


def finish(received, hidden, mixed):
    parts = []
    for r in range(4):
        pair = received[2 * r, BLOCK:, :].astype(F32) + received[2 * r + 1, BLOCK:, :].astype(F32)
        squares = pair[0:1, :] + pair[1:2, :]
        scale = lax.rsqrt(squares / HEAD_V + 1e-05)
        parts.append(jnp.broadcast_to(scale, (8, BLOCK)))
    parts.append(jnp.zeros((BLOCK - 8 * len(parts), BLOCK), F32))
    columns = jnp.transpose(jnp.concatenate(parts, axis=0))
    total = hidden[...].astype(F32)
    for r in range(4):
        terms = received[2 * r, 0:BLOCK, :].astype(F32)
        terms = terms + received[2 * r + 1, 0:BLOCK, :].astype(F32)
        total = total + columns[:, 8 * r : 8 * r + 1] * terms
    mixed[...] = total.astype(BF16)


def shards(
    hidden_in,
    seg_ids,
    norm_gain,
    w_query,
    w_key,
    w_value,
    w_gate,
    w_decay_down,
    w_decay_up,
    decay_bias,
    conv_query,
    conv_key,
    conv_value,
    head_gain,
    w_out,
):
    block = lax.axis_index("x") * ROWS_Y + lax.axis_index("y")
    block_at = jnp.reshape(block, (1,)).astype(jnp.int32)
    core_at = jnp.reshape(lax.axis_index("core"), (1,)).astype(jnp.int32)
    blocks = ROWS_X * ROWS_Y

    onward = [(i, i + 1) for i in range(blocks - 1)]
    neighbour = lax.ppermute(hidden_in, SEQ, onward)
    needed = (
        w_key,
        norm_gain.reshape(1, WIDTH),
        w_decay_down.T,
        w_decay_up,
        decay_bias.reshape(1, HEAD_K),
        seg_ids.reshape(blocks, BLOCK),
        conv_key,
        conv_value,
        hidden_in,
    )
    key_here, gain, down, up, bias, segs, taps_k, taps_v, hidden = local_call(
        fetch,
        [(a.shape, a.dtype) for a in needed],
        block_at,
        core_at,
        *needed,
        scratch=[pltpu.SemaphoreType.DMA((len(needed),))],
        scalars=2,
        anywhere=range(2, 2 + len(needed)),
    )
    (copies,) = local_call(
        spread_out, [((8, BLOCK + 8, CHUNK), BF16)], hidden, neighbour, key_here
    )
    of_core = lax.all_to_all(copies, CHIPS, 0, 0)
    whole = lax.all_gather(of_core, "core", axis=0)
    pieces, normed, keys, values, cumulated, columns, own_rows = local_call(
        block_state,
        [
            ((ROWS_Y, 2 * PIECE + 8, LANES), BF16),
            ((BLOCK + 8, WIDTH), BF16),
            ((BLOCK, HEAD_K), F32),
            ((BLOCK, CHUNK), BF16),
            ((BLOCK, HEAD_K), F32),
            ((BLOCK, BLOCK), F32),
            ((8, BLOCK), F32),
        ],
        block_at,
        whole,
        gain,
        key_here,
        w_value,
        down,
        up,
        bias,
        segs,
        taps_k,
        taps_v,
        scratch=[pltpu.VMEM((BLOCK + 8, HEAD_K), F32), pltpu.VMEM((BLOCK + 8, CHUNK), F32)],
        scalars=1,
    )
    entering, kept, totals = local_call(
        row_scan,
        [
            ((ROWS_Y, PIECE, HEAD_K), F32),
            ((ROWS_Y, 8, HEAD_K), F32),
            ((ROWS_X, 2 * PIECE + 8, LANES), BF16),
        ],
        lax.all_to_all(pieces, "y", 0, 0),
    )
    rows = lax.all_to_all(totals, "x", 0, 0)
    intra, reach, gate = local_call(
        block_attention,
        [((BLOCK, CHUNK), F32), ((BLOCK, HEAD_K), F32), ((BLOCK, CHUNK), F32)],
        normed,
        w_query,
        w_gate,
        conv_query,
        head_gain.reshape(1, CHUNK),
        keys,
        values,
        cumulated,
        columns,
        own_rows,
        totals,
        scratch=[pltpu.VMEM((BLOCK + 8, HEAD_K), F32)],
    )
    (states,) = local_call(
        carry,
        [((ROWS_Y, PIECE, HEAD_K), BF16)],
        block_at,
        rows,
        entering,
        kept,
        reach,
        scalars=1,
    )
    incoming = lax.all_to_all(states, "y", 0, 0).reshape(CHUNK, HEAD_K)
    mine, my_squares, sent = local_call(
        attend,
        [((8, BLOCK, CHUNK), F32), ((8, BLOCK), F32), ((8 * BLOCK + 8, CHUNK), BF16)],
        core_at,
        intra,
        reach,
        incoming,
        gate,
        w_out,
        scalars=1,
    )
    both = lax.all_gather(sent, "core", axis=0)
    (pairs,) = local_call(
        pair_sum, [((8, BLOCK + 8, CHUNK), BF16)], core_at, mine, my_squares, both, scalars=1
    )
    arrived = lax.all_to_all(pairs, CHIPS, 0, 0)
    (mixed,) = local_call(
        finish, [((BLOCK, CHUNK), BF16)], arrived, hidden, last=True
    )
    return mixed


def solution(mesh):
    finer = Mesh(mesh.devices.reshape(ROWS_X, ROWS_Y, 4, 2, 2), ("x", "y", "row", "zhi", "core"))
    part = ("row", "zhi", "core")
    return jax.shard_map(
        shards,
        mesh=finer,
        in_specs=(
            P(SEQ, part),
            P(),
            P(),
            P(None, "row"),
            P(None, "row"),
            P(None, part),
            P(None, part),
            P(),
            P(None, "row"),
            P("row"),
            P(None, "row"),
            P(None, "row"),
            P(None, part),
            P(("zhi", "core")),
            P(part, None),
        ),
        out_specs=P(SEQ, part),
        check_vma=False,
    )
```

```python
import jax
import jax.numpy as jnp
from jax import lax
from jax.experimental import pallas as pl
from jax.experimental.pallas import tpu as pltpu
from jax.sharding import Mesh, PartitionSpec as P

F32 = jnp.float32
BF16 = jnp.bfloat16
HIGHEST = lax.Precision.HIGHEST
HEAD_V = 512
WIDTH = 2048
BLOCK = 128
HEAD_K = 256
CHUNK = 128
LAST = (((1,), (1,)), ((), ()))
FIRST = (((0,), (0,)), ((), ()))

SEQ = ("x", "y")
GRID = ("y", "x")
CHIPS = ("row", "zhi")
ROWS_X, ROWS_Y = 4, 8
LANES = 128
BLOCKS = ROWS_X * ROWS_Y
PIECE = 2 * CHUNK // BLOCKS


def local_call(kernel, outs, *args, scratch=(), scalars=0, plain=(), anywhere=(), last=False):
    elsewhere = (*range(scalars), *plain, *anywhere)
    vmem = pl.BlockSpec(memory_space=pltpu.VMEM)
    smem = pl.BlockSpec(memory_space=pltpu.SMEM)
    args = [
        pltpu.with_memory_space_constraint(a, pltpu.HBM if i in anywhere else pltpu.VMEM)
        if i in anywhere or i not in elsewhere
        else a
        for i, a in enumerate(args)
    ]
    return pl.pallas_call(
        kernel,
        out_shape=[jax.ShapeDtypeStruct(s, t) if last else pltpu.VMEM(s, t) for s, t in outs],
        in_specs=[
            smem if i < scalars else pl.BlockSpec(memory_space=pltpu.HBM) if i in anywhere else vmem
            for i in range(len(args))
        ],
        out_specs=[vmem] * len(outs),
        scratch_shapes=list(scratch),
        name=kernel.__name__,
        compiler_params=pltpu.CompilerParams(vmem_limit_bytes=16 << 20),
    )(*args)


def dot(a, b, dims=(((1,), (0,)), ((), ())), precision=None):
    return lax.dot_general(a, b, dims, precision=precision, preferred_element_type=F32)


def halves(value):
    high = value.astype(BF16)
    return high, (value - high.astype(F32)).astype(BF16)


def pair_rows(value):
    high, low = halves(value)
    shape = (8, value.shape[1])
    index = lax.broadcasted_iota(jnp.int32, shape, 0)
    both = jnp.where(
        index == 0,
        jnp.broadcast_to(high.astype(F32), shape),
        jnp.where(index == 1, jnp.broadcast_to(low.astype(F32), shape), 0.0),
    )
    return both.astype(BF16)


def silu(value):
    return value * jax.nn.sigmoid(value)


def fetch(index, core, *refs):
    del index, core
    count = (len(refs) - 1) // 2
    arrived = refs[-1]
    copies = [
        pltpu.make_async_copy(refs[i], refs[count + i], arrived.at[i]) for i in range(count)
    ]
    for copy in copies:
        copy.start()
    for copy in copies:
        copy.wait()


def spread_out(hidden, neighbour, w_key, copies):
    del w_key
    edge = neighbour[BLOCK - 8 :, :]
    for j in range(8):
        copies[j, 0:BLOCK, :] = hidden[...]
        copies[j, BLOCK:, :] = edge


def conv(pre, taps, extended, columns):
    extended[0:8, :] = pre[BLOCK:, :]
    extended[8:, :] = pre[0:BLOCK, :]
    seg = columns[:, 0:1]
    total = taps[0:1, :] * pre[0:BLOCK, :]
    for j in range(1, 4):
        same = columns[:, 8 * j : 8 * j + 1] == seg
        total = total + jnp.where(
            same, taps[j : j + 1, :] * extended[8 - j : 8 - j + BLOCK, :], 0.0
        )
    return silu(total)


def block_state(
    index,
    whole,
    gain,
    w_key,
    w_value,
    w_down,
    w_up,
    bias,
    seg_ids,
    taps_k,
    taps_v,
    pieces,
    normed,
    keys_out,
    values_out,
    cumulated,
    columns_out,
    own_rows,
    extended_k,
    extended_v,
):
    chunks = WIDTH // CHUNK
    squares = jnp.zeros((BLOCK + 8, CHUNK), F32)
    for f in range(chunks):
        activ = whole[f % 2, f // 2].astype(F32)
        squares = squares + activ * activ
    scale = lax.rsqrt(jnp.sum(squares, axis=1, keepdims=True) / WIDTH + 1e-06)
    for f in range(chunks):
        lanes = slice(f * CHUNK, (f + 1) * CHUNK)
        activ = whole[f % 2, f // 2].astype(F32)
        normed[:, lanes] = (activ * scale * gain[:, lanes]).astype(BF16)
    rows = normed[...]
    rank_part = dot(rows, w_down[...], LAST)[0:BLOCK, :]

    at = index[0]
    own = seg_ids[pl.ds(at, 1), :].astype(F32)
    before = seg_ids[pl.ds(jnp.maximum(at - 1, 0), 1), :].astype(F32)
    before = jnp.where(at > 0, before, -1.0)
    own = jnp.broadcast_to(own, (8, BLOCK))
    before = jnp.broadcast_to(before, (8, BLOCK))
    lane = lax.broadcasted_iota(jnp.int32, (8, BLOCK), 1)
    parts = [own]
    for j in range(1, 4):
        parts.append(jnp.where(lane < j, pltpu.roll(before, j, 1), pltpu.roll(own, j, 1)))
    before = jnp.broadcast_to(before[:, BLOCK - 1 :], (8, BLOCK))
    last = jnp.broadcast_to(own[:, BLOCK - 1 :], (8, BLOCK))
    parts += [before, last]
    parts.append(jnp.zeros((BLOCK - 8 * len(parts), BLOCK), F32))
    columns = jnp.transpose(jnp.concatenate(parts, axis=0))
    columns_out[...] = columns
    own_rows[...] = own

    logits = dot(rank_part, w_up[...].astype(F32), precision=HIGHEST) + bias[...]
    log_decay = (jnp.minimum(logits, 0.0) - jnp.log(1.0 + jnp.exp(-jnp.abs(logits)))) / 16.0
    row_iota = lax.broadcasted_iota(jnp.int32, (BLOCK, BLOCK), 0)
    col_iota = lax.broadcasted_iota(jnp.int32, (BLOCK, BLOCK), 1)
    lower = jnp.where(row_iota >= col_iota, 1.0, 0.0).astype(F32)
    cum = dot(lower, log_decay, precision=HIGHEST)
    cumulated[...] = cum

    keys = conv(dot(rows, w_key[...]), taps_k, extended_k, columns)
    values = conv(dot(rows, w_value[...]), taps_v, extended_v, columns).astype(BF16)
    keys_out[...] = keys
    values_out[...] = values
    final = cum[BLOCK - 1 :, :]
    pushed = jnp.where(columns[:, 0:1] == columns[:, 40:41], keys * jnp.exp(final - cum), 0.0)
    state = dot(values, pushed.astype(BF16), FIRST)
    keep = jnp.where(before[0:1, 0:1] == last[0:1, 0:1], jnp.exp(final), 0.0)
    for h in range(2):
        lanes = slice(h * LANES, (h + 1) * LANES)
        keep_rows = pair_rows(keep[:, lanes])
        for j in range(BLOCKS // 2):
            piece = state[j * PIECE : (j + 1) * PIECE, lanes]
            pieces[h * BLOCKS // 2 + j, 0:PIECE, :] = piece.astype(BF16)
            pieces[h * BLOCKS // 2 + j, PIECE:, :] = keep_rows


def block_attention(
    normed,
    w_query,
    w_gate,
    taps_q,
    head_gain,
    keys_in,
    values,
    cumulated,
    columns,
    own_rows,
    intra,
    reach,
    gate,
    extended,
):
    rows = normed[...]
    gate[...] = silu(dot(rows, w_gate[...])[0:BLOCK, :]) * head_gain[...]
    queries = conv(dot(rows, w_query[...]), taps_q, extended, columns) * HEAD_K ** (-0.5)
    keys, cum, seg = keys_in[...], cumulated[...], columns[:, 0:1]
    row_iota = lax.broadcasted_iota(jnp.int32, (BLOCK, BLOCK), 0)
    col_iota = lax.broadcasted_iota(jnp.int32, (BLOCK, BLOCK), 1)
    reach[...] = jnp.where(seg == columns[:, 32:33], queries * jnp.exp(cum), 0.0)
    weights = jnp.zeros((BLOCK, BLOCK), F32)
    for half in (8, 16, 32, 64):
        anchors = [
            jnp.broadcast_to(cum[b + half - 1 : b + half, :], (2 * half, HEAD_K))
            for b in range(0, BLOCK, 2 * half)
        ]
        anchor = jnp.concatenate(anchors, axis=0) if len(anchors) > 1 else anchors[0]
        factor = jnp.exp(-jnp.abs(cum - anchor))
        part = dot((queries * factor).astype(BF16), (keys * factor).astype(BF16), LAST)
        inside = (
            (row_iota // (2 * half) == col_iota // (2 * half))
            & (row_iota % (2 * half) >= half)
            & (col_iota % (2 * half) < half)
        )
        weights = jnp.where(inside, part, weights)
    groups = (BLOCK // 8, 8, HEAD_K)
    cum_g, keys_g = cum.reshape(groups), keys.reshape(groups)
    queries_g = queries.reshape(groups)
    for by in range(8):
        if by:
            spread = jnp.minimum(cum_g - pltpu.roll(cum_g, by, 1), 0.0)
            product = queries_g * pltpu.roll(keys_g, by, 1) * jnp.exp(spread)
        else:
            product = queries_g * keys_g
        sums = jnp.sum(product.reshape(BLOCK, HEAD_K), axis=1, keepdims=True)
        inside = (row_iota - col_iota == by) & (row_iota % 8 >= by)
        weights = jnp.where(inside, sums, weights)
    visible = (seg == own_rows[0:1, :]) & (row_iota >= col_iota)
    weights = jnp.where(visible, weights, 0.0)
    intra[...] = dot(weights.astype(BF16), values[...])


def scan_blocks(pieces, reach, states):
    del reach
    state = jnp.zeros((PIECE, LANES), F32)
    for block in range(BLOCKS):
        at = (block % ROWS_Y) * ROWS_X + block // ROWS_Y
        states[at] = state.astype(BF16)
        pair = pieces[at, PIECE:, :].astype(F32)
        state = state * (pair[0:1, :] + pair[1:2, :]) + pieces[at, 0:PIECE, :].astype(F32)


def attend(index, intra, reach, incoming, gate, w_out, kept, kept_squares, sent):
    high, low = halves(reach[...])
    state = jnp.concatenate([incoming[0], incoming[1]], axis=1)
    attended = intra[...] + dot(high, state, LAST) + dot(low, state, LAST)
    squares = dot(jnp.ones((8, CHUNK), F32), attended * attended, LAST, precision=HIGHEST)
    terms = dot((attended * gate[...]).astype(BF16), w_out[...])
    first = index[0] == 0
    for j in range(8):
        even = terms[:, (2 * j) * CHUNK : (2 * j + 1) * CHUNK]
        odd = terms[:, (2 * j + 1) * CHUNK : (2 * j + 2) * CHUNK]
        kept[j] = jnp.where(first, even, odd)
        sent[j * BLOCK : (j + 1) * BLOCK, :] = jnp.where(first, odd, even).astype(BF16)
    kept_squares[...] = squares
    sent[8 * BLOCK :, :] = pair_rows(squares[0:1, :])


def pair_sum(index, kept, kept_squares, both, sent):
    received = both.at[1 - index[0]]
    other = received[8 * BLOCK :, :].astype(F32)
    squares = pair_rows(kept_squares[0:1, :] + other[0:1, :] + other[1:2, :])
    for j in range(8):
        terms = kept[j] + received[j * BLOCK : (j + 1) * BLOCK, :].astype(F32)
        sent[j, 0:BLOCK, :] = terms.astype(BF16)
        sent[j, BLOCK:, :] = squares


def finish(received, hidden, mixed):
    parts = []
    for r in range(4):
        pair = received[2 * r, BLOCK:, :].astype(F32) + received[2 * r + 1, BLOCK:, :].astype(F32)
        squares = pair[0:1, :] + pair[1:2, :]
        scale = lax.rsqrt(squares / HEAD_V + 1e-05)
        parts.append(jnp.broadcast_to(scale, (8, BLOCK)))
    parts.append(jnp.zeros((BLOCK - 8 * len(parts), BLOCK), F32))
    columns = jnp.transpose(jnp.concatenate(parts, axis=0))
    total = hidden[...].astype(F32)
    for r in range(4):
        terms = received[2 * r, 0:BLOCK, :].astype(F32)
        terms = terms + received[2 * r + 1, 0:BLOCK, :].astype(F32)
        total = total + columns[:, 8 * r : 8 * r + 1] * terms
    mixed[...] = total.astype(BF16)


def shards(
    hidden_in,
    seg_ids,
    norm_gain,
    w_query,
    w_key,
    w_value,
    w_gate,
    w_decay_down,
    w_decay_up,
    decay_bias,
    conv_query,
    conv_key,
    conv_value,
    head_gain,
    w_out,
):
    block = lax.axis_index("x") * ROWS_Y + lax.axis_index("y")
    block_at = jnp.reshape(block, (1,)).astype(jnp.int32)
    core_at = jnp.reshape(lax.axis_index("core"), (1,)).astype(jnp.int32)

    onward = [(i, i + 1) for i in range(BLOCKS - 1)]
    neighbour = lax.ppermute(hidden_in, SEQ, onward)
    needed = (
        w_key,
        norm_gain.reshape(1, WIDTH),
        w_decay_down.T,
        w_decay_up,
        decay_bias.reshape(1, HEAD_K),
        seg_ids.reshape(BLOCKS, BLOCK),
        conv_key,
        conv_value,
        hidden_in,
    )
    key_here, gain, down, up, bias, segs, taps_k, taps_v, hidden = local_call(
        fetch,
        [(a.shape, a.dtype) for a in needed],
        block_at,
        core_at,
        *needed,
        scratch=[pltpu.SemaphoreType.DMA((len(needed),))],
        scalars=2,
        anywhere=range(2, 2 + len(needed)),
    )
    (copies,) = local_call(
        spread_out, [((8, BLOCK + 8, CHUNK), BF16)], hidden, neighbour, key_here
    )
    of_core = lax.all_to_all(copies, CHIPS, 0, 0)
    whole = lax.all_gather(of_core, "core", axis=0)
    pieces, normed, keys, values, cumulated, columns, own_rows = local_call(
        block_state,
        [
            ((BLOCKS, PIECE + 8, LANES), BF16),
            ((BLOCK + 8, WIDTH), BF16),
            ((BLOCK, HEAD_K), F32),
            ((BLOCK, CHUNK), BF16),
            ((BLOCK, HEAD_K), F32),
            ((BLOCK, BLOCK), F32),
            ((8, BLOCK), F32),
        ],
        block_at,
        whole,
        gain,
        key_here,
        w_value,
        down,
        up,
        bias,
        segs,
        taps_k,
        taps_v,
        scratch=[pltpu.VMEM((BLOCK + 8, HEAD_K), F32), pltpu.VMEM((BLOCK + 8, CHUNK), F32)],
        scalars=1,
    )
    owned = lax.all_to_all(pieces, GRID, 0, 0)
    intra, reach, gate = local_call(
        block_attention,
        [((BLOCK, CHUNK), F32), ((BLOCK, HEAD_K), F32), ((BLOCK, CHUNK), F32)],
        normed,
        w_query,
        w_gate,
        conv_query,
        head_gain.reshape(1, CHUNK),
        keys,
        values,
        cumulated,
        columns,
        own_rows,
        scratch=[pltpu.VMEM((BLOCK + 8, HEAD_K), F32)],
    )
    (states,) = local_call(
        scan_blocks, [((BLOCKS, PIECE, LANES), BF16)], owned, reach
    )
    incoming = lax.all_to_all(states, GRID, 0, 0).reshape(2, CHUNK, LANES)
    mine, my_squares, sent = local_call(
        attend,
        [((8, BLOCK, CHUNK), F32), ((8, BLOCK), F32), ((8 * BLOCK + 8, CHUNK), BF16)],
        core_at,
        intra,
        reach,
        incoming,
        gate,
        w_out,
        scalars=1,
    )
    both = lax.all_gather(sent, "core", axis=0)
    (pairs,) = local_call(
        pair_sum, [((8, BLOCK + 8, CHUNK), BF16)], core_at, mine, my_squares, both, scalars=1
    )
    arrived = lax.all_to_all(pairs, CHIPS, 0, 0)
    (mixed,) = local_call(
        finish, [((BLOCK, CHUNK), BF16)], arrived, hidden, last=True
    )
    return mixed


def solution(mesh):
    finer = Mesh(mesh.devices.reshape(ROWS_X, ROWS_Y, 4, 2, 2), ("x", "y", "row", "zhi", "core"))
    part = ("row", "zhi", "core")
    return jax.shard_map(
        shards,
        mesh=finer,
        in_specs=(
            P(SEQ, part),
            P(),
            P(),
            P(None, "row"),
            P(None, "row"),
            P(None, part),
            P(None, part),
            P(),
            P(None, "row"),
            P("row"),
            P(None, "row"),
            P(None, "row"),
            P(None, part),
            P(("zhi", "core")),
            P(part, None),
        ),
        out_specs=P(SEQ, part),
        check_vma=False,
    )
```

```python
import jax
import jax.numpy as jnp
from jax import lax
from jax.experimental import pallas as pl
from jax.experimental.pallas import tpu as pltpu
from jax.sharding import Mesh, PartitionSpec as P

F32 = jnp.float32
BF16 = jnp.bfloat16
HIGHEST = lax.Precision.HIGHEST
HEAD_V = 512
WIDTH = 2048
BLOCK = 128
HEAD_K = 256
CHUNK = 128
LAST = (((1,), (1,)), ((), ()))
FIRST = (((0,), (0,)), ((), ()))

SEQ = ("x", "y")
GRID = ("y", "x")
CHIPS = ("row", "zhi")
ROWS_X, ROWS_Y = 4, 8
LANES = 128
BLOCKS = ROWS_X * ROWS_Y
PIECE = 2 * CHUNK // BLOCKS


def local_call(kernel, outs, *args, scratch=(), scalars=0, plain=(), anywhere=(), last=False):
    elsewhere = (*range(scalars), *plain, *anywhere)
    vmem = pl.BlockSpec(memory_space=pltpu.VMEM)
    smem = pl.BlockSpec(memory_space=pltpu.SMEM)
    args = [
        pltpu.with_memory_space_constraint(a, pltpu.HBM if i in anywhere else pltpu.VMEM)
        if i in anywhere or i not in elsewhere
        else a
        for i, a in enumerate(args)
    ]
    return pl.pallas_call(
        kernel,
        out_shape=[jax.ShapeDtypeStruct(s, t) if last else pltpu.VMEM(s, t) for s, t in outs],
        in_specs=[
            smem if i < scalars else pl.BlockSpec(memory_space=pltpu.HBM) if i in anywhere else vmem
            for i in range(len(args))
        ],
        out_specs=[vmem] * len(outs),
        scratch_shapes=list(scratch),
        name=kernel.__name__,
        compiler_params=pltpu.CompilerParams(vmem_limit_bytes=16 << 20),
    )(*args)


def dot(a, b, dims=(((1,), (0,)), ((), ())), precision=None):
    return lax.dot_general(a, b, dims, precision=precision, preferred_element_type=F32)


def halves(value):
    high = value.astype(BF16)
    return high, (value - high.astype(F32)).astype(BF16)


def pair_rows(value):
    high, low = halves(value)
    shape = (8, value.shape[1])
    index = lax.broadcasted_iota(jnp.int32, shape, 0)
    both = jnp.where(
        index == 0,
        jnp.broadcast_to(high.astype(F32), shape),
        jnp.where(index == 1, jnp.broadcast_to(low.astype(F32), shape), 0.0),
    )
    return both.astype(BF16)


def silu(value):
    return value * jax.nn.sigmoid(value)


def fetch_and_spread(index, core, *refs):
    del index, core
    *refs, copies, arrived = refs
    count = len(refs) // 2
    fetches = [
        pltpu.make_async_copy(refs[i], refs[count + i], arrived.at[i]) for i in range(count)
    ]
    for fetch in fetches:
        fetch.start()
    fetches[0].wait()
    for j in range(8):
        copies[j] = refs[count][...]
    for fetch in fetches[1:]:
        fetch.wait()


def conv(pre, edge, taps, extended, columns):
    extended[0:8, :] = jnp.zeros((8, pre.shape[1]), F32) if edge is None else edge
    extended[8:, :] = pre
    seg = columns[:, 0:1]
    total = taps[0:1, :] * pre
    for j in range(1, 4):
        same = columns[:, 8 * j : 8 * j + 1] == seg
        total = total + jnp.where(
            same, taps[j : j + 1, :] * extended[8 - j : 8 - j + BLOCK, :], 0.0
        )
    return total


def onward(pre, taps, own, following):
    sums = []
    for t in range(3):
        total = jnp.zeros((1, pre.shape[1]), F32)
        for j in range(t + 1, 4):
            at = BLOCK + t - j
            same = following[0:1, t : t + 1] == own[0:1, at : at + 1]
            total = total + jnp.where(same, taps[j : j + 1, :] * pre[at : at + 1, :], 0.0)
        sums.append(total)
    return sums


def stacked_rows(rows):
    shape = (8, LANES)
    index = lax.broadcasted_iota(jnp.int32, shape, 0)
    out = jnp.zeros(shape, F32)
    for at, row in rows.items():
        out = jnp.where(index == at, jnp.broadcast_to(row, shape), out)
    return out.astype(BF16)


def block_state(
    index,
    whole,
    gain,
    w_key,
    w_value,
    w_down,
    w_up,
    bias,
    seg_ids,
    taps_k,
    taps_v,
    pieces,
    normed,
    pre_k,
    pre_v,
    cumulated,
    columns_out,
    own_rows,
    extended_k,
    extended_v,
):
    chunks = WIDTH // CHUNK
    squares = jnp.zeros((BLOCK, CHUNK), F32)
    for f in range(chunks):
        activ = whole[f % 2, f // 2].astype(F32)
        squares = squares + activ * activ
    scale = lax.rsqrt(jnp.sum(squares, axis=1, keepdims=True) / WIDTH + 1e-06)
    for f in range(chunks):
        lanes = slice(f * CHUNK, (f + 1) * CHUNK)
        activ = whole[f % 2, f // 2].astype(F32)
        normed[:, lanes] = (activ * scale * gain[:, lanes]).astype(BF16)
    rows = normed[...]
    rank_part = dot(rows, w_down[...], LAST)

    at = index[0]
    own = seg_ids[pl.ds(at, 1), :].astype(F32)
    before = seg_ids[pl.ds(jnp.maximum(at - 1, 0), 1), :].astype(F32)
    before = jnp.where(at > 0, before, -1.0)
    following = seg_ids[pl.ds(jnp.minimum(at + 1, BLOCKS - 1), 1), :].astype(F32)
    own = jnp.broadcast_to(own, (8, BLOCK))
    before = jnp.broadcast_to(before, (8, BLOCK))
    lane = lax.broadcasted_iota(jnp.int32, (8, BLOCK), 1)
    parts = [own]
    for j in range(1, 4):
        parts.append(jnp.where(lane < j, pltpu.roll(before, j, 1), pltpu.roll(own, j, 1)))
    before = jnp.broadcast_to(before[:, BLOCK - 1 :], (8, BLOCK))
    last = jnp.broadcast_to(own[:, BLOCK - 1 :], (8, BLOCK))
    parts += [before, last]
    parts.append(jnp.zeros((BLOCK - 8 * len(parts), BLOCK), F32))
    columns = jnp.transpose(jnp.concatenate(parts, axis=0))
    columns_out[...] = columns
    own_rows[...] = own

    logits = dot(rank_part, w_up[...].astype(F32), precision=HIGHEST) + bias[...]
    log_decay = (jnp.minimum(logits, 0.0) - jnp.log(1.0 + jnp.exp(-jnp.abs(logits)))) / 16.0
    row_iota = lax.broadcasted_iota(jnp.int32, (BLOCK, BLOCK), 0)
    col_iota = lax.broadcasted_iota(jnp.int32, (BLOCK, BLOCK), 1)
    lower = jnp.where(row_iota >= col_iota, 1.0, 0.0).astype(F32)
    cum = dot(lower, log_decay, precision=HIGHEST)
    cumulated[...] = cum

    of_keys = dot(rows, w_key[...])
    of_values = dot(rows, w_value[...])
    pre_k[...] = of_keys
    pre_v[...] = of_values
    sums_k = conv(of_keys, None, taps_k, extended_k, columns)
    sums_v = conv(of_values, None, taps_v, extended_v, columns)
    next_k = onward(of_keys, taps_k, own, following)
    next_v = onward(of_values, taps_v, own, following)
    final = cum[BLOCK - 1 :, :]
    factors = jnp.where(columns[:, 0:1] == columns[:, 40:41], jnp.exp(final - cum), 0.0)
    later = lax.broadcasted_iota(jnp.int32, (BLOCK, HEAD_K), 0) >= 3
    pushed = jnp.where(later, silu(sums_k) * factors, 0.0)
    state = dot(silu(sums_v).astype(BF16), pushed.astype(BF16), FIRST)
    keep = jnp.where(before[0:1, 0:1] == last[0:1, 0:1], jnp.exp(final), 0.0)
    high, low = halves(keep)
    lane = lax.broadcasted_iota(jnp.int32, (1, LANES), 1)
    mixed_v = []
    for upper in range(2):
        mine = (lane >= LANES // 2) == (upper == 1)
        mixed_v.append(
            [
                jnp.where(mine, sums_v[t : t + 1, :], pltpu.roll(next_v[t], LANES // 2, 1))
                for t in range(3)
            ]
        )
    for h in range(2):
        lanes = slice(h * LANES, (h + 1) * LANES)
        rows_b = {0: high.astype(F32)[:, lanes], 1: low.astype(F32)[:, lanes]}
        for t in range(3):
            rows_b[2 + t] = sums_k[t : t + 1, lanes]
            rows_b[5 + t] = next_k[t][:, lanes]
        tile_b = stacked_rows(rows_b)
        for upper in range(2):
            rows_c = {2 + t: factors[t : t + 1, lanes] for t in range(3)}
            rows_c.update({5 + t: mixed_v[upper][t] for t in range(3)})
            tile_c = stacked_rows(rows_c)
            for j in range(8):
                g = 8 * upper + j
                p = h * BLOCKS // 2 + g
                pieces[p, 0:PIECE, :] = state[g * PIECE : (g + 1) * PIECE, lanes].astype(BF16)
                pieces[p, PIECE : PIECE + 8, :] = tile_b
                pieces[p, PIECE + 8 :, :] = tile_c


def queries_gate(normed, w_query, w_gate, head_gain, pre_k, pre_v, pre_q, gate, tail):
    rows = normed[...]
    gate[...] = silu(dot(rows, w_gate[...])) * head_gain[...]
    of_queries = dot(rows, w_query[...])
    pre_q[...] = of_queries
    tail[:, :HEAD_K] = of_queries[BLOCK - 8 :, :]
    tail[:, HEAD_K : 2 * HEAD_K] = pre_k[BLOCK - 8 :, :]
    tail[:, 2 * HEAD_K :] = pre_v[BLOCK - 8 :, :]


def block_attention(
    pre_q,
    pre_k,
    pre_v,
    edge,
    taps_q,
    taps_k,
    taps_v,
    cumulated,
    columns,
    own_rows,
    intra,
    reach,
    extended,
    extended_v,
):
    edges = edge[...]
    queries = silu(conv(pre_q[...], edges[:, :HEAD_K], taps_q, extended.at[0], columns))
    queries = queries * HEAD_K ** (-0.5)
    keys = silu(
        conv(pre_k[...], edges[:, HEAD_K : 2 * HEAD_K], taps_k, extended.at[1], columns)
    )
    values = silu(conv(pre_v[...], edges[:, 2 * HEAD_K :], taps_v, extended_v, columns))
    cum, seg = cumulated[...], columns[:, 0:1]
    row_iota = lax.broadcasted_iota(jnp.int32, (BLOCK, BLOCK), 0)
    col_iota = lax.broadcasted_iota(jnp.int32, (BLOCK, BLOCK), 1)
    reach[...] = jnp.where(seg == columns[:, 32:33], queries * jnp.exp(cum), 0.0)
    weights = jnp.zeros((BLOCK, BLOCK), F32)
    for half in (8, 16, 32, 64):
        anchors = [
            jnp.broadcast_to(cum[b + half - 1 : b + half, :], (2 * half, HEAD_K))
            for b in range(0, BLOCK, 2 * half)
        ]
        anchor = jnp.concatenate(anchors, axis=0) if len(anchors) > 1 else anchors[0]
        factor = jnp.exp(-jnp.abs(cum - anchor))
        part = dot((queries * factor).astype(BF16), (keys * factor).astype(BF16), LAST)
        inside = (
            (row_iota // (2 * half) == col_iota // (2 * half))
            & (row_iota % (2 * half) >= half)
            & (col_iota % (2 * half) < half)
        )
        weights = jnp.where(inside, part, weights)
    groups = (BLOCK // 8, 8, HEAD_K)
    cum_g, keys_g = cum.reshape(groups), keys.reshape(groups)
    queries_g = queries.reshape(groups)
    for by in range(8):
        if by:
            spread = jnp.minimum(cum_g - pltpu.roll(cum_g, by, 1), 0.0)
            product = queries_g * pltpu.roll(keys_g, by, 1) * jnp.exp(spread)
        else:
            product = queries_g * keys_g
        sums = jnp.sum(product.reshape(BLOCK, HEAD_K), axis=1, keepdims=True)
        inside = (row_iota - col_iota == by) & (row_iota % 8 >= by)
        weights = jnp.where(inside, sums, weights)
    visible = (seg == own_rows[0:1, :]) & (row_iota >= col_iota)
    weights = jnp.where(visible, weights, 0.0)
    intra[...] = dot(weights.astype(BF16), values.astype(BF16))


def scan_blocks(index, pieces, reach, states):
    del reach
    owner = (index[0] % ROWS_Y) * ROWS_X + index[0] // ROWS_Y
    first = (owner % (BLOCKS // 2)) * PIECE
    shape = (PIECE, LANES)
    lane = lax.broadcasted_iota(jnp.int32, shape, 1)
    chosen = lane == lax.broadcasted_iota(jnp.int32, shape, 0) + first
    state = jnp.zeros(shape, F32)
    back_b = back_c = jnp.zeros((8, LANES), F32)
    for block in range(BLOCKS):
        at = (block % ROWS_Y) * ROWS_X + block // ROWS_Y
        states[at] = state.astype(BF16)
        tile_b = pieces[at, PIECE : PIECE + 8, :].astype(F32)
        tile_c = pieces[at, PIECE + 8 :, :].astype(F32)
        pushed = silu(tile_b + pltpu.roll(back_b, 5, 0)) * tile_c
        values = silu(tile_c + pltpu.roll(back_c, LANES // 2, 1))
        added = pieces[at, 0:PIECE, :].astype(F32)
        for t in range(3):
            row = jnp.broadcast_to(values[5 + t : 6 + t, :], shape)
            column = jnp.sum(jnp.where(chosen, row, 0.0), axis=1, keepdims=True)
            added = added + column * pushed[2 + t : 3 + t, :]
        state = state * (tile_b[0:1, :] + tile_b[1:2, :]) + added
        back_b, back_c = tile_b, tile_c


def attend(index, intra, reach, incoming, gate, w_out, kept, kept_squares, sent):
    high, low = halves(reach[...])
    state = jnp.concatenate([incoming[0], incoming[1]], axis=1)
    attended = intra[...] + dot(high, state, LAST) + dot(low, state, LAST)
    squares = dot(jnp.ones((8, CHUNK), F32), attended * attended, LAST, precision=HIGHEST)
    terms = dot((attended * gate[...]).astype(BF16), w_out[...])
    first = index[0] == 0
    for j in range(8):
        even = terms[:, (2 * j) * CHUNK : (2 * j + 1) * CHUNK]
        odd = terms[:, (2 * j + 1) * CHUNK : (2 * j + 2) * CHUNK]
        kept[j] = jnp.where(first, even, odd)
        sent[j * BLOCK : (j + 1) * BLOCK, :] = jnp.where(first, odd, even).astype(BF16)
    kept_squares[...] = squares
    sent[8 * BLOCK :, :] = pair_rows(squares[0:1, :])


def pair_sum(index, kept, kept_squares, both, sent):
    received = both.at[1 - index[0]]
    other = received[8 * BLOCK :, :].astype(F32)
    squares = pair_rows(kept_squares[0:1, :] + other[0:1, :] + other[1:2, :])
    for j in range(8):
        terms = kept[j] + received[j * BLOCK : (j + 1) * BLOCK, :].astype(F32)
        sent[j, 0:BLOCK, :] = terms.astype(BF16)
        sent[j, BLOCK:, :] = squares


def finish(received, hidden, mixed):
    parts = []
    for r in range(4):
        pair = received[2 * r, BLOCK:, :].astype(F32) + received[2 * r + 1, BLOCK:, :].astype(F32)
        squares = pair[0:1, :] + pair[1:2, :]
        scale = lax.rsqrt(squares / HEAD_V + 1e-05)
        parts.append(jnp.broadcast_to(scale, (8, BLOCK)))
    parts.append(jnp.zeros((BLOCK - 8 * len(parts), BLOCK), F32))
    columns = jnp.transpose(jnp.concatenate(parts, axis=0))
    total = hidden[...].astype(F32)
    for r in range(4):
        terms = received[2 * r, 0:BLOCK, :].astype(F32)
        terms = terms + received[2 * r + 1, 0:BLOCK, :].astype(F32)
        total = total + columns[:, 8 * r : 8 * r + 1] * terms
    mixed[...] = total.astype(BF16)


def shards(
    hidden_in,
    seg_ids,
    norm_gain,
    w_query,
    w_key,
    w_value,
    w_gate,
    w_decay_down,
    w_decay_up,
    decay_bias,
    conv_query,
    conv_key,
    conv_value,
    head_gain,
    w_out,
):
    block = lax.axis_index("x") * ROWS_Y + lax.axis_index("y")
    block_at = jnp.reshape(block, (1,)).astype(jnp.int32)
    core_at = jnp.reshape(lax.axis_index("core"), (1,)).astype(jnp.int32)

    needed = (
        hidden_in,
        norm_gain.reshape(1, WIDTH),
        w_decay_down.T,
        w_decay_up,
        decay_bias.reshape(1, HEAD_K),
        seg_ids.reshape(BLOCKS, BLOCK),
        conv_query,
        conv_key,
        conv_value,
        head_gain.reshape(1, CHUNK),
    )
    hidden, gain, down, up, bias, segs, taps_q, taps_k, taps_v, out_gain, copies = local_call(
        fetch_and_spread,
        [*((a.shape, a.dtype) for a in needed), ((8, BLOCK, CHUNK), BF16)],
        block_at,
        core_at,
        *needed,
        scratch=[pltpu.SemaphoreType.DMA((len(needed),))],
        scalars=2,
        anywhere=range(2, 2 + len(needed)),
    )
    of_core = lax.all_to_all(copies, CHIPS, 0, 0)
    whole = lax.all_gather(of_core, "core", axis=0)
    pieces, normed, pre_k, pre_v, cumulated, columns, own_rows = local_call(
        block_state,
        [
            ((BLOCKS, PIECE + 16, LANES), BF16),
            ((BLOCK, WIDTH), BF16),
            ((BLOCK, HEAD_K), F32),
            ((BLOCK, CHUNK), F32),
            ((BLOCK, HEAD_K), F32),
            ((BLOCK, BLOCK), F32),
            ((8, BLOCK), F32),
        ],
        block_at,
        whole,
        gain,
        w_key,
        w_value,
        down,
        up,
        bias,
        segs,
        taps_k,
        taps_v,
        scratch=[pltpu.VMEM((BLOCK + 8, HEAD_K), F32), pltpu.VMEM((BLOCK + 8, CHUNK), F32)],
        scalars=1,
    )
    owned = lax.all_to_all(pieces, GRID, 0, 0)
    pre_q, gate, tail = local_call(
        queries_gate,
        [((BLOCK, HEAD_K), F32), ((BLOCK, CHUNK), F32), ((8, 2 * HEAD_K + CHUNK), F32)],
        normed,
        w_query,
        w_gate,
        out_gain,
        pre_k,
        pre_v,
    )
    edge = lax.ppermute(tail, SEQ, [(i, i + 1) for i in range(BLOCKS - 1)])
    intra, reach = local_call(
        block_attention,
        [((BLOCK, CHUNK), F32), ((BLOCK, HEAD_K), F32)],
        pre_q,
        pre_k,
        pre_v,
        edge,
        taps_q,
        taps_k,
        taps_v,
        cumulated,
        columns,
        own_rows,
        scratch=[
            pltpu.VMEM((2, BLOCK + 8, HEAD_K), F32),
            pltpu.VMEM((BLOCK + 8, CHUNK), F32),
        ],
    )
    (states,) = local_call(
        scan_blocks,
        [((BLOCKS, PIECE, LANES), BF16)],
        block_at,
        owned,
        reach,
        scalars=1,
    )
    incoming = lax.all_to_all(states, GRID, 0, 0).reshape(2, CHUNK, LANES)
    mine, my_squares, sent = local_call(
        attend,
        [((8, BLOCK, CHUNK), F32), ((8, BLOCK), F32), ((8 * BLOCK + 8, CHUNK), BF16)],
        core_at,
        intra,
        reach,
        incoming,
        gate,
        w_out,
        scalars=1,
    )
    both = lax.all_gather(sent, "core", axis=0)
    (pairs,) = local_call(
        pair_sum, [((8, BLOCK + 8, CHUNK), BF16)], core_at, mine, my_squares, both, scalars=1
    )
    arrived = lax.all_to_all(pairs, CHIPS, 0, 0)
    (mixed,) = local_call(
        finish, [((BLOCK, CHUNK), BF16)], arrived, hidden, last=True
    )
    return mixed


def solution(mesh):
    finer = Mesh(mesh.devices.reshape(ROWS_X, ROWS_Y, 4, 2, 2), ("x", "y", "row", "zhi", "core"))
    part = ("row", "zhi", "core")
    return jax.shard_map(
        shards,
        mesh=finer,
        in_specs=(
            P(SEQ, part),
            P(),
            P(),
            P(None, "row"),
            P(None, "row"),
            P(None, part),
            P(None, part),
            P(),
            P(None, "row"),
            P("row"),
            P(None, "row"),
            P(None, "row"),
            P(None, part),
            P(("zhi", "core")),
            P(part, None),
        ),
        out_specs=P(SEQ, part),
        check_vma=False,
    )
```

```python
import jax
import jax.numpy as jnp
from jax import lax
from jax.experimental import pallas as pl
from jax.experimental.pallas import tpu as pltpu
from jax.sharding import Mesh, PartitionSpec as P

F32 = jnp.float32
BF16 = jnp.bfloat16
HIGHEST = lax.Precision.HIGHEST
HEAD_V = 512
WIDTH = 2048
BLOCK = 128
HEAD_K = 256
CHUNK = 128
LAST = (((1,), (1,)), ((), ()))
FIRST = (((0,), (0,)), ((), ()))

SEQ = ("x", "y")
GRID = ("y", "x")
CHIPS = ("row", "zhi")
ROWS_X, ROWS_Y = 4, 8
LANES = 128
BLOCKS = ROWS_X * ROWS_Y
PIECE = 2 * CHUNK // BLOCKS


def local_call(kernel, outs, *args, scratch=(), scalars=0, plain=(), anywhere=(), last=False):
    elsewhere = (*range(scalars), *plain, *anywhere)
    vmem = pl.BlockSpec(memory_space=pltpu.VMEM)
    smem = pl.BlockSpec(memory_space=pltpu.SMEM)
    args = [
        pltpu.with_memory_space_constraint(a, pltpu.HBM if i in anywhere else pltpu.VMEM)
        if i in anywhere or i not in elsewhere
        else a
        for i, a in enumerate(args)
    ]
    return pl.pallas_call(
        kernel,
        out_shape=[jax.ShapeDtypeStruct(s, t) if last else pltpu.VMEM(s, t) for s, t in outs],
        in_specs=[
            smem if i < scalars else pl.BlockSpec(memory_space=pltpu.HBM) if i in anywhere else vmem
            for i in range(len(args))
        ],
        out_specs=[vmem] * len(outs),
        scratch_shapes=list(scratch),
        name=kernel.__name__,
        compiler_params=pltpu.CompilerParams(vmem_limit_bytes=16 << 20),
    )(*args)


def dot(a, b, dims=(((1,), (0,)), ((), ())), precision=None):
    return lax.dot_general(a, b, dims, precision=precision, preferred_element_type=F32)


def halves(value):
    high = value.astype(BF16)
    return high, (value - high.astype(F32)).astype(BF16)


def pair_rows(value):
    high, low = halves(value)
    shape = (8, value.shape[1])
    index = lax.broadcasted_iota(jnp.int32, shape, 0)
    both = jnp.where(
        index == 0,
        jnp.broadcast_to(high.astype(F32), shape),
        jnp.where(index == 1, jnp.broadcast_to(low.astype(F32), shape), 0.0),
    )
    return both.astype(BF16)


def silu(value):
    return value * jax.nn.sigmoid(value)


def fetch_and_spread(index, core, *refs):
    del index, core
    *refs, copies, arrived = refs
    count = len(refs) // 2
    fetches = [
        pltpu.make_async_copy(refs[i], refs[count + i], arrived.at[i]) for i in range(count)
    ]
    for fetch in fetches:
        fetch.start()
    fetches[0].wait()
    for j in range(8):
        copies[j] = refs[count][...]
    for fetch in fetches[1:]:
        fetch.wait()


def conv(pre, edge, taps, extended, columns):
    extended[0:8, :] = jnp.zeros((8, pre.shape[1]), F32) if edge is None else edge
    extended[8:, :] = pre
    seg = columns[:, 0:1]
    total = taps[0:1, :] * pre
    for j in range(1, 4):
        same = columns[:, 8 * j : 8 * j + 1] == seg
        total = total + jnp.where(
            same, taps[j : j + 1, :] * extended[8 - j : 8 - j + BLOCK, :], 0.0
        )
    return total


def onward(pre, taps, own, following):
    sums = []
    for t in range(3):
        total = jnp.zeros((1, pre.shape[1]), F32)
        for j in range(t + 1, 4):
            at = BLOCK + t - j
            same = following[0:1, t : t + 1] == own[0:1, at : at + 1]
            total = total + jnp.where(same, taps[j : j + 1, :] * pre[at : at + 1, :], 0.0)
        sums.append(total)
    return sums


def stacked_rows(rows):
    shape = (8, LANES)
    index = lax.broadcasted_iota(jnp.int32, shape, 0)
    out = jnp.zeros(shape, F32)
    for at, row in rows.items():
        out = jnp.where(index == at, jnp.broadcast_to(row, shape), out)
    return out.astype(BF16)


def block_state(
    index,
    whole,
    gain,
    query_hbm,
    w_key,
    w_value,
    w_down,
    w_up,
    bias,
    seg_ids,
    taps_k,
    taps_v,
    pieces,
    tail,
    normed,
    pre_q,
    pre_k,
    pre_v,
    cumulated,
    columns_out,
    own_rows,
    extended_k,
    extended_v,
    w_query,
    arrived,
):
    fetch = pltpu.make_async_copy(query_hbm, w_query, arrived.at[0])
    fetch.start()
    chunks = WIDTH // CHUNK
    squares = jnp.zeros((BLOCK, CHUNK), F32)
    for f in range(chunks):
        activ = whole[f % 2, f // 2].astype(F32)
        squares = squares + activ * activ
    scale = lax.rsqrt(jnp.sum(squares, axis=1, keepdims=True) / WIDTH + 1e-06)
    for f in range(chunks):
        lanes = slice(f * CHUNK, (f + 1) * CHUNK)
        activ = whole[f % 2, f // 2].astype(F32)
        normed[:, lanes] = (activ * scale * gain[:, lanes]).astype(BF16)
    rows = normed[...]
    rank_part = dot(rows, w_down[...], LAST)

    at = index[0]
    own = seg_ids[pl.ds(at, 1), :].astype(F32)
    before = seg_ids[pl.ds(jnp.maximum(at - 1, 0), 1), :].astype(F32)
    before = jnp.where(at > 0, before, -1.0)
    following = seg_ids[pl.ds(jnp.minimum(at + 1, BLOCKS - 1), 1), :].astype(F32)
    own = jnp.broadcast_to(own, (8, BLOCK))
    before = jnp.broadcast_to(before, (8, BLOCK))
    lane = lax.broadcasted_iota(jnp.int32, (8, BLOCK), 1)
    parts = [own]
    for j in range(1, 4):
        parts.append(jnp.where(lane < j, pltpu.roll(before, j, 1), pltpu.roll(own, j, 1)))
    before = jnp.broadcast_to(before[:, BLOCK - 1 :], (8, BLOCK))
    last = jnp.broadcast_to(own[:, BLOCK - 1 :], (8, BLOCK))
    parts += [before, last]
    parts.append(jnp.zeros((BLOCK - 8 * len(parts), BLOCK), F32))
    columns = jnp.transpose(jnp.concatenate(parts, axis=0))
    columns_out[...] = columns
    own_rows[...] = own

    logits = dot(rank_part, w_up[...].astype(F32), precision=HIGHEST) + bias[...]
    log_decay = (jnp.minimum(logits, 0.0) - jnp.log(1.0 + jnp.exp(-jnp.abs(logits)))) / 16.0
    row_iota = lax.broadcasted_iota(jnp.int32, (BLOCK, BLOCK), 0)
    col_iota = lax.broadcasted_iota(jnp.int32, (BLOCK, BLOCK), 1)
    lower = jnp.where(row_iota >= col_iota, 1.0, 0.0).astype(F32)
    cum = dot(lower, log_decay, precision=HIGHEST)
    cumulated[...] = cum

    of_keys = dot(rows, w_key[...])
    of_values = dot(rows, w_value[...])
    pre_k[...] = of_keys
    pre_v[...] = of_values
    sums_k = conv(of_keys, None, taps_k, extended_k, columns)
    sums_v = conv(of_values, None, taps_v, extended_v, columns)
    next_k = onward(of_keys, taps_k, own, following)
    next_v = onward(of_values, taps_v, own, following)
    final = cum[BLOCK - 1 :, :]
    factors = jnp.where(columns[:, 0:1] == columns[:, 40:41], jnp.exp(final - cum), 0.0)
    later = lax.broadcasted_iota(jnp.int32, (BLOCK, HEAD_K), 0) >= 3
    pushed = jnp.where(later, silu(sums_k) * factors, 0.0)
    state = dot(silu(sums_v).astype(BF16), pushed.astype(BF16), FIRST)
    keep = jnp.where(before[0:1, 0:1] == last[0:1, 0:1], jnp.exp(final), 0.0)
    high, low = halves(keep)
    lane = lax.broadcasted_iota(jnp.int32, (1, LANES), 1)
    mixed_v = []
    for upper in range(2):
        mine = (lane >= LANES // 2) == (upper == 1)
        mixed_v.append(
            [
                jnp.where(mine, sums_v[t : t + 1, :], pltpu.roll(next_v[t], LANES // 2, 1))
                for t in range(3)
            ]
        )
    for h in range(2):
        lanes = slice(h * LANES, (h + 1) * LANES)
        rows_b = {0: high.astype(F32)[:, lanes], 1: low.astype(F32)[:, lanes]}
        for t in range(3):
            rows_b[2 + t] = sums_k[t : t + 1, lanes]
            rows_b[5 + t] = next_k[t][:, lanes]
        tile_b = stacked_rows(rows_b)
        for upper in range(2):
            rows_c = {2 + t: factors[t : t + 1, lanes] for t in range(3)}
            rows_c.update({5 + t: mixed_v[upper][t] for t in range(3)})
            tile_c = stacked_rows(rows_c)
            for j in range(8):
                g = 8 * upper + j
                p = h * BLOCKS // 2 + g
                pieces[p, 0:PIECE, :] = state[g * PIECE : (g + 1) * PIECE, lanes].astype(BF16)
                pieces[p, PIECE : PIECE + 8, :] = tile_b
                pieces[p, PIECE + 8 :, :] = tile_c
    fetch.wait()
    of_queries = dot(rows, w_query[...])
    pre_q[...] = of_queries
    tail[:, :HEAD_K] = of_queries[BLOCK - 8 :, :]
    tail[:, HEAD_K : 2 * HEAD_K] = of_keys[BLOCK - 8 :, :]
    tail[:, 2 * HEAD_K :] = of_values[BLOCK - 8 :, :]


def block_attention(
    normed,
    w_gate,
    head_gain,
    pre_q,
    pre_k,
    pre_v,
    edge,
    taps_q,
    taps_k,
    taps_v,
    cumulated,
    columns,
    own_rows,
    left,
    intra,
    reach,
    gate,
    extended,
    extended_v,
):
    del left
    gate[...] = silu(dot(normed[...], w_gate[...])) * head_gain[...]
    edges = edge[...]
    queries = silu(conv(pre_q[...], edges[:, :HEAD_K], taps_q, extended.at[0], columns))
    queries = queries * HEAD_K ** (-0.5)
    keys = silu(
        conv(pre_k[...], edges[:, HEAD_K : 2 * HEAD_K], taps_k, extended.at[1], columns)
    )
    values = silu(conv(pre_v[...], edges[:, 2 * HEAD_K :], taps_v, extended_v, columns))
    cum, seg = cumulated[...], columns[:, 0:1]
    row_iota = lax.broadcasted_iota(jnp.int32, (BLOCK, BLOCK), 0)
    col_iota = lax.broadcasted_iota(jnp.int32, (BLOCK, BLOCK), 1)
    reach[...] = jnp.where(seg == columns[:, 32:33], queries * jnp.exp(cum), 0.0)
    weights = jnp.zeros((BLOCK, BLOCK), F32)
    for half in (8, 16, 32, 64):
        anchors = [
            jnp.broadcast_to(cum[b + half - 1 : b + half, :], (2 * half, HEAD_K))
            for b in range(0, BLOCK, 2 * half)
        ]
        anchor = jnp.concatenate(anchors, axis=0) if len(anchors) > 1 else anchors[0]
        factor = jnp.exp(-jnp.abs(cum - anchor))
        part = dot((queries * factor).astype(BF16), (keys * factor).astype(BF16), LAST)
        inside = (
            (row_iota // (2 * half) == col_iota // (2 * half))
            & (row_iota % (2 * half) >= half)
            & (col_iota % (2 * half) < half)
        )
        weights = jnp.where(inside, part, weights)
    groups = (BLOCK // 8, 8, HEAD_K)
    cum_g, keys_g = cum.reshape(groups), keys.reshape(groups)
    queries_g = queries.reshape(groups)
    for by in range(8):
        if by:
            spread = jnp.minimum(cum_g - pltpu.roll(cum_g, by, 1), 0.0)
            product = queries_g * pltpu.roll(keys_g, by, 1) * jnp.exp(spread)
        else:
            product = queries_g * keys_g
        sums = jnp.sum(product.reshape(BLOCK, HEAD_K), axis=1, keepdims=True)
        inside = (row_iota - col_iota == by) & (row_iota % 8 >= by)
        weights = jnp.where(inside, sums, weights)
    visible = (seg == own_rows[0:1, :]) & (row_iota >= col_iota)
    weights = jnp.where(visible, weights, 0.0)
    intra[...] = dot(weights.astype(BF16), values.astype(BF16))


def scan_blocks(index, pieces, states, left):
    owner = (index[0] % ROWS_Y) * ROWS_X + index[0] // ROWS_Y
    first = (owner % (BLOCKS // 2)) * PIECE
    shape = (PIECE, LANES)
    lane = lax.broadcasted_iota(jnp.int32, shape, 1)
    chosen = lane == lax.broadcasted_iota(jnp.int32, shape, 0) + first
    state = jnp.zeros(shape, F32)
    back_b = back_c = jnp.zeros((8, LANES), F32)
    for block in range(BLOCKS):
        at = (block % ROWS_Y) * ROWS_X + block // ROWS_Y
        states[at] = state.astype(BF16)
        tile_b = pieces[at, PIECE : PIECE + 8, :].astype(F32)
        tile_c = pieces[at, PIECE + 8 :, :].astype(F32)
        pushed = silu(tile_b + pltpu.roll(back_b, 5, 0)) * tile_c
        values = silu(tile_c + pltpu.roll(back_c, LANES // 2, 1))
        added = pieces[at, 0:PIECE, :].astype(F32)
        for t in range(3):
            row = jnp.broadcast_to(values[5 + t : 6 + t, :], shape)
            column = jnp.sum(jnp.where(chosen, row, 0.0), axis=1, keepdims=True)
            added = added + column * pushed[2 + t : 3 + t, :]
        state = state * (tile_b[0:1, :] + tile_b[1:2, :]) + added
        back_b, back_c = tile_b, tile_c
    left[...] = state


def attend(index, intra, reach, incoming, gate, w_out, kept, kept_squares, sent):
    high, low = halves(reach[...])
    state = jnp.concatenate([incoming[0], incoming[1]], axis=1)
    attended = intra[...] + dot(high, state, LAST) + dot(low, state, LAST)
    squares = dot(jnp.ones((8, CHUNK), F32), attended * attended, LAST, precision=HIGHEST)
    terms = dot((attended * gate[...]).astype(BF16), w_out[...])
    first = index[0] == 0
    for j in range(8):
        even = terms[:, (2 * j) * CHUNK : (2 * j + 1) * CHUNK]
        odd = terms[:, (2 * j + 1) * CHUNK : (2 * j + 2) * CHUNK]
        kept[j] = jnp.where(first, even, odd)
        sent[j * BLOCK : (j + 1) * BLOCK, :] = jnp.where(first, odd, even).astype(BF16)
    kept_squares[...] = squares
    sent[8 * BLOCK :, :] = pair_rows(squares[0:1, :])


def pair_sum(index, kept, kept_squares, both, sent):
    received = both.at[1 - index[0]]
    other = received[8 * BLOCK :, :].astype(F32)
    squares = pair_rows(kept_squares[0:1, :] + other[0:1, :] + other[1:2, :])
    for j in range(8):
        terms = kept[j] + received[j * BLOCK : (j + 1) * BLOCK, :].astype(F32)
        sent[j, 0:BLOCK, :] = terms.astype(BF16)
        sent[j, BLOCK:, :] = squares


def finish(received, hidden, mixed):
    parts = []
    for r in range(4):
        pair = received[2 * r, BLOCK:, :].astype(F32) + received[2 * r + 1, BLOCK:, :].astype(F32)
        squares = pair[0:1, :] + pair[1:2, :]
        scale = lax.rsqrt(squares / HEAD_V + 1e-05)
        parts.append(jnp.broadcast_to(scale, (8, BLOCK)))
    parts.append(jnp.zeros((BLOCK - 8 * len(parts), BLOCK), F32))
    columns = jnp.transpose(jnp.concatenate(parts, axis=0))
    total = hidden[...].astype(F32)
    for r in range(4):
        terms = received[2 * r, 0:BLOCK, :].astype(F32)
        terms = terms + received[2 * r + 1, 0:BLOCK, :].astype(F32)
        total = total + columns[:, 8 * r : 8 * r + 1] * terms
    mixed[...] = total.astype(BF16)


def shards(
    hidden_in,
    seg_ids,
    norm_gain,
    w_query,
    w_key,
    w_value,
    w_gate,
    w_decay_down,
    w_decay_up,
    decay_bias,
    conv_query,
    conv_key,
    conv_value,
    head_gain,
    w_out,
):
    block = lax.axis_index("x") * ROWS_Y + lax.axis_index("y")
    block_at = jnp.reshape(block, (1,)).astype(jnp.int32)
    core_at = jnp.reshape(lax.axis_index("core"), (1,)).astype(jnp.int32)

    needed = (
        hidden_in,
        norm_gain.reshape(1, WIDTH),
        w_decay_down.T,
        w_decay_up,
        decay_bias.reshape(1, HEAD_K),
        seg_ids.reshape(BLOCKS, BLOCK),
        conv_query,
        conv_key,
        conv_value,
        w_value,
    )
    hidden, gain, down, up, bias, segs, taps_q, taps_k, taps_v, value_here, copies = local_call(
        fetch_and_spread,
        [*((a.shape, a.dtype) for a in needed), ((8, BLOCK, CHUNK), BF16)],
        block_at,
        core_at,
        *needed,
        scratch=[pltpu.SemaphoreType.DMA((len(needed),))],
        scalars=2,
        anywhere=range(2, 2 + len(needed)),
    )
    of_core = lax.all_to_all(copies, CHIPS, 0, 0)
    whole = lax.all_gather(of_core, "core", axis=0)
    pieces, tail, normed, pre_q, pre_k, pre_v, cumulated, columns, own_rows = local_call(
        block_state,
        [
            ((BLOCKS, PIECE + 16, LANES), BF16),
            ((8, 2 * HEAD_K + CHUNK), F32),
            ((BLOCK, WIDTH), BF16),
            ((BLOCK, HEAD_K), F32),
            ((BLOCK, HEAD_K), F32),
            ((BLOCK, CHUNK), F32),
            ((BLOCK, HEAD_K), F32),
            ((BLOCK, BLOCK), F32),
            ((8, BLOCK), F32),
        ],
        block_at,
        whole,
        gain,
        w_query,
        w_key,
        value_here,
        down,
        up,
        bias,
        segs,
        taps_k,
        taps_v,
        scratch=[
            pltpu.VMEM((BLOCK + 8, HEAD_K), F32),
            pltpu.VMEM((BLOCK + 8, CHUNK), F32),
            pltpu.VMEM((WIDTH, HEAD_K), BF16),
            pltpu.SemaphoreType.DMA((1,)),
        ],
        scalars=1,
        anywhere=(3,),
    )
    edge = lax.ppermute(tail, SEQ, [(i, i + 1) for i in range(BLOCKS - 1)])
    owned = lax.all_to_all(pieces, GRID, 0, 0)
    states, left = local_call(
        scan_blocks,
        [((BLOCKS, PIECE, LANES), BF16), ((PIECE, LANES), F32)],
        block_at,
        owned,
        scalars=1,
    )
    incoming = lax.all_to_all(states, GRID, 0, 0).reshape(2, CHUNK, LANES)
    intra, reach, gate = local_call(
        block_attention,
        [((BLOCK, CHUNK), F32), ((BLOCK, HEAD_K), F32), ((BLOCK, CHUNK), F32)],
        normed,
        w_gate,
        head_gain.reshape(1, CHUNK),
        pre_q,
        pre_k,
        pre_v,
        edge,
        taps_q,
        taps_k,
        taps_v,
        cumulated,
        columns,
        own_rows,
        left,
        scratch=[
            pltpu.VMEM((2, BLOCK + 8, HEAD_K), F32),
            pltpu.VMEM((BLOCK + 8, CHUNK), F32),
        ],
    )
    mine, my_squares, sent = local_call(
        attend,
        [((8, BLOCK, CHUNK), F32), ((8, BLOCK), F32), ((8 * BLOCK + 8, CHUNK), BF16)],
        core_at,
        intra,
        reach,
        incoming,
        gate,
        w_out,
        scalars=1,
    )
    both = lax.all_gather(sent, "core", axis=0)
    (pairs,) = local_call(
        pair_sum, [((8, BLOCK + 8, CHUNK), BF16)], core_at, mine, my_squares, both, scalars=1
    )
    arrived = lax.all_to_all(pairs, CHIPS, 0, 0)
    (mixed,) = local_call(
        finish, [((BLOCK, CHUNK), BF16)], arrived, hidden, last=True
    )
    return mixed


def solution(mesh):
    finer = Mesh(mesh.devices.reshape(ROWS_X, ROWS_Y, 4, 2, 2), ("x", "y", "row", "zhi", "core"))
    part = ("row", "zhi", "core")
    return jax.shard_map(
        shards,
        mesh=finer,
        in_specs=(
            P(SEQ, part),
            P(),
            P(),
            P(None, "row"),
            P(None, "row"),
            P(None, part),
            P(None, part),
            P(),
            P(None, "row"),
            P("row"),
            P(None, "row"),
            P(None, "row"),
            P(None, part),
            P(("zhi", "core")),
            P(part, None),
        ),
        out_specs=P(SEQ, part),
        check_vma=False,
    )
```

```python
import jax
import jax.numpy as jnp
from jax import lax
from jax.experimental import pallas as pl
from jax.experimental.pallas import tpu as pltpu
from jax.sharding import Mesh, PartitionSpec as P

F32 = jnp.float32
BF16 = jnp.bfloat16
HIGHEST = lax.Precision.HIGHEST
HEAD_V = 512
WIDTH = 2048
BLOCK = 128
HEAD_K = 256
CHUNK = 128
LAST = (((1,), (1,)), ((), ()))
FIRST = (((0,), (0,)), ((), ()))

SEQ = ("x", "y")
GRID = ("y", "x")
CHIPS = ("row", "zhi")
ROWS_X, ROWS_Y = 4, 8
LANES = 128
BLOCKS = ROWS_X * ROWS_Y
PIECE = 2 * CHUNK // BLOCKS


def local_call(kernel, outs, *args, scratch=(), scalars=0, plain=(), anywhere=(), last=False):
    elsewhere = (*range(scalars), *plain, *anywhere)
    vmem = pl.BlockSpec(memory_space=pltpu.VMEM)
    smem = pl.BlockSpec(memory_space=pltpu.SMEM)
    args = [
        pltpu.with_memory_space_constraint(a, pltpu.HBM if i in anywhere else pltpu.VMEM)
        if i in anywhere or i not in elsewhere
        else a
        for i, a in enumerate(args)
    ]
    return pl.pallas_call(
        kernel,
        out_shape=[jax.ShapeDtypeStruct(s, t) if last else pltpu.VMEM(s, t) for s, t in outs],
        in_specs=[
            smem if i < scalars else pl.BlockSpec(memory_space=pltpu.HBM) if i in anywhere else vmem
            for i in range(len(args))
        ],
        out_specs=[vmem] * len(outs),
        scratch_shapes=list(scratch),
        name=kernel.__name__,
        compiler_params=pltpu.CompilerParams(vmem_limit_bytes=16 << 20),
    )(*args)


def dot(a, b, dims=(((1,), (0,)), ((), ())), precision=None):
    return lax.dot_general(a, b, dims, precision=precision, preferred_element_type=F32)


def halves(value):
    high = value.astype(BF16)
    return high, (value - high.astype(F32)).astype(BF16)


def pair_rows(value):
    high, low = halves(value)
    shape = (8, value.shape[1])
    index = lax.broadcasted_iota(jnp.int32, shape, 0)
    both = jnp.where(
        index == 0,
        jnp.broadcast_to(high.astype(F32), shape),
        jnp.where(index == 1, jnp.broadcast_to(low.astype(F32), shape), 0.0),
    )
    return both.astype(BF16)


def silu(value):
    return value * jax.nn.sigmoid(value)


def fetch_and_spread(index, core, *refs):
    del index, core
    *refs, copies, arrived = refs
    count = len(refs) // 2
    fetches = [
        pltpu.make_async_copy(refs[i], refs[count + i], arrived.at[i]) for i in range(count)
    ]
    for fetch in fetches:
        fetch.start()
    fetches[0].wait()
    for j in range(8):
        copies[j] = refs[count][...]
    for fetch in fetches[1:]:
        fetch.wait()


def conv(pre, edge, taps, extended, columns):
    extended[0:8, :] = jnp.zeros((8, pre.shape[1]), F32) if edge is None else edge
    extended[8:, :] = pre
    seg = columns[:, 0:1]
    total = taps[0:1, :] * pre
    for j in range(1, 4):
        same = columns[:, 8 * j : 8 * j + 1] == seg
        total = total + jnp.where(
            same, taps[j : j + 1, :] * extended[8 - j : 8 - j + BLOCK, :], 0.0
        )
    return total


def onward(pre, taps, own, following):
    sums = []
    for t in range(3):
        total = jnp.zeros((1, pre.shape[1]), F32)
        for j in range(t + 1, 4):
            at = BLOCK + t - j
            same = following[0:1, t : t + 1] == own[0:1, at : at + 1]
            total = total + jnp.where(same, taps[j : j + 1, :] * pre[at : at + 1, :], 0.0)
        sums.append(total)
    return sums


def stacked_rows(rows):
    shape = (8, LANES)
    index = lax.broadcasted_iota(jnp.int32, shape, 0)
    out = jnp.zeros(shape, F32)
    for at, row in rows.items():
        out = jnp.where(index == at, jnp.broadcast_to(row, shape), out)
    return out.astype(BF16)


def block_state(
    index,
    whole,
    gain,
    query_hbm,
    w_key,
    w_value,
    w_down,
    w_up,
    bias,
    seg_ids,
    taps_k,
    taps_v,
    pieces,
    tail,
    normed,
    pre_q,
    pre_k,
    pre_v,
    cumulated,
    columns_out,
    own_rows,
    extended_k,
    extended_v,
    w_query,
    arrived,
):
    fetch = pltpu.make_async_copy(query_hbm, w_query, arrived.at[0])
    fetch.start()
    chunks = WIDTH // CHUNK
    squares = jnp.zeros((BLOCK, CHUNK), F32)
    for f in range(chunks):
        activ = whole[f % 2, f // 2].astype(F32)
        squares = squares + activ * activ
    scale = lax.rsqrt(jnp.sum(squares, axis=1, keepdims=True) / WIDTH + 1e-06)
    for f in range(chunks):
        lanes = slice(f * CHUNK, (f + 1) * CHUNK)
        activ = whole[f % 2, f // 2].astype(F32)
        normed[:, lanes] = (activ * scale * gain[:, lanes]).astype(BF16)
    rows = normed[...]
    rank_part = dot(rows, w_down[...], LAST)

    at = index[0]
    own = seg_ids[pl.ds(at, 1), :].astype(F32)
    before = seg_ids[pl.ds(jnp.maximum(at - 1, 0), 1), :].astype(F32)
    before = jnp.where(at > 0, before, -1.0)
    following = seg_ids[pl.ds(jnp.minimum(at + 1, BLOCKS - 1), 1), :].astype(F32)
    own = jnp.broadcast_to(own, (8, BLOCK))
    before = jnp.broadcast_to(before, (8, BLOCK))
    lane = lax.broadcasted_iota(jnp.int32, (8, BLOCK), 1)
    parts = [own]
    for j in range(1, 4):
        parts.append(jnp.where(lane < j, pltpu.roll(before, j, 1), pltpu.roll(own, j, 1)))
    before = jnp.broadcast_to(before[:, BLOCK - 1 :], (8, BLOCK))
    last = jnp.broadcast_to(own[:, BLOCK - 1 :], (8, BLOCK))
    parts += [before, last]
    parts.append(jnp.zeros((BLOCK - 8 * len(parts), BLOCK), F32))
    columns = jnp.transpose(jnp.concatenate(parts, axis=0))
    columns_out[...] = columns
    own_rows[...] = own

    logits = dot(rank_part, w_up[...].astype(F32), precision=HIGHEST) + bias[...]
    log_decay = (jnp.minimum(logits, 0.0) - jnp.log(1.0 + jnp.exp(-jnp.abs(logits)))) / 16.0
    row_iota = lax.broadcasted_iota(jnp.int32, (BLOCK, BLOCK), 0)
    col_iota = lax.broadcasted_iota(jnp.int32, (BLOCK, BLOCK), 1)
    lower = jnp.where(row_iota >= col_iota, 1.0, 0.0).astype(F32)
    cum = dot(lower, log_decay, precision=HIGHEST)
    cumulated[...] = cum

    of_keys = dot(rows, w_key[...])
    of_values = dot(rows, w_value[...])
    pre_k[...] = of_keys
    pre_v[...] = of_values
    sums_k = conv(of_keys, None, taps_k, extended_k, columns)
    sums_v = conv(of_values, None, taps_v, extended_v, columns)
    next_k = onward(of_keys, taps_k, own, following)
    next_v = onward(of_values, taps_v, own, following)
    final = cum[BLOCK - 1 :, :]
    factors = jnp.where(columns[:, 0:1] == columns[:, 40:41], jnp.exp(final - cum), 0.0)
    later = lax.broadcasted_iota(jnp.int32, (BLOCK, HEAD_K), 0) >= 3
    pushed = jnp.where(later, silu(sums_k) * factors, 0.0)
    state = dot(silu(sums_v).astype(BF16), pushed.astype(BF16), FIRST)
    keep = jnp.where(before[0:1, 0:1] == last[0:1, 0:1], jnp.exp(final), 0.0)
    high, low = halves(keep)
    lane = lax.broadcasted_iota(jnp.int32, (1, LANES), 1)
    mixed_v = []
    for upper in range(2):
        mine = (lane >= LANES // 2) == (upper == 1)
        mixed_v.append(
            [
                jnp.where(mine, sums_v[t : t + 1, :], pltpu.roll(next_v[t], LANES // 2, 1))
                for t in range(3)
            ]
        )
    for h in range(2):
        lanes = slice(h * LANES, (h + 1) * LANES)
        rows_b = {0: high.astype(F32)[:, lanes], 1: low.astype(F32)[:, lanes]}
        for t in range(3):
            rows_b[2 + t] = sums_k[t : t + 1, lanes]
            rows_b[5 + t] = next_k[t][:, lanes]
        tile_b = stacked_rows(rows_b)
        for upper in range(2):
            rows_c = {2 + t: factors[t : t + 1, lanes] for t in range(3)}
            rows_c.update({5 + t: mixed_v[upper][t] for t in range(3)})
            tile_c = stacked_rows(rows_c)
            for j in range(8):
                g = 8 * upper + j
                p = h * BLOCKS // 2 + g
                pieces[p, 0:PIECE, :] = state[g * PIECE : (g + 1) * PIECE, lanes].astype(BF16)
                pieces[p, PIECE : PIECE + 8, :] = tile_b
                pieces[p, PIECE + 8 :, :] = tile_c
    fetch.wait()
    of_queries = dot(rows, w_query[...])
    pre_q[...] = of_queries
    tail[:, :HEAD_K] = of_queries[BLOCK - 8 :, :]
    tail[:, HEAD_K : 2 * HEAD_K] = of_keys[BLOCK - 8 :, :]
    tail[:, 2 * HEAD_K :] = of_values[BLOCK - 8 :, :]


def block_attention(
    normed,
    w_gate,
    head_gain,
    pre_q,
    pre_k,
    pre_v,
    edge,
    taps_q,
    taps_k,
    taps_v,
    cumulated,
    columns,
    own_rows,
    left,
    intra,
    reach,
    gate,
    extended,
    extended_v,
):
    del left
    gate[...] = silu(dot(normed[...], w_gate[...])) * head_gain[...]
    edges = edge[...]
    queries = silu(conv(pre_q[...], edges[:, :HEAD_K], taps_q, extended.at[0], columns))
    queries = queries * HEAD_K ** (-0.5)
    keys = silu(
        conv(pre_k[...], edges[:, HEAD_K : 2 * HEAD_K], taps_k, extended.at[1], columns)
    )
    values = silu(conv(pre_v[...], edges[:, 2 * HEAD_K :], taps_v, extended_v, columns))
    cum, seg = cumulated[...], columns[:, 0:1]
    row_iota = lax.broadcasted_iota(jnp.int32, (BLOCK, BLOCK), 0)
    col_iota = lax.broadcasted_iota(jnp.int32, (BLOCK, BLOCK), 1)
    reach[...] = jnp.where(seg == columns[:, 32:33], queries * jnp.exp(cum), 0.0)
    weights = jnp.zeros((BLOCK, BLOCK), F32)
    for half in (8, 16, 32, 64):
        anchors = [
            jnp.broadcast_to(cum[b + half - 1 : b + half, :], (2 * half, HEAD_K))
            for b in range(0, BLOCK, 2 * half)
        ]
        anchor = jnp.concatenate(anchors, axis=0) if len(anchors) > 1 else anchors[0]
        factor = jnp.exp(-jnp.abs(cum - anchor))
        part = dot((queries * factor).astype(BF16), (keys * factor).astype(BF16), LAST)
        inside = (
            (row_iota // (2 * half) == col_iota // (2 * half))
            & (row_iota % (2 * half) >= half)
            & (col_iota % (2 * half) < half)
        )
        weights = jnp.where(inside, part, weights)
    groups = (BLOCK // 8, 8, HEAD_K)
    cum_g, keys_g = cum.reshape(groups), keys.reshape(groups)
    queries_g = queries.reshape(groups)
    for by in range(8):
        if by:
            spread = jnp.minimum(cum_g - pltpu.roll(cum_g, by, 1), 0.0)
            product = queries_g * pltpu.roll(keys_g, by, 1) * jnp.exp(spread)
        else:
            product = queries_g * keys_g
        sums = jnp.sum(product.reshape(BLOCK, HEAD_K), axis=1, keepdims=True)
        inside = (row_iota - col_iota == by) & (row_iota % 8 >= by)
        weights = jnp.where(inside, sums, weights)
    visible = (seg == own_rows[0:1, :]) & (row_iota >= col_iota)
    weights = jnp.where(visible, weights, 0.0)
    intra[...] = dot(weights.astype(BF16), values.astype(BF16))


def scan_blocks(index, pieces, edge, states, left):
    del edge
    owner = (index[0] % ROWS_Y) * ROWS_X + index[0] // ROWS_Y
    first = (owner % (BLOCKS // 2)) * PIECE
    order = [(block % ROWS_Y) * ROWS_X + block // ROWS_Y for block in range(BLOCKS)]
    shape = (BLOCKS, 8, LANES)
    tiles_b = jnp.stack([pieces[at, PIECE : PIECE + 8, :].astype(F32) for at in order])
    tiles_c = jnp.stack([pieces[at, PIECE + 8 :, :].astype(F32) for at in order])
    nothing = jnp.zeros((1, 8, LANES), F32)
    back_b = jnp.concatenate([nothing, tiles_b[:-1]], axis=0)
    back_c = jnp.concatenate([nothing, tiles_c[:-1]], axis=0)
    pushed = silu(tiles_b + pltpu.roll(back_b, 5, 1)) * tiles_c
    values = pltpu.roll(silu(tiles_c + pltpu.roll(back_c, LANES // 2, 2)), 5, 1)
    row = lax.broadcasted_iota(jnp.int32, shape, 1)
    values = jnp.where((row >= 2) & (row < 5), values, 0.0)
    rows = BLOCKS * 8
    lane = lax.broadcasted_iota(jnp.int32, (PIECE, LANES), 1)
    chosen = lane == lax.broadcasted_iota(jnp.int32, (PIECE, LANES), 0) + first
    chosen = jnp.where(chosen, 1.0, 0.0).astype(BF16)
    mine = dot(chosen, values.reshape(rows, LANES).astype(BF16), LAST)
    same = lax.broadcasted_iota(jnp.int32, (rows, rows), 0) // 8
    same = same == lax.broadcasted_iota(jnp.int32, (rows, rows), 1) // 8
    spread = jnp.where(same, jnp.concatenate([mine] * BLOCKS, axis=0), 0.0)
    added = dot(spread.astype(BF16), pushed.reshape(rows, LANES).astype(BF16))
    state = jnp.zeros((PIECE, LANES), F32)
    for block, at in enumerate(order):
        states[at] = state.astype(BF16)
        decay = tiles_b[block, 0:1, :] + tiles_b[block, 1:2, :]
        own = pieces[at, 0:PIECE, :].astype(F32) + added[block * 8 : block * 8 + 8, :]
        state = state * decay + own
    left[...] = state


def attend(index, intra, reach, incoming, gate, w_out, kept, kept_squares, sent):
    high, low = halves(reach[...])
    state = jnp.concatenate([incoming[0], incoming[1]], axis=1)
    attended = intra[...] + dot(high, state, LAST) + dot(low, state, LAST)
    squares = dot(jnp.ones((8, CHUNK), F32), attended * attended, LAST, precision=HIGHEST)
    terms = dot((attended * gate[...]).astype(BF16), w_out[...])
    first = index[0] == 0
    for j in range(8):
        even = terms[:, (2 * j) * CHUNK : (2 * j + 1) * CHUNK]
        odd = terms[:, (2 * j + 1) * CHUNK : (2 * j + 2) * CHUNK]
        kept[j] = jnp.where(first, even, odd)
        sent[j * BLOCK : (j + 1) * BLOCK, :] = jnp.where(first, odd, even).astype(BF16)
    kept_squares[...] = squares
    sent[8 * BLOCK :, :] = pair_rows(squares[0:1, :])


def pair_sum(index, kept, kept_squares, both, sent):
    received = both.at[1 - index[0]]
    other = received[8 * BLOCK :, :].astype(F32)
    squares = pair_rows(kept_squares[0:1, :] + other[0:1, :] + other[1:2, :])
    for j in range(8):
        terms = kept[j] + received[j * BLOCK : (j + 1) * BLOCK, :].astype(F32)
        sent[j, 0:BLOCK, :] = terms.astype(BF16)
        sent[j, BLOCK:, :] = squares


def finish(received, hidden, mixed):
    parts = []
    for r in range(4):
        pair = received[2 * r, BLOCK:, :].astype(F32) + received[2 * r + 1, BLOCK:, :].astype(F32)
        squares = pair[0:1, :] + pair[1:2, :]
        scale = lax.rsqrt(squares / HEAD_V + 1e-05)
        parts.append(jnp.broadcast_to(scale, (8, BLOCK)))
    parts.append(jnp.zeros((BLOCK - 8 * len(parts), BLOCK), F32))
    columns = jnp.transpose(jnp.concatenate(parts, axis=0))
    total = hidden[...].astype(F32)
    for r in range(4):
        terms = received[2 * r, 0:BLOCK, :].astype(F32)
        terms = terms + received[2 * r + 1, 0:BLOCK, :].astype(F32)
        total = total + columns[:, 8 * r : 8 * r + 1] * terms
    mixed[...] = total.astype(BF16)


def shards(
    hidden_in,
    seg_ids,
    norm_gain,
    w_query,
    w_key,
    w_value,
    w_gate,
    w_decay_down,
    w_decay_up,
    decay_bias,
    conv_query,
    conv_key,
    conv_value,
    head_gain,
    w_out,
):
    block = lax.axis_index("x") * ROWS_Y + lax.axis_index("y")
    block_at = jnp.reshape(block, (1,)).astype(jnp.int32)
    core_at = jnp.reshape(lax.axis_index("core"), (1,)).astype(jnp.int32)

    needed = (
        hidden_in,
        norm_gain.reshape(1, WIDTH),
        w_decay_down.T,
        w_decay_up,
        decay_bias.reshape(1, HEAD_K),
        seg_ids.reshape(BLOCKS, BLOCK),
        conv_query,
        conv_key,
        conv_value,
        w_value,
    )
    hidden, gain, down, up, bias, segs, taps_q, taps_k, taps_v, value_here, copies = local_call(
        fetch_and_spread,
        [*((a.shape, a.dtype) for a in needed), ((8, BLOCK, CHUNK), BF16)],
        block_at,
        core_at,
        *needed,
        scratch=[pltpu.SemaphoreType.DMA((len(needed),))],
        scalars=2,
        anywhere=range(2, 2 + len(needed)),
    )
    of_core = lax.all_to_all(copies, CHIPS, 0, 0)
    whole = lax.all_gather(of_core, "core", axis=0)
    pieces, tail, normed, pre_q, pre_k, pre_v, cumulated, columns, own_rows = local_call(
        block_state,
        [
            ((BLOCKS, PIECE + 16, LANES), BF16),
            ((8, 2 * HEAD_K + CHUNK), F32),
            ((BLOCK, WIDTH), BF16),
            ((BLOCK, HEAD_K), F32),
            ((BLOCK, HEAD_K), F32),
            ((BLOCK, CHUNK), F32),
            ((BLOCK, HEAD_K), F32),
            ((BLOCK, BLOCK), F32),
            ((8, BLOCK), F32),
        ],
        block_at,
        whole,
        gain,
        w_query,
        w_key,
        value_here,
        down,
        up,
        bias,
        segs,
        taps_k,
        taps_v,
        scratch=[
            pltpu.VMEM((BLOCK + 8, HEAD_K), F32),
            pltpu.VMEM((BLOCK + 8, CHUNK), F32),
            pltpu.VMEM((WIDTH, HEAD_K), BF16),
            pltpu.SemaphoreType.DMA((1,)),
        ],
        scalars=1,
        anywhere=(3,),
    )
    edge = lax.ppermute(tail, SEQ, [(i, i + 1) for i in range(BLOCKS - 1)])
    owned = lax.all_to_all(pieces, GRID, 0, 0)
    states, left = local_call(
        scan_blocks,
        [((BLOCKS, PIECE, LANES), BF16), ((PIECE, LANES), F32)],
        block_at,
        owned,
        edge,
        scalars=1,
    )
    incoming = lax.all_to_all(states, GRID, 0, 0).reshape(2, CHUNK, LANES)
    intra, reach, gate = local_call(
        block_attention,
        [((BLOCK, CHUNK), F32), ((BLOCK, HEAD_K), F32), ((BLOCK, CHUNK), F32)],
        normed,
        w_gate,
        head_gain.reshape(1, CHUNK),
        pre_q,
        pre_k,
        pre_v,
        edge,
        taps_q,
        taps_k,
        taps_v,
        cumulated,
        columns,
        own_rows,
        left,
        scratch=[
            pltpu.VMEM((2, BLOCK + 8, HEAD_K), F32),
            pltpu.VMEM((BLOCK + 8, CHUNK), F32),
        ],
    )
    mine, my_squares, sent = local_call(
        attend,
        [((8, BLOCK, CHUNK), F32), ((8, BLOCK), F32), ((8 * BLOCK + 8, CHUNK), BF16)],
        core_at,
        intra,
        reach,
        incoming,
        gate,
        w_out,
        scalars=1,
    )
    both = lax.all_gather(sent, "core", axis=0)
    (pairs,) = local_call(
        pair_sum, [((8, BLOCK + 8, CHUNK), BF16)], core_at, mine, my_squares, both, scalars=1
    )
    arrived = lax.all_to_all(pairs, CHIPS, 0, 0)
    (mixed,) = local_call(
        finish, [((BLOCK, CHUNK), BF16)], arrived, hidden, last=True
    )
    return mixed


def solution(mesh):
    finer = Mesh(mesh.devices.reshape(ROWS_X, ROWS_Y, 4, 2, 2), ("x", "y", "row", "zhi", "core"))
    part = ("row", "zhi", "core")
    return jax.shard_map(
        shards,
        mesh=finer,
        in_specs=(
            P(SEQ, part),
            P(),
            P(),
            P(None, "row"),
            P(None, "row"),
            P(None, part),
            P(None, part),
            P(),
            P(None, "row"),
            P("row"),
            P(None, "row"),
            P(None, "row"),
            P(None, part),
            P(("zhi", "core")),
            P(part, None),
        ),
        out_specs=P(SEQ, part),
        check_vma=False,
    )
```

```python
import jax
import jax.numpy as jnp
from jax import lax
from jax.experimental import pallas as pl
from jax.experimental.pallas import tpu as pltpu
from jax.sharding import Mesh, PartitionSpec as P

F32 = jnp.float32
BF16 = jnp.bfloat16
HIGHEST = lax.Precision.HIGHEST
HEAD_V = 512
WIDTH = 2048
BLOCK = 128
HEAD_K = 256
CHUNK = 128
LAST = (((1,), (1,)), ((), ()))
FIRST = (((0,), (0,)), ((), ()))

SEQ = ("x", "y")
GRID = ("y", "x")
CHIPS = ("row", "zhi")
ROWS_X, ROWS_Y = 4, 8
LANES = 128
BLOCKS = ROWS_X * ROWS_Y
PIECE = 2 * CHUNK // BLOCKS


def local_call(kernel, outs, *args, scratch=(), scalars=0, plain=(), anywhere=(), last=False):
    elsewhere = (*range(scalars), *plain, *anywhere)
    vmem = pl.BlockSpec(memory_space=pltpu.VMEM)
    smem = pl.BlockSpec(memory_space=pltpu.SMEM)
    args = [
        pltpu.with_memory_space_constraint(a, pltpu.HBM if i in anywhere else pltpu.VMEM)
        if i in anywhere or i not in elsewhere
        else a
        for i, a in enumerate(args)
    ]
    return pl.pallas_call(
        kernel,
        out_shape=[jax.ShapeDtypeStruct(s, t) if last else pltpu.VMEM(s, t) for s, t in outs],
        in_specs=[
            smem if i < scalars else pl.BlockSpec(memory_space=pltpu.HBM) if i in anywhere else vmem
            for i in range(len(args))
        ],
        out_specs=[vmem] * len(outs),
        scratch_shapes=list(scratch),
        name=kernel.__name__,
        compiler_params=pltpu.CompilerParams(vmem_limit_bytes=16 << 20),
    )(*args)


def dot(a, b, dims=(((1,), (0,)), ((), ())), precision=None):
    return lax.dot_general(a, b, dims, precision=precision, preferred_element_type=F32)


def halves(value):
    high = value.astype(BF16)
    return high, (value - high.astype(F32)).astype(BF16)


def pair_rows(value):
    high, low = halves(value)
    shape = (8, value.shape[1])
    index = lax.broadcasted_iota(jnp.int32, shape, 0)
    both = jnp.where(
        index == 0,
        jnp.broadcast_to(high.astype(F32), shape),
        jnp.where(index == 1, jnp.broadcast_to(low.astype(F32), shape), 0.0),
    )
    return both.astype(BF16)


def silu(value):
    return value * jax.nn.sigmoid(value)


def fetch_and_spread(index, core, *refs):
    del index, core
    *refs, copies, taps, arrived, gain = refs
    count = (len(refs) + 1) // 2
    targets = [*refs[count:], gain]
    fetches = [pltpu.make_async_copy(refs[i], targets[i], arrived.at[i]) for i in range(count)]
    for fetch in fetches:
        fetch.start()
    fetches[0].wait()
    for j in range(8):
        copies[j] = refs[count][...]
    for fetch in fetches[1:]:
        fetch.wait()
    taps[0:4, :] = refs[2 * count - 2][...]
    taps[4:8, :CHUNK] = jnp.broadcast_to(gain[...], (4, CHUNK))
    taps[4:8, CHUNK:] = jnp.zeros((4, HEAD_K - CHUNK), F32)


def conv(pre, edge, taps, extended, columns):
    extended[0:8, :] = jnp.zeros((8, pre.shape[1]), F32) if edge is None else edge
    extended[8:, :] = pre
    seg = columns[:, 0:1]
    total = taps[0:1, :] * pre
    for j in range(1, 4):
        same = columns[:, 8 * j : 8 * j + 1] == seg
        total = total + jnp.where(
            same, taps[j : j + 1, :] * extended[8 - j : 8 - j + BLOCK, :], 0.0
        )
    return total


def onward(pre, taps, own, following):
    sums = []
    for t in range(3):
        total = jnp.zeros((1, pre.shape[1]), F32)
        for j in range(t + 1, 4):
            at = BLOCK + t - j
            same = following[0:1, t : t + 1] == own[0:1, at : at + 1]
            total = total + jnp.where(same, taps[j : j + 1, :] * pre[at : at + 1, :], 0.0)
        sums.append(total)
    return sums


def stacked_rows(rows):
    shape = (8, LANES)
    index = lax.broadcasted_iota(jnp.int32, shape, 0)
    out = jnp.zeros(shape, F32)
    for at, row in rows.items():
        out = jnp.where(index == at, jnp.broadcast_to(row, shape), out)
    return out.astype(BF16)


def block_state(
    index,
    whole,
    gain,
    query_hbm,
    w_key,
    w_value,
    w_down,
    w_up,
    bias,
    seg_ids,
    taps_k,
    taps_v,
    pieces,
    tail,
    normed,
    pre_q,
    pre_k,
    pre_v,
    cumulated,
    columns_out,
    own_rows,
    extended_k,
    extended_v,
    w_query,
    arrived,
):
    fetch = pltpu.make_async_copy(query_hbm, w_query, arrived.at[0])
    fetch.start()
    chunks = WIDTH // CHUNK
    squares = jnp.zeros((BLOCK, CHUNK), F32)
    for f in range(chunks):
        activ = whole[f % 2, f // 2].astype(F32)
        squares = squares + activ * activ
    scale = lax.rsqrt(jnp.sum(squares, axis=1, keepdims=True) / WIDTH + 1e-06)
    for f in range(chunks):
        lanes = slice(f * CHUNK, (f + 1) * CHUNK)
        activ = whole[f % 2, f // 2].astype(F32)
        normed[:, lanes] = (activ * scale * gain[:, lanes]).astype(BF16)
    rows = normed[...]
    rank_part = dot(rows, w_down[...], LAST)

    at = index[0]
    own = seg_ids[pl.ds(at, 1), :].astype(F32)
    before = seg_ids[pl.ds(jnp.maximum(at - 1, 0), 1), :].astype(F32)
    before = jnp.where(at > 0, before, -1.0)
    following = seg_ids[pl.ds(jnp.minimum(at + 1, BLOCKS - 1), 1), :].astype(F32)
    own = jnp.broadcast_to(own, (8, BLOCK))
    before = jnp.broadcast_to(before, (8, BLOCK))
    lane = lax.broadcasted_iota(jnp.int32, (8, BLOCK), 1)
    parts = [own]
    for j in range(1, 4):
        parts.append(jnp.where(lane < j, pltpu.roll(before, j, 1), pltpu.roll(own, j, 1)))
    before = jnp.broadcast_to(before[:, BLOCK - 1 :], (8, BLOCK))
    last = jnp.broadcast_to(own[:, BLOCK - 1 :], (8, BLOCK))
    parts += [before, last]
    parts.append(jnp.zeros((BLOCK - 8 * len(parts), BLOCK), F32))
    columns = jnp.transpose(jnp.concatenate(parts, axis=0))
    columns_out[...] = columns
    own_rows[...] = own

    logits = dot(rank_part, w_up[...].astype(F32), precision=HIGHEST) + bias[...]
    log_decay = (jnp.minimum(logits, 0.0) - jnp.log(1.0 + jnp.exp(-jnp.abs(logits)))) / 16.0
    row_iota = lax.broadcasted_iota(jnp.int32, (BLOCK, BLOCK), 0)
    col_iota = lax.broadcasted_iota(jnp.int32, (BLOCK, BLOCK), 1)
    lower = jnp.where(row_iota >= col_iota, 1.0, 0.0).astype(F32)
    cum = dot(lower, log_decay, precision=HIGHEST)
    cumulated[...] = cum

    of_keys = dot(rows, w_key[...])
    of_values = dot(rows, w_value[...])
    pre_k[...] = of_keys
    pre_v[...] = of_values
    sums_k = conv(of_keys, None, taps_k, extended_k, columns)
    sums_v = conv(of_values, None, taps_v, extended_v, columns)
    next_k = onward(of_keys, taps_k, own, following)
    next_v = onward(of_values, taps_v, own, following)
    final = cum[BLOCK - 1 :, :]
    factors = jnp.where(columns[:, 0:1] == columns[:, 40:41], jnp.exp(final - cum), 0.0)
    later = lax.broadcasted_iota(jnp.int32, (BLOCK, HEAD_K), 0) >= 3
    pushed = jnp.where(later, silu(sums_k) * factors, 0.0)
    state = dot(silu(sums_v).astype(BF16), pushed.astype(BF16), FIRST)
    keep = jnp.where(before[0:1, 0:1] == last[0:1, 0:1], jnp.exp(final), 0.0)
    high, low = halves(keep)
    lane = lax.broadcasted_iota(jnp.int32, (1, LANES), 1)
    mixed_v = []
    for upper in range(2):
        mine = (lane >= LANES // 2) == (upper == 1)
        mixed_v.append(
            [
                jnp.where(mine, sums_v[t : t + 1, :], pltpu.roll(next_v[t], LANES // 2, 1))
                for t in range(3)
            ]
        )
    for h in range(2):
        lanes = slice(h * LANES, (h + 1) * LANES)
        rows_b = {0: high.astype(F32)[:, lanes], 1: low.astype(F32)[:, lanes]}
        for t in range(3):
            rows_b[2 + t] = sums_k[t : t + 1, lanes]
            rows_b[5 + t] = next_k[t][:, lanes]
        tile_b = stacked_rows(rows_b)
        for upper in range(2):
            rows_c = {2 + t: factors[t : t + 1, lanes] for t in range(3)}
            rows_c.update({5 + t: mixed_v[upper][t] for t in range(3)})
            tile_c = stacked_rows(rows_c)
            for j in range(8):
                g = 8 * upper + j
                p = h * BLOCKS // 2 + g
                pieces[p, 0:PIECE, :] = state[g * PIECE : (g + 1) * PIECE, lanes].astype(BF16)
                pieces[p, PIECE : PIECE + 8, :] = tile_b
                pieces[p, PIECE + 8 :, :] = tile_c
    fetch.wait()
    of_queries = dot(rows, w_query[...])
    pre_q[...] = of_queries
    tail[:, :HEAD_K] = of_queries[BLOCK - 8 :, :]
    tail[:, HEAD_K : 2 * HEAD_K] = of_keys[BLOCK - 8 :, :]
    tail[:, 2 * HEAD_K :] = of_values[BLOCK - 8 :, :]


def output_gate(normed, w_gate, taps, left, gate):
    del left
    gate[...] = silu(dot(normed[...], w_gate[...])) * taps[4:5, :CHUNK]


def block_attention(
    pre_q,
    pre_k,
    pre_v,
    edge,
    taps_q,
    taps_k,
    taps_v,
    cumulated,
    columns,
    own_rows,
    left,
    intra,
    reach,
    extended,
    extended_v,
):
    del left
    edges = edge[...]
    queries = silu(conv(pre_q[...], edges[:, :HEAD_K], taps_q, extended.at[0], columns))
    queries = queries * HEAD_K ** (-0.5)
    keys = silu(
        conv(pre_k[...], edges[:, HEAD_K : 2 * HEAD_K], taps_k, extended.at[1], columns)
    )
    values = silu(conv(pre_v[...], edges[:, 2 * HEAD_K :], taps_v, extended_v, columns))
    cum, seg = cumulated[...], columns[:, 0:1]
    row_iota = lax.broadcasted_iota(jnp.int32, (BLOCK, BLOCK), 0)
    col_iota = lax.broadcasted_iota(jnp.int32, (BLOCK, BLOCK), 1)
    reach[...] = jnp.where(seg == columns[:, 32:33], queries * jnp.exp(cum), 0.0)
    weights = jnp.zeros((BLOCK, BLOCK), F32)
    for half in (8, 16, 32, 64):
        anchors = [
            jnp.broadcast_to(cum[b + half - 1 : b + half, :], (2 * half, HEAD_K))
            for b in range(0, BLOCK, 2 * half)
        ]
        anchor = jnp.concatenate(anchors, axis=0) if len(anchors) > 1 else anchors[0]
        factor = jnp.exp(-jnp.abs(cum - anchor))
        part = dot((queries * factor).astype(BF16), (keys * factor).astype(BF16), LAST)
        inside = (
            (row_iota // (2 * half) == col_iota // (2 * half))
            & (row_iota % (2 * half) >= half)
            & (col_iota % (2 * half) < half)
        )
        weights = jnp.where(inside, part, weights)
    groups = (BLOCK // 8, 8, HEAD_K)
    cum_g, keys_g = cum.reshape(groups), keys.reshape(groups)
    queries_g = queries.reshape(groups)
    for by in range(8):
        if by:
            spread = jnp.minimum(cum_g - pltpu.roll(cum_g, by, 1), 0.0)
            product = queries_g * pltpu.roll(keys_g, by, 1) * jnp.exp(spread)
        else:
            product = queries_g * keys_g
        sums = jnp.sum(product.reshape(BLOCK, HEAD_K), axis=1, keepdims=True)
        inside = (row_iota - col_iota == by) & (row_iota % 8 >= by)
        weights = jnp.where(inside, sums, weights)
    visible = (seg == own_rows[0:1, :]) & (row_iota >= col_iota)
    weights = jnp.where(visible, weights, 0.0)
    intra[...] = dot(weights.astype(BF16), values.astype(BF16))


def scan_blocks(index, pieces, states, left):
    owner = (index[0] % ROWS_Y) * ROWS_X + index[0] // ROWS_Y
    first = (owner % (BLOCKS // 2)) * PIECE
    order = [(block % ROWS_Y) * ROWS_X + block // ROWS_Y for block in range(BLOCKS)]
    shape = (BLOCKS, 8, LANES)
    tiles_b = jnp.stack([pieces[at, PIECE : PIECE + 8, :].astype(F32) for at in order])
    tiles_c = jnp.stack([pieces[at, PIECE + 8 :, :].astype(F32) for at in order])
    nothing = jnp.zeros((1, 8, LANES), F32)
    back_b = jnp.concatenate([nothing, tiles_b[:-1]], axis=0)
    back_c = jnp.concatenate([nothing, tiles_c[:-1]], axis=0)
    pushed = silu(tiles_b + pltpu.roll(back_b, 5, 1)) * tiles_c
    values = pltpu.roll(silu(tiles_c + pltpu.roll(back_c, LANES // 2, 2)), 5, 1)
    row = lax.broadcasted_iota(jnp.int32, shape, 1)
    values = jnp.where((row >= 2) & (row < 5), values, 0.0)
    rows = BLOCKS * 8
    lane = lax.broadcasted_iota(jnp.int32, (PIECE, LANES), 1)
    chosen = lane == lax.broadcasted_iota(jnp.int32, (PIECE, LANES), 0) + first
    chosen = jnp.where(chosen, 1.0, 0.0).astype(BF16)
    mine = dot(chosen, values.reshape(rows, LANES).astype(BF16), LAST)
    same = lax.broadcasted_iota(jnp.int32, (rows, rows), 0) // 8
    same = same == lax.broadcasted_iota(jnp.int32, (rows, rows), 1) // 8
    spread = jnp.where(same, jnp.concatenate([mine] * BLOCKS, axis=0), 0.0)
    added = dot(spread.astype(BF16), pushed.reshape(rows, LANES).astype(BF16))
    state = jnp.zeros((PIECE, LANES), F32)
    for block, at in enumerate(order):
        states[at] = state.astype(BF16)
        decay = tiles_b[block, 0:1, :] + tiles_b[block, 1:2, :]
        own = pieces[at, 0:PIECE, :].astype(F32) + added[block * 8 : block * 8 + 8, :]
        state = state * decay + own
    left[...] = state


def attend(index, intra, reach, incoming, gate, w_out, kept, kept_squares, sent):
    high, low = halves(reach[...])
    state = jnp.concatenate([incoming[0], incoming[1]], axis=1)
    attended = intra[...] + dot(high, state, LAST) + dot(low, state, LAST)
    squares = dot(jnp.ones((8, CHUNK), F32), attended * attended, LAST, precision=HIGHEST)
    terms = dot((attended * gate[...]).astype(BF16), w_out[...])
    first = index[0] == 0
    for j in range(8):
        even = terms[:, (2 * j) * CHUNK : (2 * j + 1) * CHUNK]
        odd = terms[:, (2 * j + 1) * CHUNK : (2 * j + 2) * CHUNK]
        kept[j] = jnp.where(first, even, odd)
        sent[j * BLOCK : (j + 1) * BLOCK, :] = jnp.where(first, odd, even).astype(BF16)
    kept_squares[...] = squares
    sent[8 * BLOCK :, :] = pair_rows(squares[0:1, :])


def pair_sum(index, kept, kept_squares, both, sent):
    received = both.at[1 - index[0]]
    other = received[8 * BLOCK :, :].astype(F32)
    squares = pair_rows(kept_squares[0:1, :] + other[0:1, :] + other[1:2, :])
    for j in range(8):
        terms = kept[j] + received[j * BLOCK : (j + 1) * BLOCK, :].astype(F32)
        sent[j, 0:BLOCK, :] = terms.astype(BF16)
        sent[j, BLOCK:, :] = squares


def finish(received, hidden, mixed):
    parts = []
    for r in range(4):
        pair = received[2 * r, BLOCK:, :].astype(F32) + received[2 * r + 1, BLOCK:, :].astype(F32)
        squares = pair[0:1, :] + pair[1:2, :]
        scale = lax.rsqrt(squares / HEAD_V + 1e-05)
        parts.append(jnp.broadcast_to(scale, (8, BLOCK)))
    parts.append(jnp.zeros((BLOCK - 8 * len(parts), BLOCK), F32))
    columns = jnp.transpose(jnp.concatenate(parts, axis=0))
    total = hidden[...].astype(F32)
    for r in range(4):
        terms = received[2 * r, 0:BLOCK, :].astype(F32)
        terms = terms + received[2 * r + 1, 0:BLOCK, :].astype(F32)
        total = total + columns[:, 8 * r : 8 * r + 1] * terms
    mixed[...] = total.astype(BF16)


def shards(
    hidden_in,
    seg_ids,
    norm_gain,
    w_query,
    w_key,
    w_value,
    w_gate,
    w_decay_down,
    w_decay_up,
    decay_bias,
    conv_query,
    conv_key,
    conv_value,
    head_gain,
    w_out,
):
    block = lax.axis_index("x") * ROWS_Y + lax.axis_index("y")
    block_at = jnp.reshape(block, (1,)).astype(jnp.int32)
    core_at = jnp.reshape(lax.axis_index("core"), (1,)).astype(jnp.int32)

    needed = (
        hidden_in,
        norm_gain.reshape(1, WIDTH),
        w_decay_down.T,
        w_decay_up,
        decay_bias.reshape(1, HEAD_K),
        seg_ids.reshape(BLOCKS, BLOCK),
        conv_key,
        conv_value,
        w_value,
        conv_query,
        head_gain.reshape(1, CHUNK),
    )
    hidden, gain, down, up, bias, segs, taps_k, taps_v, value_here, _, copies, taps_q = local_call(
        fetch_and_spread,
        [
            *((a.shape, a.dtype) for a in needed[:-1]),
            ((8, BLOCK, CHUNK), BF16),
            ((8, HEAD_K), F32),
        ],
        block_at,
        core_at,
        *needed,
        scratch=[pltpu.SemaphoreType.DMA((len(needed),)), pltpu.VMEM((1, CHUNK), F32)],
        scalars=2,
        anywhere=range(2, 2 + len(needed)),
    )
    of_core = lax.all_to_all(copies, CHIPS, 0, 0)
    whole = lax.all_gather(of_core, "core", axis=0)
    pieces, tail, normed, pre_q, pre_k, pre_v, cumulated, columns, own_rows = local_call(
        block_state,
        [
            ((BLOCKS, PIECE + 16, LANES), BF16),
            ((8, 2 * HEAD_K + CHUNK), F32),
            ((BLOCK, WIDTH), BF16),
            ((BLOCK, HEAD_K), F32),
            ((BLOCK, HEAD_K), F32),
            ((BLOCK, CHUNK), F32),
            ((BLOCK, HEAD_K), F32),
            ((BLOCK, BLOCK), F32),
            ((8, BLOCK), F32),
        ],
        block_at,
        whole,
        gain,
        w_query,
        w_key,
        value_here,
        down,
        up,
        bias,
        segs,
        taps_k,
        taps_v,
        scratch=[
            pltpu.VMEM((BLOCK + 8, HEAD_K), F32),
            pltpu.VMEM((BLOCK + 8, CHUNK), F32),
            pltpu.VMEM((WIDTH, HEAD_K), BF16),
            pltpu.SemaphoreType.DMA((1,)),
        ],
        scalars=1,
        anywhere=(3,),
    )
    edge = lax.ppermute(tail, SEQ, [(i, i + 1) for i in range(BLOCKS - 1)])
    owned = lax.all_to_all(pieces, GRID, 0, 0)
    states, left = local_call(
        scan_blocks,
        [((BLOCKS, PIECE, LANES), BF16), ((PIECE, LANES), F32)],
        block_at,
        owned,
        scalars=1,
    )
    incoming = lax.all_to_all(states, GRID, 0, 0).reshape(2, CHUNK, LANES)
    (gate,) = local_call(output_gate, [((BLOCK, CHUNK), F32)], normed, w_gate, taps_q, left)
    intra, reach = local_call(
        block_attention,
        [((BLOCK, CHUNK), F32), ((BLOCK, HEAD_K), F32)],
        pre_q,
        pre_k,
        pre_v,
        edge,
        taps_q,
        taps_k,
        taps_v,
        cumulated,
        columns,
        own_rows,
        left,
        scratch=[
            pltpu.VMEM((2, BLOCK + 8, HEAD_K), F32),
            pltpu.VMEM((BLOCK + 8, CHUNK), F32),
        ],
    )
    mine, my_squares, sent = local_call(
        attend,
        [((8, BLOCK, CHUNK), F32), ((8, BLOCK), F32), ((8 * BLOCK + 8, CHUNK), BF16)],
        core_at,
        intra,
        reach,
        incoming,
        gate,
        w_out,
        scalars=1,
    )
    both = lax.all_gather(sent, "core", axis=0)
    (pairs,) = local_call(
        pair_sum, [((8, BLOCK + 8, CHUNK), BF16)], core_at, mine, my_squares, both, scalars=1
    )
    arrived = lax.all_to_all(pairs, CHIPS, 0, 0)
    (mixed,) = local_call(
        finish, [((BLOCK, CHUNK), BF16)], arrived, hidden, last=True
    )
    return mixed


def solution(mesh):
    finer = Mesh(mesh.devices.reshape(ROWS_X, ROWS_Y, 4, 2, 2), ("x", "y", "row", "zhi", "core"))
    part = ("row", "zhi", "core")
    return jax.shard_map(
        shards,
        mesh=finer,
        in_specs=(
            P(SEQ, part),
            P(),
            P(),
            P(None, "row"),
            P(None, "row"),
            P(None, part),
            P(None, part),
            P(),
            P(None, "row"),
            P("row"),
            P(None, "row"),
            P(None, "row"),
            P(None, part),
            P(("zhi", "core")),
            P(part, None),
        ),
        out_specs=P(SEQ, part),
        check_vma=False,
    )
```

```python
import jax
import jax.numpy as jnp
from jax import lax
from jax.experimental import pallas as pl
from jax.experimental.pallas import tpu as pltpu
from jax.sharding import Mesh, PartitionSpec as P

F32 = jnp.float32
BF16 = jnp.bfloat16
HIGHEST = lax.Precision.HIGHEST
HEAD_V = 512
WIDTH = 2048
BLOCK = 128
HEAD_K = 256
CHUNK = 128
LAST = (((1,), (1,)), ((), ()))
FIRST = (((0,), (0,)), ((), ()))

SEQ = ("x", "y")
GRID = ("y", "x")
CHIPS = ("row", "zhi")
ROWS_X, ROWS_Y = 4, 8
LANES = 128
BLOCKS = ROWS_X * ROWS_Y
PIECE = 2 * CHUNK // BLOCKS


def local_call(kernel, outs, *args, scratch=(), scalars=0, plain=(), anywhere=(), last=False):
    elsewhere = (*range(scalars), *plain, *anywhere)
    vmem = pl.BlockSpec(memory_space=pltpu.VMEM)
    smem = pl.BlockSpec(memory_space=pltpu.SMEM)
    args = [
        pltpu.with_memory_space_constraint(a, pltpu.HBM if i in anywhere else pltpu.VMEM)
        if i in anywhere or i not in elsewhere
        else a
        for i, a in enumerate(args)
    ]
    return pl.pallas_call(
        kernel,
        out_shape=[jax.ShapeDtypeStruct(s, t) if last else pltpu.VMEM(s, t) for s, t in outs],
        in_specs=[
            smem if i < scalars else pl.BlockSpec(memory_space=pltpu.HBM) if i in anywhere else vmem
            for i in range(len(args))
        ],
        out_specs=[vmem] * len(outs),
        scratch_shapes=list(scratch),
        name=kernel.__name__,
        compiler_params=pltpu.CompilerParams(vmem_limit_bytes=16 << 20),
    )(*args)


def dot(a, b, dims=(((1,), (0,)), ((), ())), precision=None):
    return lax.dot_general(a, b, dims, precision=precision, preferred_element_type=F32)


def halves(value):
    high = value.astype(BF16)
    return high, (value - high.astype(F32)).astype(BF16)


def pair_rows(value):
    high, low = halves(value)
    shape = (8, value.shape[1])
    index = lax.broadcasted_iota(jnp.int32, shape, 0)
    both = jnp.where(
        index == 0,
        jnp.broadcast_to(high.astype(F32), shape),
        jnp.where(index == 1, jnp.broadcast_to(low.astype(F32), shape), 0.0),
    )
    return both.astype(BF16)


def silu(value):
    return value * jax.nn.sigmoid(value)


def fetch_and_spread(index, core, *refs):
    del index, core
    *refs, copies, arrived = refs
    count = len(refs) // 2
    fetches = [
        pltpu.make_async_copy(refs[i], refs[count + i], arrived.at[i]) for i in range(count)
    ]
    for fetch in fetches:
        fetch.start()
    fetches[0].wait()
    for j in range(8):
        copies[j] = refs[count][...]
    for fetch in fetches[1:]:
        fetch.wait()


def conv(pre, edge, taps, extended, columns):
    extended[0:8, :] = jnp.zeros((8, pre.shape[1]), F32) if edge is None else edge
    extended[8:, :] = pre
    seg = columns[:, 0:1]
    total = taps[0:1, :] * pre
    for j in range(1, 4):
        same = columns[:, 8 * j : 8 * j + 1] == seg
        total = total + jnp.where(
            same, taps[j : j + 1, :] * extended[8 - j : 8 - j + BLOCK, :], 0.0
        )
    return total


def onward(pre, taps, own, following):
    sums = []
    for t in range(3):
        total = jnp.zeros((1, pre.shape[1]), F32)
        for j in range(t + 1, 4):
            at = BLOCK + t - j
            same = following[0:1, t : t + 1] == own[0:1, at : at + 1]
            total = total + jnp.where(same, taps[j : j + 1, :] * pre[at : at + 1, :], 0.0)
        sums.append(total)
    return sums


def stacked_rows(rows):
    shape = (8, LANES)
    index = lax.broadcasted_iota(jnp.int32, shape, 0)
    out = jnp.zeros(shape, F32)
    for at, row in rows.items():
        out = jnp.where(index == at, jnp.broadcast_to(row, shape), out)
    return out.astype(BF16)


def block_state(
    index,
    whole,
    gain,
    query_hbm,
    w_key,
    w_value,
    w_down,
    w_up,
    bias,
    seg_ids,
    taps_k,
    taps_v,
    pieces,
    tail,
    gained,
    row_scale,
    pre_q,
    pre_k,
    pre_v,
    cumulated,
    columns_out,
    own_rows,
    extended_k,
    extended_v,
    w_query,
    arrived,
):
    fetch = pltpu.make_async_copy(query_hbm, w_query, arrived.at[0])
    fetch.start()
    squares = jnp.zeros((BLOCK, CHUNK), F32)
    for f in range(WIDTH // CHUNK):
        lanes = slice(f * CHUNK, (f + 1) * CHUNK)
        activ = whole[f % 2, f // 2].astype(F32)
        squares = squares + activ * activ
        gained[:, lanes] = (activ * gain[:, lanes]).astype(BF16)
    scale = lax.rsqrt(jnp.sum(squares, axis=1, keepdims=True) / WIDTH + 1e-06)
    row_scale[...] = jnp.broadcast_to(scale, (BLOCK, CHUNK))
    rows = gained[...]
    rank_part = dot(rows, w_down[...], LAST) * scale

    at = index[0]
    own = seg_ids[pl.ds(at, 1), :].astype(F32)
    before = seg_ids[pl.ds(jnp.maximum(at - 1, 0), 1), :].astype(F32)
    before = jnp.where(at > 0, before, -1.0)
    following = seg_ids[pl.ds(jnp.minimum(at + 1, BLOCKS - 1), 1), :].astype(F32)
    own = jnp.broadcast_to(own, (8, BLOCK))
    before = jnp.broadcast_to(before, (8, BLOCK))
    lane = lax.broadcasted_iota(jnp.int32, (8, BLOCK), 1)
    parts = [own]
    for j in range(1, 4):
        parts.append(jnp.where(lane < j, pltpu.roll(before, j, 1), pltpu.roll(own, j, 1)))
    before = jnp.broadcast_to(before[:, BLOCK - 1 :], (8, BLOCK))
    last = jnp.broadcast_to(own[:, BLOCK - 1 :], (8, BLOCK))
    parts += [before, last]
    parts.append(jnp.zeros((BLOCK - 8 * len(parts), BLOCK), F32))
    columns = jnp.transpose(jnp.concatenate(parts, axis=0))
    columns_out[...] = columns
    own_rows[...] = own

    logits = dot(rank_part, w_up[...].astype(F32), precision=HIGHEST) + bias[...]
    log_decay = (jnp.minimum(logits, 0.0) - jnp.log(1.0 + jnp.exp(-jnp.abs(logits)))) / 16.0
    row_iota = lax.broadcasted_iota(jnp.int32, (BLOCK, BLOCK), 0)
    col_iota = lax.broadcasted_iota(jnp.int32, (BLOCK, BLOCK), 1)
    lower = jnp.where(row_iota >= col_iota, 1.0, 0.0).astype(F32)
    cum = dot(lower, log_decay, precision=HIGHEST)
    cumulated[...] = cum

    of_keys = dot(rows, w_key[...]) * scale
    of_values = dot(rows, w_value[...]) * scale
    pre_k[...] = of_keys
    pre_v[...] = of_values
    sums_k = conv(of_keys, None, taps_k, extended_k, columns)
    sums_v = conv(of_values, None, taps_v, extended_v, columns)
    next_k = onward(of_keys, taps_k, own, following)
    next_v = onward(of_values, taps_v, own, following)
    final = cum[BLOCK - 1 :, :]
    factors = jnp.where(columns[:, 0:1] == columns[:, 40:41], jnp.exp(final - cum), 0.0)
    later = lax.broadcasted_iota(jnp.int32, (BLOCK, HEAD_K), 0) >= 3
    pushed = jnp.where(later, silu(sums_k) * factors, 0.0)
    state = dot(silu(sums_v).astype(BF16), pushed.astype(BF16), FIRST)
    keep = jnp.where(before[0:1, 0:1] == last[0:1, 0:1], jnp.exp(final), 0.0)
    high, low = halves(keep)
    lane = lax.broadcasted_iota(jnp.int32, (1, LANES), 1)
    mixed_v = []
    for upper in range(2):
        mine = (lane >= LANES // 2) == (upper == 1)
        mixed_v.append(
            [
                jnp.where(mine, sums_v[t : t + 1, :], pltpu.roll(next_v[t], LANES // 2, 1))
                for t in range(3)
            ]
        )
    for h in range(2):
        lanes = slice(h * LANES, (h + 1) * LANES)
        rows_b = {0: high.astype(F32)[:, lanes], 1: low.astype(F32)[:, lanes]}
        for t in range(3):
            rows_b[2 + t] = sums_k[t : t + 1, lanes]
            rows_b[5 + t] = next_k[t][:, lanes]
        tile_b = stacked_rows(rows_b)
        for upper in range(2):
            rows_c = {2 + t: factors[t : t + 1, lanes] for t in range(3)}
            rows_c.update({5 + t: mixed_v[upper][t] for t in range(3)})
            tile_c = stacked_rows(rows_c)
            for j in range(8):
                g = 8 * upper + j
                p = h * BLOCKS // 2 + g
                pieces[p, 0:PIECE, :] = state[g * PIECE : (g + 1) * PIECE, lanes].astype(BF16)
                pieces[p, PIECE : PIECE + 8, :] = tile_b
                pieces[p, PIECE + 8 :, :] = tile_c
    fetch.wait()
    of_queries = dot(rows, w_query[...]) * scale
    pre_q[...] = of_queries
    tail[:, :HEAD_K] = of_queries[BLOCK - 8 :, :]
    tail[:, HEAD_K : 2 * HEAD_K] = of_keys[BLOCK - 8 :, :]
    tail[:, 2 * HEAD_K :] = of_values[BLOCK - 8 :, :]


def output_gate(gained, row_scale, w_gate, head_gain, left, gate):
    del left
    gate[...] = silu(dot(gained[...], w_gate[...]) * row_scale[...]) * head_gain[...]


def block_attention(
    pre_q,
    pre_k,
    pre_v,
    edge,
    taps_q,
    taps_k,
    taps_v,
    cumulated,
    columns,
    own_rows,
    left,
    intra,
    reach,
    extended,
    extended_v,
):
    del left
    edges = edge[...]
    queries = silu(conv(pre_q[...], edges[:, :HEAD_K], taps_q, extended.at[0], columns))
    queries = queries * HEAD_K ** (-0.5)
    keys = silu(
        conv(pre_k[...], edges[:, HEAD_K : 2 * HEAD_K], taps_k, extended.at[1], columns)
    )
    values = silu(conv(pre_v[...], edges[:, 2 * HEAD_K :], taps_v, extended_v, columns))
    cum, seg = cumulated[...], columns[:, 0:1]
    row_iota = lax.broadcasted_iota(jnp.int32, (BLOCK, BLOCK), 0)
    col_iota = lax.broadcasted_iota(jnp.int32, (BLOCK, BLOCK), 1)
    reach[...] = jnp.where(seg == columns[:, 32:33], queries * jnp.exp(cum), 0.0)
    weights = jnp.zeros((BLOCK, BLOCK), F32)
    for half in (8, 16, 32, 64):
        anchors = [
            jnp.broadcast_to(cum[b + half - 1 : b + half, :], (2 * half, HEAD_K))
            for b in range(0, BLOCK, 2 * half)
        ]
        anchor = jnp.concatenate(anchors, axis=0) if len(anchors) > 1 else anchors[0]
        factor = jnp.exp(-jnp.abs(cum - anchor))
        part = dot((queries * factor).astype(BF16), (keys * factor).astype(BF16), LAST)
        inside = (
            (row_iota // (2 * half) == col_iota // (2 * half))
            & (row_iota % (2 * half) >= half)
            & (col_iota % (2 * half) < half)
        )
        weights = jnp.where(inside, part, weights)
    groups = (BLOCK // 8, 8, HEAD_K)
    cum_g, keys_g = cum.reshape(groups), keys.reshape(groups)
    queries_g = queries.reshape(groups)
    for by in range(8):
        if by:
            spread = jnp.minimum(cum_g - pltpu.roll(cum_g, by, 1), 0.0)
            product = queries_g * pltpu.roll(keys_g, by, 1) * jnp.exp(spread)
        else:
            product = queries_g * keys_g
        sums = jnp.sum(product.reshape(BLOCK, HEAD_K), axis=1, keepdims=True)
        inside = (row_iota - col_iota == by) & (row_iota % 8 >= by)
        weights = jnp.where(inside, sums, weights)
    visible = (seg == own_rows[0:1, :]) & (row_iota >= col_iota)
    weights = jnp.where(visible, weights, 0.0)
    intra[...] = dot(weights.astype(BF16), values.astype(BF16))


def scan_blocks(index, pieces, states, left):
    owner = (index[0] % ROWS_Y) * ROWS_X + index[0] // ROWS_Y
    first = (owner % (BLOCKS // 2)) * PIECE
    order = [(block % ROWS_Y) * ROWS_X + block // ROWS_Y for block in range(BLOCKS)]
    shape = (BLOCKS, 8, LANES)
    tiles_b = jnp.stack([pieces[at, PIECE : PIECE + 8, :].astype(F32) for at in order])
    tiles_c = jnp.stack([pieces[at, PIECE + 8 :, :].astype(F32) for at in order])
    nothing = jnp.zeros((1, 8, LANES), F32)
    back_b = jnp.concatenate([nothing, tiles_b[:-1]], axis=0)
    back_c = jnp.concatenate([nothing, tiles_c[:-1]], axis=0)
    pushed = silu(tiles_b + pltpu.roll(back_b, 5, 1)) * tiles_c
    values = pltpu.roll(silu(tiles_c + pltpu.roll(back_c, LANES // 2, 2)), 5, 1)
    row = lax.broadcasted_iota(jnp.int32, shape, 1)
    values = jnp.where((row >= 2) & (row < 5), values, 0.0)
    rows = BLOCKS * 8
    lane = lax.broadcasted_iota(jnp.int32, (PIECE, LANES), 1)
    chosen = lane == lax.broadcasted_iota(jnp.int32, (PIECE, LANES), 0) + first
    chosen = jnp.where(chosen, 1.0, 0.0).astype(BF16)
    mine = dot(chosen, values.reshape(rows, LANES).astype(BF16), LAST)
    same = lax.broadcasted_iota(jnp.int32, (rows, rows), 0) // 8
    same = same == lax.broadcasted_iota(jnp.int32, (rows, rows), 1) // 8
    spread = jnp.where(same, jnp.concatenate([mine] * BLOCKS, axis=0), 0.0)
    added = dot(spread.astype(BF16), pushed.reshape(rows, LANES).astype(BF16))
    state = jnp.zeros((PIECE, LANES), F32)
    for block, at in enumerate(order):
        states[at] = state.astype(BF16)
        decay = tiles_b[block, 0:1, :] + tiles_b[block, 1:2, :]
        own = pieces[at, 0:PIECE, :].astype(F32) + added[block * 8 : block * 8 + 8, :]
        state = state * decay + own
    left[...] = state


def attend(index, intra, reach, incoming, gate, w_out, kept, kept_squares, sent):
    high, low = halves(reach[...])
    state = jnp.concatenate([incoming[0], incoming[1]], axis=1)
    attended = intra[...] + dot(high, state, LAST) + dot(low, state, LAST)
    squares = dot(jnp.ones((8, CHUNK), F32), attended * attended, LAST, precision=HIGHEST)
    terms = dot((attended * gate[...]).astype(BF16), w_out[...])
    first = index[0] == 0
    for j in range(8):
        even = terms[:, (2 * j) * CHUNK : (2 * j + 1) * CHUNK]
        odd = terms[:, (2 * j + 1) * CHUNK : (2 * j + 2) * CHUNK]
        kept[j] = jnp.where(first, even, odd)
        sent[j * BLOCK : (j + 1) * BLOCK, :] = jnp.where(first, odd, even).astype(BF16)
    kept_squares[...] = squares
    sent[8 * BLOCK :, :] = pair_rows(squares[0:1, :])


def pair_sum(index, kept, kept_squares, both, sent):
    received = both.at[1 - index[0]]
    other = received[8 * BLOCK :, :].astype(F32)
    squares = pair_rows(kept_squares[0:1, :] + other[0:1, :] + other[1:2, :])
    for j in range(8):
        terms = kept[j] + received[j * BLOCK : (j + 1) * BLOCK, :].astype(F32)
        sent[j, 0:BLOCK, :] = terms.astype(BF16)
        sent[j, BLOCK:, :] = squares


def finish(received, hidden, mixed):
    parts = []
    for r in range(4):
        pair = received[2 * r, BLOCK:, :].astype(F32) + received[2 * r + 1, BLOCK:, :].astype(F32)
        squares = pair[0:1, :] + pair[1:2, :]
        scale = lax.rsqrt(squares / HEAD_V + 1e-05)
        parts.append(jnp.broadcast_to(scale, (8, BLOCK)))
    parts.append(jnp.zeros((BLOCK - 8 * len(parts), BLOCK), F32))
    columns = jnp.transpose(jnp.concatenate(parts, axis=0))
    total = hidden[...].astype(F32)
    for r in range(4):
        terms = received[2 * r, 0:BLOCK, :].astype(F32)
        terms = terms + received[2 * r + 1, 0:BLOCK, :].astype(F32)
        total = total + columns[:, 8 * r : 8 * r + 1] * terms
    mixed[...] = total.astype(BF16)


def shards(
    hidden_in,
    seg_ids,
    norm_gain,
    w_query,
    w_key,
    w_value,
    w_gate,
    w_decay_down,
    w_decay_up,
    decay_bias,
    conv_query,
    conv_key,
    conv_value,
    head_gain,
    w_out,
):
    block = lax.axis_index("x") * ROWS_Y + lax.axis_index("y")
    block_at = jnp.reshape(block, (1,)).astype(jnp.int32)
    core_at = jnp.reshape(lax.axis_index("core"), (1,)).astype(jnp.int32)

    needed = (
        hidden_in,
        norm_gain.reshape(1, WIDTH),
        w_decay_down.T,
        w_decay_up,
        decay_bias.reshape(1, HEAD_K),
        seg_ids.reshape(BLOCKS, BLOCK),
        conv_query,
        conv_key,
        conv_value,
        w_value,
    )
    hidden, gain, down, up, bias, segs, taps_q, taps_k, taps_v, value_here, copies = local_call(
        fetch_and_spread,
        [*((a.shape, a.dtype) for a in needed), ((8, BLOCK, CHUNK), BF16)],
        block_at,
        core_at,
        *needed,
        scratch=[pltpu.SemaphoreType.DMA((len(needed),))],
        scalars=2,
        anywhere=range(2, 2 + len(needed)),
    )
    of_core = lax.all_to_all(copies, CHIPS, 0, 0)
    whole = lax.all_gather(of_core, "core", axis=0)
    pieces, tail, gained, row_scale, pre_q, pre_k, pre_v, cumulated, columns, own_rows = local_call(
        block_state,
        [
            ((BLOCKS, PIECE + 16, LANES), BF16),
            ((8, 2 * HEAD_K + CHUNK), F32),
            ((BLOCK, WIDTH), BF16),
            ((BLOCK, CHUNK), F32),
            ((BLOCK, HEAD_K), F32),
            ((BLOCK, HEAD_K), F32),
            ((BLOCK, CHUNK), F32),
            ((BLOCK, HEAD_K), F32),
            ((BLOCK, BLOCK), F32),
            ((8, BLOCK), F32),
        ],
        block_at,
        whole,
        gain,
        w_query,
        w_key,
        value_here,
        down,
        up,
        bias,
        segs,
        taps_k,
        taps_v,
        scratch=[
            pltpu.VMEM((BLOCK + 8, HEAD_K), F32),
            pltpu.VMEM((BLOCK + 8, CHUNK), F32),
            pltpu.VMEM((WIDTH, HEAD_K), BF16),
            pltpu.SemaphoreType.DMA((1,)),
        ],
        scalars=1,
        anywhere=(3,),
    )
    edge = lax.ppermute(tail, SEQ, [(i, i + 1) for i in range(BLOCKS - 1)])
    owned = lax.all_to_all(pieces, GRID, 0, 0)
    states, left = local_call(
        scan_blocks,
        [((BLOCKS, PIECE, LANES), BF16), ((PIECE, LANES), F32)],
        block_at,
        owned,
        scalars=1,
    )
    incoming = lax.all_to_all(states, GRID, 0, 0).reshape(2, CHUNK, LANES)
    (gate,) = local_call(
        output_gate,
        [((BLOCK, CHUNK), F32)],
        gained,
        row_scale,
        w_gate,
        head_gain.reshape(1, CHUNK),
        left,
    )
    intra, reach = local_call(
        block_attention,
        [((BLOCK, CHUNK), F32), ((BLOCK, HEAD_K), F32)],
        pre_q,
        pre_k,
        pre_v,
        edge,
        taps_q,
        taps_k,
        taps_v,
        cumulated,
        columns,
        own_rows,
        left,
        scratch=[
            pltpu.VMEM((2, BLOCK + 8, HEAD_K), F32),
            pltpu.VMEM((BLOCK + 8, CHUNK), F32),
        ],
    )
    mine, my_squares, sent = local_call(
        attend,
        [((8, BLOCK, CHUNK), F32), ((8, BLOCK), F32), ((8 * BLOCK + 8, CHUNK), BF16)],
        core_at,
        intra,
        reach,
        incoming,
        gate,
        w_out,
        scalars=1,
    )
    both = lax.all_gather(sent, "core", axis=0)
    (pairs,) = local_call(
        pair_sum, [((8, BLOCK + 8, CHUNK), BF16)], core_at, mine, my_squares, both, scalars=1
    )
    arrived = lax.all_to_all(pairs, CHIPS, 0, 0)
    (mixed,) = local_call(
        finish, [((BLOCK, CHUNK), BF16)], arrived, hidden, last=True
    )
    return mixed


def solution(mesh):
    finer = Mesh(mesh.devices.reshape(ROWS_X, ROWS_Y, 4, 2, 2), ("x", "y", "row", "zhi", "core"))
    part = ("row", "zhi", "core")
    return jax.shard_map(
        shards,
        mesh=finer,
        in_specs=(
            P(SEQ, part),
            P(),
            P(),
            P(None, "row"),
            P(None, "row"),
            P(None, part),
            P(None, part),
            P(),
            P(None, "row"),
            P("row"),
            P(None, "row"),
            P(None, "row"),
            P(None, part),
            P(("zhi", "core")),
            P(part, None),
        ),
        out_specs=P(SEQ, part),
        check_vma=False,
    )
```

```python
import jax
import jax.numpy as jnp
from jax import lax
from jax.experimental import pallas as pl
from jax.experimental.pallas import tpu as pltpu
from jax.sharding import Mesh, PartitionSpec as P

F32 = jnp.float32
BF16 = jnp.bfloat16
HIGHEST = lax.Precision.HIGHEST
HEAD_V = 512
WIDTH = 2048
BLOCK = 128
HEAD_K = 256
CHUNK = 128
LAST = (((1,), (1,)), ((), ()))
FIRST = (((0,), (0,)), ((), ()))

SEQ = ("x", "y")
GRID = ("y", "x")
CHIPS = ("row", "zhi")
ROWS_X, ROWS_Y = 4, 8
LANES = 128
BLOCKS = ROWS_X * ROWS_Y
PIECE = 2 * CHUNK // BLOCKS


def local_call(kernel, outs, *args, scratch=(), scalars=0, plain=(), anywhere=(), last=False):
    elsewhere = (*range(scalars), *plain, *anywhere)
    vmem = pl.BlockSpec(memory_space=pltpu.VMEM)
    smem = pl.BlockSpec(memory_space=pltpu.SMEM)
    args = [
        pltpu.with_memory_space_constraint(a, pltpu.HBM if i in anywhere else pltpu.VMEM)
        if i in anywhere or i not in elsewhere
        else a
        for i, a in enumerate(args)
    ]
    return pl.pallas_call(
        kernel,
        out_shape=[jax.ShapeDtypeStruct(s, t) if last else pltpu.VMEM(s, t) for s, t in outs],
        in_specs=[
            smem if i < scalars else pl.BlockSpec(memory_space=pltpu.HBM) if i in anywhere else vmem
            for i in range(len(args))
        ],
        out_specs=[vmem] * len(outs),
        scratch_shapes=list(scratch),
        name=kernel.__name__,
        compiler_params=pltpu.CompilerParams(vmem_limit_bytes=16 << 20),
    )(*args)


def dot(a, b, dims=(((1,), (0,)), ((), ())), precision=None):
    return lax.dot_general(a, b, dims, precision=precision, preferred_element_type=F32)


def halves(value):
    high = value.astype(BF16)
    return high, (value - high.astype(F32)).astype(BF16)


def pair_rows(value):
    high, low = halves(value)
    shape = (8, value.shape[1])
    index = lax.broadcasted_iota(jnp.int32, shape, 0)
    both = jnp.where(
        index == 0,
        jnp.broadcast_to(high.astype(F32), shape),
        jnp.where(index == 1, jnp.broadcast_to(low.astype(F32), shape), 0.0),
    )
    return both.astype(BF16)


def silu(value):
    return value * jax.nn.sigmoid(value)


def fetch_and_spread(index, core, *refs):
    del index, core
    *refs, copies, arrived = refs
    count = len(refs) // 2
    fetches = [
        pltpu.make_async_copy(refs[i], refs[count + i], arrived.at[i]) for i in range(count)
    ]
    for fetch in fetches:
        fetch.start()
    fetches[0].wait()
    for j in range(8):
        copies[j, 0:BLOCK, :] = refs[count][...]
        copies[j, BLOCK:, :] = jnp.zeros((8, CHUNK), BF16)
    for fetch in fetches[1:]:
        fetch.wait()


def conv(pre, edge, taps, extended, columns):
    extended[0:8, :] = jnp.zeros((8, pre.shape[1]), F32) if edge is None else edge
    extended[8:, :] = pre
    seg = columns[:, 0:1]
    total = taps[0:1, :] * pre
    for j in range(1, 4):
        same = columns[:, 8 * j : 8 * j + 1] == seg
        total = total + jnp.where(
            same, taps[j : j + 1, :] * extended[8 - j : 8 - j + BLOCK, :], 0.0
        )
    return total


def onward(pre, taps, own, following):
    sums = []
    for t in range(3):
        total = jnp.zeros((1, pre.shape[1]), F32)
        for j in range(t + 1, 4):
            at = BLOCK + t - j
            same = following[0:1, t : t + 1] == own[0:1, at : at + 1]
            total = total + jnp.where(same, taps[j : j + 1, :] * pre[at : at + 1, :], 0.0)
        sums.append(total)
    return sums


def stacked_rows(rows):
    shape = (8, LANES)
    index = lax.broadcasted_iota(jnp.int32, shape, 0)
    out = jnp.zeros(shape, F32)
    for at, row in rows.items():
        out = jnp.where(index == at, jnp.broadcast_to(row, shape), out)
    return out.astype(BF16)


def block_state(
    index,
    whole,
    gain,
    query_hbm,
    w_key,
    w_value,
    w_down,
    w_up,
    bias,
    seg_ids,
    taps_k,
    taps_v,
    pieces,
    tail,
    gained,
    row_scale,
    pre_q,
    pre_k,
    pre_v,
    cumulated,
    columns_out,
    own_rows,
    extended_k,
    extended_v,
    w_query,
    arrived,
):
    fetch = pltpu.make_async_copy(query_hbm, w_query, arrived.at[0])
    fetch.start()
    squares = jnp.zeros((BLOCK, CHUNK), F32)
    for f in range(WIDTH // CHUNK):
        lanes = slice(f * CHUNK, (f + 1) * CHUNK)
        activ = whole[f % 2, f // 2, 0:BLOCK, :].astype(F32)
        squares = squares + activ * activ
        gained[:, lanes] = (activ * gain[:, lanes]).astype(BF16)
    scale = lax.rsqrt(jnp.sum(squares, axis=1, keepdims=True) / WIDTH + 1e-06)
    row_scale[...] = jnp.broadcast_to(scale, (BLOCK, CHUNK))
    rows = gained[...]
    rank_part = dot(rows, w_down[...], LAST) * scale

    at = index[0]
    own = seg_ids[pl.ds(at, 1), :].astype(F32)
    before = seg_ids[pl.ds(jnp.maximum(at - 1, 0), 1), :].astype(F32)
    before = jnp.where(at > 0, before, -1.0)
    following = seg_ids[pl.ds(jnp.minimum(at + 1, BLOCKS - 1), 1), :].astype(F32)
    own = jnp.broadcast_to(own, (8, BLOCK))
    before = jnp.broadcast_to(before, (8, BLOCK))
    lane = lax.broadcasted_iota(jnp.int32, (8, BLOCK), 1)
    parts = [own]
    for j in range(1, 4):
        parts.append(jnp.where(lane < j, pltpu.roll(before, j, 1), pltpu.roll(own, j, 1)))
    before = jnp.broadcast_to(before[:, BLOCK - 1 :], (8, BLOCK))
    last = jnp.broadcast_to(own[:, BLOCK - 1 :], (8, BLOCK))
    parts += [before, last]
    parts.append(jnp.zeros((BLOCK - 8 * len(parts), BLOCK), F32))
    columns = jnp.transpose(jnp.concatenate(parts, axis=0))
    columns_out[...] = columns
    own_rows[...] = own

    logits = dot(rank_part, w_up[...].astype(F32), precision=HIGHEST) + bias[...]
    log_decay = (jnp.minimum(logits, 0.0) - jnp.log(1.0 + jnp.exp(-jnp.abs(logits)))) / 16.0
    row_iota = lax.broadcasted_iota(jnp.int32, (BLOCK, BLOCK), 0)
    col_iota = lax.broadcasted_iota(jnp.int32, (BLOCK, BLOCK), 1)
    lower = jnp.where(row_iota >= col_iota, 1.0, 0.0).astype(F32)
    cum = dot(lower, log_decay, precision=HIGHEST)
    cumulated[...] = cum

    of_keys = dot(rows, w_key[...]) * scale
    of_values = dot(rows, w_value[...]) * scale
    pre_k[...] = of_keys
    pre_v[...] = of_values
    sums_k = conv(of_keys, None, taps_k, extended_k, columns)
    sums_v = conv(of_values, None, taps_v, extended_v, columns)
    next_k = onward(of_keys, taps_k, own, following)
    next_v = onward(of_values, taps_v, own, following)
    final = cum[BLOCK - 1 :, :]
    factors = jnp.where(columns[:, 0:1] == columns[:, 40:41], jnp.exp(final - cum), 0.0)
    later = lax.broadcasted_iota(jnp.int32, (BLOCK, HEAD_K), 0) >= 3
    pushed = jnp.where(later, silu(sums_k) * factors, 0.0)
    state = dot(silu(sums_v).astype(BF16), pushed.astype(BF16), FIRST)
    keep = jnp.where(before[0:1, 0:1] == last[0:1, 0:1], jnp.exp(final), 0.0)
    high, low = halves(keep)
    lane = lax.broadcasted_iota(jnp.int32, (1, LANES), 1)
    mixed_v = []
    for upper in range(2):
        mine = (lane >= LANES // 2) == (upper == 1)
        mixed_v.append(
            [
                jnp.where(mine, sums_v[t : t + 1, :], pltpu.roll(next_v[t], LANES // 2, 1))
                for t in range(3)
            ]
        )
    for h in range(2):
        lanes = slice(h * LANES, (h + 1) * LANES)
        rows_b = {0: high.astype(F32)[:, lanes], 1: low.astype(F32)[:, lanes]}
        for t in range(3):
            rows_b[2 + t] = sums_k[t : t + 1, lanes]
            rows_b[5 + t] = next_k[t][:, lanes]
        tile_b = stacked_rows(rows_b)
        for upper in range(2):
            rows_c = {2 + t: factors[t : t + 1, lanes] for t in range(3)}
            rows_c.update({5 + t: mixed_v[upper][t] for t in range(3)})
            tile_c = stacked_rows(rows_c)
            for j in range(8):
                g = 8 * upper + j
                p = h * BLOCKS // 2 + g
                pieces[p, 0:PIECE, :] = state[g * PIECE : (g + 1) * PIECE, lanes].astype(BF16)
                pieces[p, PIECE : PIECE + 8, :] = tile_b
                pieces[p, PIECE + 8 :, :] = tile_c
    fetch.wait()
    of_queries = dot(rows, w_query[...]) * scale
    pre_q[...] = of_queries
    tail[:, :HEAD_K] = of_queries[BLOCK - 8 :, :]
    tail[:, HEAD_K : 2 * HEAD_K] = of_keys[BLOCK - 8 :, :]
    tail[:, 2 * HEAD_K :] = of_values[BLOCK - 8 :, :]


def output_gate(gained, row_scale, w_gate, head_gain, left, gate):
    del left
    gate[...] = silu(dot(gained[...], w_gate[...]) * row_scale[...]) * head_gain[...]


def block_attention(
    pre_q,
    pre_k,
    pre_v,
    edge,
    taps_q,
    taps_k,
    taps_v,
    cumulated,
    columns,
    own_rows,
    left,
    intra,
    reach,
    extended,
    extended_v,
):
    del left
    edges = edge[...]
    queries = silu(conv(pre_q[...], edges[:, :HEAD_K], taps_q, extended.at[0], columns))
    queries = queries * HEAD_K ** (-0.5)
    keys = silu(
        conv(pre_k[...], edges[:, HEAD_K : 2 * HEAD_K], taps_k, extended.at[1], columns)
    )
    values = silu(conv(pre_v[...], edges[:, 2 * HEAD_K :], taps_v, extended_v, columns))
    cum, seg = cumulated[...], columns[:, 0:1]
    row_iota = lax.broadcasted_iota(jnp.int32, (BLOCK, BLOCK), 0)
    col_iota = lax.broadcasted_iota(jnp.int32, (BLOCK, BLOCK), 1)
    reach[...] = jnp.where(seg == columns[:, 32:33], queries * jnp.exp(cum), 0.0)
    weights = jnp.zeros((BLOCK, BLOCK), F32)
    for half in (8, 16, 32, 64):
        anchors = [
            jnp.broadcast_to(cum[b + half - 1 : b + half, :], (2 * half, HEAD_K))
            for b in range(0, BLOCK, 2 * half)
        ]
        anchor = jnp.concatenate(anchors, axis=0) if len(anchors) > 1 else anchors[0]
        factor = jnp.exp(-jnp.abs(cum - anchor))
        part = dot((queries * factor).astype(BF16), (keys * factor).astype(BF16), LAST)
        inside = (
            (row_iota // (2 * half) == col_iota // (2 * half))
            & (row_iota % (2 * half) >= half)
            & (col_iota % (2 * half) < half)
        )
        weights = jnp.where(inside, part, weights)
    groups = (BLOCK // 8, 8, HEAD_K)
    cum_g, keys_g = cum.reshape(groups), keys.reshape(groups)
    queries_g = queries.reshape(groups)
    for by in range(8):
        if by:
            spread = jnp.minimum(cum_g - pltpu.roll(cum_g, by, 1), 0.0)
            product = queries_g * pltpu.roll(keys_g, by, 1) * jnp.exp(spread)
        else:
            product = queries_g * keys_g
        sums = jnp.sum(product.reshape(BLOCK, HEAD_K), axis=1, keepdims=True)
        inside = (row_iota - col_iota == by) & (row_iota % 8 >= by)
        weights = jnp.where(inside, sums, weights)
    visible = (seg == own_rows[0:1, :]) & (row_iota >= col_iota)
    weights = jnp.where(visible, weights, 0.0)
    intra[...] = dot(weights.astype(BF16), values.astype(BF16))


def scan_blocks(index, pieces, states, left):
    owner = (index[0] % ROWS_Y) * ROWS_X + index[0] // ROWS_Y
    first = (owner % (BLOCKS // 2)) * PIECE
    order = [(block % ROWS_Y) * ROWS_X + block // ROWS_Y for block in range(BLOCKS)]
    shape = (BLOCKS, 8, LANES)
    tiles_b = jnp.stack([pieces[at, PIECE : PIECE + 8, :].astype(F32) for at in order])
    tiles_c = jnp.stack([pieces[at, PIECE + 8 :, :].astype(F32) for at in order])
    nothing = jnp.zeros((1, 8, LANES), F32)
    back_b = jnp.concatenate([nothing, tiles_b[:-1]], axis=0)
    back_c = jnp.concatenate([nothing, tiles_c[:-1]], axis=0)
    pushed = silu(tiles_b + pltpu.roll(back_b, 5, 1)) * tiles_c
    values = pltpu.roll(silu(tiles_c + pltpu.roll(back_c, LANES // 2, 2)), 5, 1)
    row = lax.broadcasted_iota(jnp.int32, shape, 1)
    values = jnp.where((row >= 2) & (row < 5), values, 0.0)
    rows = BLOCKS * 8
    lane = lax.broadcasted_iota(jnp.int32, (PIECE, LANES), 1)
    chosen = lane == lax.broadcasted_iota(jnp.int32, (PIECE, LANES), 0) + first
    chosen = jnp.where(chosen, 1.0, 0.0).astype(BF16)
    mine = dot(chosen, values.reshape(rows, LANES).astype(BF16), LAST)
    same = lax.broadcasted_iota(jnp.int32, (rows, rows), 0) // 8
    same = same == lax.broadcasted_iota(jnp.int32, (rows, rows), 1) // 8
    spread = jnp.where(same, jnp.concatenate([mine] * BLOCKS, axis=0), 0.0)
    added = dot(spread.astype(BF16), pushed.reshape(rows, LANES).astype(BF16))
    state = jnp.zeros((PIECE, LANES), F32)
    for block, at in enumerate(order):
        states[at] = state.astype(BF16)
        decay = tiles_b[block, 0:1, :] + tiles_b[block, 1:2, :]
        own = pieces[at, 0:PIECE, :].astype(F32) + added[block * 8 : block * 8 + 8, :]
        state = state * decay + own
    left[...] = state


def attend(index, intra, reach, incoming, gate, w_out, kept, kept_squares, sent):
    high, low = halves(reach[...])
    state = jnp.concatenate([incoming[0], incoming[1]], axis=1)
    attended = intra[...] + dot(high, state, LAST) + dot(low, state, LAST)
    squares = dot(jnp.ones((8, CHUNK), F32), attended * attended, LAST, precision=HIGHEST)
    terms = dot((attended * gate[...]).astype(BF16), w_out[...])
    first = index[0] == 0
    for j in range(8):
        even = terms[:, (2 * j) * CHUNK : (2 * j + 1) * CHUNK]
        odd = terms[:, (2 * j + 1) * CHUNK : (2 * j + 2) * CHUNK]
        kept[j] = jnp.where(first, even, odd)
        sent[j * BLOCK : (j + 1) * BLOCK, :] = jnp.where(first, odd, even).astype(BF16)
    kept_squares[...] = squares
    sent[8 * BLOCK :, :] = pair_rows(squares[0:1, :])


def pair_sum(index, kept, kept_squares, both, sent):
    received = both.at[1 - index[0]]
    other = received[8 * BLOCK :, :].astype(F32)
    squares = pair_rows(kept_squares[0:1, :] + other[0:1, :] + other[1:2, :])
    for j in range(8):
        terms = kept[j] + received[j * BLOCK : (j + 1) * BLOCK, :].astype(F32)
        sent[j, 0:BLOCK, :] = terms.astype(BF16)
        sent[j, BLOCK:, :] = squares


def finish(received, hidden, mixed):
    parts = []
    for r in range(4):
        pair = received[2 * r, BLOCK:, :].astype(F32) + received[2 * r + 1, BLOCK:, :].astype(F32)
        squares = pair[0:1, :] + pair[1:2, :]
        scale = lax.rsqrt(squares / HEAD_V + 1e-05)
        parts.append(jnp.broadcast_to(scale, (8, BLOCK)))
    parts.append(jnp.zeros((BLOCK - 8 * len(parts), BLOCK), F32))
    columns = jnp.transpose(jnp.concatenate(parts, axis=0))
    total = hidden[...].astype(F32)
    for r in range(4):
        terms = received[2 * r, 0:BLOCK, :].astype(F32)
        terms = terms + received[2 * r + 1, 0:BLOCK, :].astype(F32)
        total = total + columns[:, 8 * r : 8 * r + 1] * terms
    mixed[...] = total.astype(BF16)


def shards(
    hidden_in,
    seg_ids,
    norm_gain,
    w_query,
    w_key,
    w_value,
    w_gate,
    w_decay_down,
    w_decay_up,
    decay_bias,
    conv_query,
    conv_key,
    conv_value,
    head_gain,
    w_out,
):
    block = lax.axis_index("x") * ROWS_Y + lax.axis_index("y")
    block_at = jnp.reshape(block, (1,)).astype(jnp.int32)
    core_at = jnp.reshape(lax.axis_index("core"), (1,)).astype(jnp.int32)

    needed = (
        hidden_in,
        norm_gain.reshape(1, WIDTH),
        w_decay_down.T,
        w_decay_up,
        decay_bias.reshape(1, HEAD_K),
        seg_ids.reshape(BLOCKS, BLOCK),
        conv_query,
        conv_key,
        conv_value,
        w_value,
    )
    hidden, gain, down, up, bias, segs, taps_q, taps_k, taps_v, value_here, copies = local_call(
        fetch_and_spread,
        [*((a.shape, a.dtype) for a in needed), ((8, BLOCK + 8, CHUNK), BF16)],
        block_at,
        core_at,
        *needed,
        scratch=[pltpu.SemaphoreType.DMA((len(needed),))],
        scalars=2,
        anywhere=range(2, 2 + len(needed)),
    )
    of_core = lax.all_to_all(copies, CHIPS, 0, 0)
    whole = lax.all_gather(of_core, "core", axis=0)
    pieces, tail, gained, row_scale, pre_q, pre_k, pre_v, cumulated, columns, own_rows = local_call(
        block_state,
        [
            ((BLOCKS, PIECE + 16, LANES), BF16),
            ((8, 2 * HEAD_K + CHUNK), F32),
            ((BLOCK, WIDTH), BF16),
            ((BLOCK, CHUNK), F32),
            ((BLOCK, HEAD_K), F32),
            ((BLOCK, HEAD_K), F32),
            ((BLOCK, CHUNK), F32),
            ((BLOCK, HEAD_K), F32),
            ((BLOCK, BLOCK), F32),
            ((8, BLOCK), F32),
        ],
        block_at,
        whole,
        gain,
        w_query,
        w_key,
        value_here,
        down,
        up,
        bias,
        segs,
        taps_k,
        taps_v,
        scratch=[
            pltpu.VMEM((BLOCK + 8, HEAD_K), F32),
            pltpu.VMEM((BLOCK + 8, CHUNK), F32),
            pltpu.VMEM((WIDTH, HEAD_K), BF16),
            pltpu.SemaphoreType.DMA((1,)),
        ],
        scalars=1,
        anywhere=(3,),
    )
    edge = lax.ppermute(tail, SEQ, [(i, i + 1) for i in range(BLOCKS - 1)])
    owned = lax.all_to_all(pieces, GRID, 0, 0)
    states, left = local_call(
        scan_blocks,
        [((BLOCKS, PIECE, LANES), BF16), ((PIECE, LANES), F32)],
        block_at,
        owned,
        scalars=1,
    )
    incoming = lax.all_to_all(states, GRID, 0, 0).reshape(2, CHUNK, LANES)
    (gate,) = local_call(
        output_gate,
        [((BLOCK, CHUNK), F32)],
        gained,
        row_scale,
        w_gate,
        head_gain.reshape(1, CHUNK),
        left,
    )
    intra, reach = local_call(
        block_attention,
        [((BLOCK, CHUNK), F32), ((BLOCK, HEAD_K), F32)],
        pre_q,
        pre_k,
        pre_v,
        edge,
        taps_q,
        taps_k,
        taps_v,
        cumulated,
        columns,
        own_rows,
        left,
        scratch=[
            pltpu.VMEM((2, BLOCK + 8, HEAD_K), F32),
            pltpu.VMEM((BLOCK + 8, CHUNK), F32),
        ],
    )
    mine, my_squares, sent = local_call(
        attend,
        [((8, BLOCK, CHUNK), F32), ((8, BLOCK), F32), ((8 * BLOCK + 8, CHUNK), BF16)],
        core_at,
        intra,
        reach,
        incoming,
        gate,
        w_out,
        scalars=1,
    )
    both = lax.all_gather(sent, "core", axis=0)
    (pairs,) = local_call(
        pair_sum, [((8, BLOCK + 8, CHUNK), BF16)], core_at, mine, my_squares, both, scalars=1
    )
    arrived = lax.all_to_all(pairs, CHIPS, 0, 0)
    (mixed,) = local_call(
        finish, [((BLOCK, CHUNK), BF16)], arrived, hidden, last=True
    )
    return mixed


def solution(mesh):
    finer = Mesh(mesh.devices.reshape(ROWS_X, ROWS_Y, 4, 2, 2), ("x", "y", "row", "zhi", "core"))
    part = ("row", "zhi", "core")
    return jax.shard_map(
        shards,
        mesh=finer,
        in_specs=(
            P(SEQ, part),
            P(),
            P(),
            P(None, "row"),
            P(None, "row"),
            P(None, part),
            P(None, part),
            P(),
            P(None, "row"),
            P("row"),
            P(None, "row"),
            P(None, "row"),
            P(None, part),
            P(("zhi", "core")),
            P(part, None),
        ),
        out_specs=P(SEQ, part),
        check_vma=False,
    )
```

```python
import jax
import jax.numpy as jnp
from jax import lax
from jax.experimental import pallas as pl
from jax.experimental.pallas import tpu as pltpu
from jax.sharding import Mesh, PartitionSpec as P

F32 = jnp.float32
BF16 = jnp.bfloat16
HIGHEST = lax.Precision.HIGHEST
HEAD_V = 512
WIDTH = 2048
BLOCK = 128
HEAD_K = 256
CHUNK = 128
LAST = (((1,), (1,)), ((), ()))
FIRST = (((0,), (0,)), ((), ()))

SEQ = ("x", "y")
GRID = ("y", "x")
CHIPS = ("row", "zhi")
ROWS_X, ROWS_Y = 4, 8
LANES = 128
BLOCKS = ROWS_X * ROWS_Y
PIECE = 2 * CHUNK // BLOCKS


def local_call(kernel, outs, *args, scratch=(), scalars=0, plain=(), anywhere=(), last=False):
    elsewhere = (*range(scalars), *plain, *anywhere)
    vmem = pl.BlockSpec(memory_space=pltpu.VMEM)
    smem = pl.BlockSpec(memory_space=pltpu.SMEM)
    args = [
        pltpu.with_memory_space_constraint(a, pltpu.HBM if i in anywhere else pltpu.VMEM)
        if i in anywhere or i not in elsewhere
        else a
        for i, a in enumerate(args)
    ]
    return pl.pallas_call(
        kernel,
        out_shape=[jax.ShapeDtypeStruct(s, t) if last else pltpu.VMEM(s, t) for s, t in outs],
        in_specs=[
            smem if i < scalars else pl.BlockSpec(memory_space=pltpu.HBM) if i in anywhere else vmem
            for i in range(len(args))
        ],
        out_specs=[vmem] * len(outs),
        scratch_shapes=list(scratch),
        name=kernel.__name__,
        compiler_params=pltpu.CompilerParams(vmem_limit_bytes=16 << 20),
    )(*args)


def dot(a, b, dims=(((1,), (0,)), ((), ())), precision=None):
    return lax.dot_general(a, b, dims, precision=precision, preferred_element_type=F32)


def halves(value):
    high = value.astype(BF16)
    return high, (value - high.astype(F32)).astype(BF16)


def pair_rows(value):
    high, low = halves(value)
    shape = (8, value.shape[1])
    index = lax.broadcasted_iota(jnp.int32, shape, 0)
    both = jnp.where(
        index == 0,
        jnp.broadcast_to(high.astype(F32), shape),
        jnp.where(index == 1, jnp.broadcast_to(low.astype(F32), shape), 0.0),
    )
    return both.astype(BF16)


def silu(value):
    return value * jax.nn.sigmoid(value)


def fetch_and_spread(index, core, *refs):
    del index, core
    *refs, copies, arrived = refs
    count = len(refs) // 2
    fetches = [
        pltpu.make_async_copy(refs[i], refs[count + i], arrived.at[i]) for i in range(count)
    ]
    for fetch in fetches:
        fetch.start()
    fetches[0].wait()
    for j in range(8):
        copies[j] = refs[count][...]
    for fetch in fetches[1:]:
        fetch.wait()


def conv(pre, edge, taps, extended, columns):
    extended[0:8, :] = jnp.zeros((8, pre.shape[1]), F32) if edge is None else edge
    extended[8:, :] = pre
    seg = columns[:, 0:1]
    total = taps[0:1, :] * pre
    for j in range(1, 4):
        same = columns[:, 8 * j : 8 * j + 1] == seg
        total = total + jnp.where(
            same, taps[j : j + 1, :] * extended[8 - j : 8 - j + BLOCK, :], 0.0
        )
    return total


def onward(pre, taps, own, following):
    sums = []
    for t in range(3):
        total = jnp.zeros((1, pre.shape[1]), F32)
        for j in range(t + 1, 4):
            at = BLOCK + t - j
            same = following[0:1, t : t + 1] == own[0:1, at : at + 1]
            total = total + jnp.where(same, taps[j : j + 1, :] * pre[at : at + 1, :], 0.0)
        sums.append(total)
    return sums


def stacked_rows(rows):
    shape = (8, LANES)
    index = lax.broadcasted_iota(jnp.int32, shape, 0)
    out = jnp.zeros(shape, F32)
    for at, row in rows.items():
        out = jnp.where(index == at, jnp.broadcast_to(row, shape), out)
    return out.astype(BF16)


def block_state(
    index,
    whole,
    gain,
    value_hbm,
    query_hbm,
    w_key,
    w_down,
    w_up,
    bias,
    seg_ids,
    taps_k,
    taps_v,
    pieces,
    tail,
    gained,
    row_scale,
    pre_q,
    pre_k,
    pre_v,
    cumulated,
    columns_out,
    own_rows,
    extended_k,
    extended_v,
    w_value,
    w_query,
    arrived,
):
    fetch_value = pltpu.make_async_copy(value_hbm, w_value, arrived.at[0])
    fetch_query = pltpu.make_async_copy(query_hbm, w_query, arrived.at[1])
    fetch_value.start()
    fetch_query.start()
    squares = jnp.zeros((BLOCK, CHUNK), F32)
    for f in range(WIDTH // CHUNK):
        lanes = slice(f * CHUNK, (f + 1) * CHUNK)
        activ = whole[f % 2, f // 2].astype(F32)
        squares = squares + activ * activ
        gained[:, lanes] = (activ * gain[:, lanes]).astype(BF16)
    scale = lax.rsqrt(jnp.sum(squares, axis=1, keepdims=True) / WIDTH + 1e-06)
    row_scale[...] = jnp.broadcast_to(scale, (BLOCK, CHUNK))
    rows = gained[...]
    rank_part = dot(rows, w_down[...], LAST) * scale

    at = index[0]
    own = seg_ids[pl.ds(at, 1), :].astype(F32)
    before = seg_ids[pl.ds(jnp.maximum(at - 1, 0), 1), :].astype(F32)
    before = jnp.where(at > 0, before, -1.0)
    following = seg_ids[pl.ds(jnp.minimum(at + 1, BLOCKS - 1), 1), :].astype(F32)
    own = jnp.broadcast_to(own, (8, BLOCK))
    before = jnp.broadcast_to(before, (8, BLOCK))
    lane = lax.broadcasted_iota(jnp.int32, (8, BLOCK), 1)
    parts = [own]
    for j in range(1, 4):
        parts.append(jnp.where(lane < j, pltpu.roll(before, j, 1), pltpu.roll(own, j, 1)))
    before = jnp.broadcast_to(before[:, BLOCK - 1 :], (8, BLOCK))
    last = jnp.broadcast_to(own[:, BLOCK - 1 :], (8, BLOCK))
    parts += [before, last]
    parts.append(jnp.zeros((BLOCK - 8 * len(parts), BLOCK), F32))
    columns = jnp.transpose(jnp.concatenate(parts, axis=0))
    columns_out[...] = columns
    own_rows[...] = own

    logits = dot(rank_part, w_up[...].astype(F32), precision=HIGHEST) + bias[...]
    log_decay = (jnp.minimum(logits, 0.0) - jnp.log(1.0 + jnp.exp(-jnp.abs(logits)))) / 16.0
    row_iota = lax.broadcasted_iota(jnp.int32, (BLOCK, BLOCK), 0)
    col_iota = lax.broadcasted_iota(jnp.int32, (BLOCK, BLOCK), 1)
    lower = jnp.where(row_iota >= col_iota, 1.0, 0.0).astype(F32)
    cum = dot(lower, log_decay, precision=HIGHEST)
    cumulated[...] = cum

    of_keys = dot(rows, w_key[...]) * scale
    fetch_value.wait()
    of_values = dot(rows, w_value[...]) * scale
    pre_k[...] = of_keys
    pre_v[...] = of_values
    sums_k = conv(of_keys, None, taps_k, extended_k, columns)
    sums_v = conv(of_values, None, taps_v, extended_v, columns)
    next_k = onward(of_keys, taps_k, own, following)
    next_v = onward(of_values, taps_v, own, following)
    final = cum[BLOCK - 1 :, :]
    factors = jnp.where(columns[:, 0:1] == columns[:, 40:41], jnp.exp(final - cum), 0.0)
    later = lax.broadcasted_iota(jnp.int32, (BLOCK, HEAD_K), 0) >= 3
    pushed = jnp.where(later, silu(sums_k) * factors, 0.0)
    state = dot(silu(sums_v).astype(BF16), pushed.astype(BF16), FIRST)
    keep = jnp.where(before[0:1, 0:1] == last[0:1, 0:1], jnp.exp(final), 0.0)
    high, low = halves(keep)
    lane = lax.broadcasted_iota(jnp.int32, (1, LANES), 1)
    mixed_v = []
    for upper in range(2):
        mine = (lane >= LANES // 2) == (upper == 1)
        mixed_v.append(
            [
                jnp.where(mine, sums_v[t : t + 1, :], pltpu.roll(next_v[t], LANES // 2, 1))
                for t in range(3)
            ]
        )
    for h in range(2):
        lanes = slice(h * LANES, (h + 1) * LANES)
        rows_b = {0: high.astype(F32)[:, lanes], 1: low.astype(F32)[:, lanes]}
        for t in range(3):
            rows_b[2 + t] = sums_k[t : t + 1, lanes]
            rows_b[5 + t] = next_k[t][:, lanes]
        tile_b = stacked_rows(rows_b)
        for upper in range(2):
            rows_c = {2 + t: factors[t : t + 1, lanes] for t in range(3)}
            rows_c.update({5 + t: mixed_v[upper][t] for t in range(3)})
            tile_c = stacked_rows(rows_c)
            for j in range(8):
                g = 8 * upper + j
                p = h * BLOCKS // 2 + g
                pieces[p, 0:PIECE, :] = state[g * PIECE : (g + 1) * PIECE, lanes].astype(BF16)
                pieces[p, PIECE : PIECE + 8, :] = tile_b
                pieces[p, PIECE + 8 :, :] = tile_c
    fetch_query.wait()
    of_queries = dot(rows, w_query[...]) * scale
    pre_q[...] = of_queries
    tail[:, :HEAD_K] = of_queries[BLOCK - 8 :, :]
    tail[:, HEAD_K : 2 * HEAD_K] = of_keys[BLOCK - 8 :, :]
    tail[:, 2 * HEAD_K :] = of_values[BLOCK - 8 :, :]


def output_gate(gained, row_scale, w_gate, head_gain, left, gate):
    del left
    gate[...] = silu(dot(gained[...], w_gate[...]) * row_scale[...]) * head_gain[...]


def block_attention(
    pre_q,
    pre_k,
    pre_v,
    edge,
    taps_q,
    taps_k,
    taps_v,
    cumulated,
    columns,
    own_rows,
    left,
    intra,
    reach,
    extended,
    extended_v,
):
    del left
    edges = edge[...]
    queries = silu(conv(pre_q[...], edges[:, :HEAD_K], taps_q, extended.at[0], columns))
    queries = queries * HEAD_K ** (-0.5)
    keys = silu(
        conv(pre_k[...], edges[:, HEAD_K : 2 * HEAD_K], taps_k, extended.at[1], columns)
    )
    values = silu(conv(pre_v[...], edges[:, 2 * HEAD_K :], taps_v, extended_v, columns))
    cum, seg = cumulated[...], columns[:, 0:1]
    row_iota = lax.broadcasted_iota(jnp.int32, (BLOCK, BLOCK), 0)
    col_iota = lax.broadcasted_iota(jnp.int32, (BLOCK, BLOCK), 1)
    reach[...] = jnp.where(seg == columns[:, 32:33], queries * jnp.exp(cum), 0.0)
    weights = jnp.zeros((BLOCK, BLOCK), F32)
    for half in (8, 16, 32, 64):
        anchors = [
            jnp.broadcast_to(cum[b + half - 1 : b + half, :], (2 * half, HEAD_K))
            for b in range(0, BLOCK, 2 * half)
        ]
        anchor = jnp.concatenate(anchors, axis=0) if len(anchors) > 1 else anchors[0]
        factor = jnp.exp(-jnp.abs(cum - anchor))
        part = dot((queries * factor).astype(BF16), (keys * factor).astype(BF16), LAST)
        inside = (
            (row_iota // (2 * half) == col_iota // (2 * half))
            & (row_iota % (2 * half) >= half)
            & (col_iota % (2 * half) < half)
        )
        weights = jnp.where(inside, part, weights)
    groups = (BLOCK // 8, 8, HEAD_K)
    cum_g, keys_g = cum.reshape(groups), keys.reshape(groups)
    queries_g = queries.reshape(groups)
    for by in range(8):
        if by:
            spread = jnp.minimum(cum_g - pltpu.roll(cum_g, by, 1), 0.0)
            product = queries_g * pltpu.roll(keys_g, by, 1) * jnp.exp(spread)
        else:
            product = queries_g * keys_g
        sums = jnp.sum(product.reshape(BLOCK, HEAD_K), axis=1, keepdims=True)
        inside = (row_iota - col_iota == by) & (row_iota % 8 >= by)
        weights = jnp.where(inside, sums, weights)
    visible = (seg == own_rows[0:1, :]) & (row_iota >= col_iota)
    weights = jnp.where(visible, weights, 0.0)
    intra[...] = dot(weights.astype(BF16), values.astype(BF16))


def scan_blocks(index, pieces, states, left):
    owner = (index[0] % ROWS_Y) * ROWS_X + index[0] // ROWS_Y
    first = (owner % (BLOCKS // 2)) * PIECE
    order = [(block % ROWS_Y) * ROWS_X + block // ROWS_Y for block in range(BLOCKS)]
    shape = (BLOCKS, 8, LANES)
    tiles_b = jnp.stack([pieces[at, PIECE : PIECE + 8, :].astype(F32) for at in order])
    tiles_c = jnp.stack([pieces[at, PIECE + 8 :, :].astype(F32) for at in order])
    nothing = jnp.zeros((1, 8, LANES), F32)
    back_b = jnp.concatenate([nothing, tiles_b[:-1]], axis=0)
    back_c = jnp.concatenate([nothing, tiles_c[:-1]], axis=0)
    pushed = silu(tiles_b + pltpu.roll(back_b, 5, 1)) * tiles_c
    values = pltpu.roll(silu(tiles_c + pltpu.roll(back_c, LANES // 2, 2)), 5, 1)
    row = lax.broadcasted_iota(jnp.int32, shape, 1)
    values = jnp.where((row >= 2) & (row < 5), values, 0.0)
    rows = BLOCKS * 8
    lane = lax.broadcasted_iota(jnp.int32, (PIECE, LANES), 1)
    chosen = lane == lax.broadcasted_iota(jnp.int32, (PIECE, LANES), 0) + first
    chosen = jnp.where(chosen, 1.0, 0.0).astype(BF16)
    mine = dot(chosen, values.reshape(rows, LANES).astype(BF16), LAST)
    same = lax.broadcasted_iota(jnp.int32, (rows, rows), 0) // 8
    same = same == lax.broadcasted_iota(jnp.int32, (rows, rows), 1) // 8
    spread = jnp.where(same, jnp.concatenate([mine] * BLOCKS, axis=0), 0.0)
    added = dot(spread.astype(BF16), pushed.reshape(rows, LANES).astype(BF16))
    state = jnp.zeros((PIECE, LANES), F32)
    for block, at in enumerate(order):
        states[at] = state.astype(BF16)
        decay = tiles_b[block, 0:1, :] + tiles_b[block, 1:2, :]
        own = pieces[at, 0:PIECE, :].astype(F32) + added[block * 8 : block * 8 + 8, :]
        state = state * decay + own
    left[...] = state


def attend(index, intra, reach, incoming, gate, w_out, kept, kept_squares, sent):
    high, low = halves(reach[...])
    state = jnp.concatenate([incoming[0], incoming[1]], axis=1)
    attended = intra[...] + dot(high, state, LAST) + dot(low, state, LAST)
    squares = dot(jnp.ones((8, CHUNK), F32), attended * attended, LAST, precision=HIGHEST)
    terms = dot((attended * gate[...]).astype(BF16), w_out[...])
    first = index[0] == 0
    for j in range(8):
        even = terms[:, (2 * j) * CHUNK : (2 * j + 1) * CHUNK]
        odd = terms[:, (2 * j + 1) * CHUNK : (2 * j + 2) * CHUNK]
        kept[j] = jnp.where(first, even, odd)
        sent[j * BLOCK : (j + 1) * BLOCK, :] = jnp.where(first, odd, even).astype(BF16)
    kept_squares[...] = squares
    sent[8 * BLOCK :, :] = pair_rows(squares[0:1, :])


def pair_sum(index, kept, kept_squares, both, sent):
    received = both.at[1 - index[0]]
    other = received[8 * BLOCK :, :].astype(F32)
    squares = pair_rows(kept_squares[0:1, :] + other[0:1, :] + other[1:2, :])
    for j in range(8):
        terms = kept[j] + received[j * BLOCK : (j + 1) * BLOCK, :].astype(F32)
        sent[j, 0:BLOCK, :] = terms.astype(BF16)
        sent[j, BLOCK:, :] = squares


def finish(received, hidden, mixed):
    parts = []
    for r in range(4):
        pair = received[2 * r, BLOCK:, :].astype(F32) + received[2 * r + 1, BLOCK:, :].astype(F32)
        squares = pair[0:1, :] + pair[1:2, :]
        scale = lax.rsqrt(squares / HEAD_V + 1e-05)
        parts.append(jnp.broadcast_to(scale, (8, BLOCK)))
    parts.append(jnp.zeros((BLOCK - 8 * len(parts), BLOCK), F32))
    columns = jnp.transpose(jnp.concatenate(parts, axis=0))
    total = hidden[...].astype(F32)
    for r in range(4):
        terms = received[2 * r, 0:BLOCK, :].astype(F32)
        terms = terms + received[2 * r + 1, 0:BLOCK, :].astype(F32)
        total = total + columns[:, 8 * r : 8 * r + 1] * terms
    mixed[...] = total.astype(BF16)


def shards(
    hidden_in,
    seg_ids,
    norm_gain,
    w_query,
    w_key,
    w_value,
    w_gate,
    w_decay_down,
    w_decay_up,
    decay_bias,
    conv_query,
    conv_key,
    conv_value,
    head_gain,
    w_out,
):
    block = lax.axis_index("x") * ROWS_Y + lax.axis_index("y")
    block_at = jnp.reshape(block, (1,)).astype(jnp.int32)
    core_at = jnp.reshape(lax.axis_index("core"), (1,)).astype(jnp.int32)

    needed = (
        hidden_in,
        norm_gain.reshape(1, WIDTH),
        w_decay_down.T,
        w_decay_up,
        decay_bias.reshape(1, HEAD_K),
        seg_ids.reshape(BLOCKS, BLOCK),
        conv_query,
        conv_key,
        conv_value,
    )
    hidden, gain, down, up, bias, segs, taps_q, taps_k, taps_v, copies = local_call(
        fetch_and_spread,
        [*((a.shape, a.dtype) for a in needed), ((8, BLOCK, CHUNK), BF16)],
        block_at,
        core_at,
        *needed,
        scratch=[pltpu.SemaphoreType.DMA((len(needed),))],
        scalars=2,
        anywhere=range(2, 2 + len(needed)),
    )
    of_core = lax.all_to_all(copies, CHIPS, 0, 0)
    whole = lax.all_gather(of_core, "core", axis=0)
    pieces, tail, gained, row_scale, pre_q, pre_k, pre_v, cumulated, columns, own_rows = local_call(
        block_state,
        [
            ((BLOCKS, PIECE + 16, LANES), BF16),
            ((8, 2 * HEAD_K + CHUNK), F32),
            ((BLOCK, WIDTH), BF16),
            ((BLOCK, CHUNK), F32),
            ((BLOCK, HEAD_K), F32),
            ((BLOCK, HEAD_K), F32),
            ((BLOCK, CHUNK), F32),
            ((BLOCK, HEAD_K), F32),
            ((BLOCK, BLOCK), F32),
            ((8, BLOCK), F32),
        ],
        block_at,
        whole,
        gain,
        w_value,
        w_query,
        w_key,
        down,
        up,
        bias,
        segs,
        taps_k,
        taps_v,
        scratch=[
            pltpu.VMEM((BLOCK + 8, HEAD_K), F32),
            pltpu.VMEM((BLOCK + 8, CHUNK), F32),
            pltpu.VMEM((WIDTH, CHUNK), BF16),
            pltpu.VMEM((WIDTH, HEAD_K), BF16),
            pltpu.SemaphoreType.DMA((2,)),
        ],
        scalars=1,
        anywhere=(3, 4),
    )
    edge = lax.ppermute(tail, SEQ, [(i, i + 1) for i in range(BLOCKS - 1)])
    owned = lax.all_to_all(pieces, GRID, 0, 0)
    states, left = local_call(
        scan_blocks,
        [((BLOCKS, PIECE, LANES), BF16), ((PIECE, LANES), F32)],
        block_at,
        owned,
        scalars=1,
    )
    incoming = lax.all_to_all(states, GRID, 0, 0).reshape(2, CHUNK, LANES)
    (gate,) = local_call(
        output_gate,
        [((BLOCK, CHUNK), F32)],
        gained,
        row_scale,
        w_gate,
        head_gain.reshape(1, CHUNK),
        left,
    )
    intra, reach = local_call(
        block_attention,
        [((BLOCK, CHUNK), F32), ((BLOCK, HEAD_K), F32)],
        pre_q,
        pre_k,
        pre_v,
        edge,
        taps_q,
        taps_k,
        taps_v,
        cumulated,
        columns,
        own_rows,
        left,
        scratch=[
            pltpu.VMEM((2, BLOCK + 8, HEAD_K), F32),
            pltpu.VMEM((BLOCK + 8, CHUNK), F32),
        ],
    )
    mine, my_squares, sent = local_call(
        attend,
        [((8, BLOCK, CHUNK), F32), ((8, BLOCK), F32), ((8 * BLOCK + 8, CHUNK), BF16)],
        core_at,
        intra,
        reach,
        incoming,
        gate,
        w_out,
        scalars=1,
    )
    both = lax.all_gather(sent, "core", axis=0)
    (pairs,) = local_call(
        pair_sum, [((8, BLOCK + 8, CHUNK), BF16)], core_at, mine, my_squares, both, scalars=1
    )
    arrived = lax.all_to_all(pairs, CHIPS, 0, 0)
    (mixed,) = local_call(
        finish, [((BLOCK, CHUNK), BF16)], arrived, hidden, last=True
    )
    return mixed


def solution(mesh):
    finer = Mesh(mesh.devices.reshape(ROWS_X, ROWS_Y, 4, 2, 2), ("x", "y", "row", "zhi", "core"))
    part = ("row", "zhi", "core")
    return jax.shard_map(
        shards,
        mesh=finer,
        in_specs=(
            P(SEQ, part),
            P(),
            P(),
            P(None, "row"),
            P(None, "row"),
            P(None, part),
            P(None, part),
            P(),
            P(None, "row"),
            P("row"),
            P(None, "row"),
            P(None, "row"),
            P(None, part),
            P(("zhi", "core")),
            P(part, None),
        ),
        out_specs=P(SEQ, part),
        check_vma=False,
    )
```

```python
import jax
import jax.numpy as jnp
from jax import lax
from jax.experimental import pallas as pl
from jax.experimental.pallas import tpu as pltpu
from jax.sharding import Mesh, PartitionSpec as P

F32 = jnp.float32
BF16 = jnp.bfloat16
HEAD_V = 512
WIDTH = 2048
BLOCK = 128
HEAD_K = 256
CHUNK = 128
LAST = (((1,), (1,)), ((), ()))
FIRST = (((0,), (0,)), ((), ()))

SEQ = ("x", "y")
GRID = ("y", "x")
CHIPS = ("row", "zhi")
ROWS_X, ROWS_Y = 4, 8
LANES = 128
BLOCKS = ROWS_X * ROWS_Y
PIECE = 2 * CHUNK // BLOCKS


def local_call(kernel, outs, *args, scratch=(), scalars=0, plain=(), anywhere=(), last=False):
    elsewhere = (*range(scalars), *plain, *anywhere)
    vmem = pl.BlockSpec(memory_space=pltpu.VMEM)
    smem = pl.BlockSpec(memory_space=pltpu.SMEM)
    args = [
        pltpu.with_memory_space_constraint(a, pltpu.HBM if i in anywhere else pltpu.VMEM)
        if i in anywhere or i not in elsewhere
        else a
        for i, a in enumerate(args)
    ]
    return pl.pallas_call(
        kernel,
        out_shape=[jax.ShapeDtypeStruct(s, t) if last else pltpu.VMEM(s, t) for s, t in outs],
        in_specs=[
            smem if i < scalars else pl.BlockSpec(memory_space=pltpu.HBM) if i in anywhere else vmem
            for i in range(len(args))
        ],
        out_specs=[vmem] * len(outs),
        scratch_shapes=list(scratch),
        name=kernel.__name__,
        compiler_params=pltpu.CompilerParams(vmem_limit_bytes=16 << 20),
    )(*args)


def dot(a, b, dims=(((1,), (0,)), ((), ()))):
    return lax.dot_general(a, b, dims, preferred_element_type=F32)


def halves(value):
    high = value.astype(BF16)
    return high, (value - high.astype(F32)).astype(BF16)


def thirds(value):
    high, _ = halves(value)
    middle, low = halves(value - high.astype(F32))
    return high, middle, low


def pair_rows(value):
    high, low = halves(value)
    shape = (8, value.shape[1])
    index = lax.broadcasted_iota(jnp.int32, shape, 0)
    both = jnp.where(
        index == 0,
        jnp.broadcast_to(high.astype(F32), shape),
        jnp.where(index == 1, jnp.broadcast_to(low.astype(F32), shape), 0.0),
    )
    return both.astype(BF16)


def silu(value):
    return value * jax.nn.sigmoid(value)


def fetch_and_spread(index, core, *refs):
    del index, core
    *refs, copies, arrived = refs
    count = len(refs) // 2
    fetches = [
        pltpu.make_async_copy(refs[i], refs[count + i], arrived.at[i]) for i in range(count)
    ]
    for fetch in fetches:
        fetch.start()
    fetches[0].wait()
    for j in range(8):
        copies[j] = refs[count][...]
    for fetch in fetches[1:]:
        fetch.wait()


def conv(pre, edge, taps, extended, columns):
    extended[0:8, :] = jnp.zeros((8, pre.shape[1]), F32) if edge is None else edge
    extended[8:, :] = pre
    seg = columns[:, 0:1]
    total = taps[0:1, :] * pre
    for j in range(1, 4):
        same = columns[:, 8 * j : 8 * j + 1] == seg
        total = total + jnp.where(
            same, taps[j : j + 1, :] * extended[8 - j : 8 - j + BLOCK, :], 0.0
        )
    return total


def onward(pre, taps, own, following):
    sums = []
    for t in range(3):
        total = jnp.zeros((1, pre.shape[1]), F32)
        for j in range(t + 1, 4):
            at = BLOCK + t - j
            same = following[0:1, t : t + 1] == own[0:1, at : at + 1]
            total = total + jnp.where(same, taps[j : j + 1, :] * pre[at : at + 1, :], 0.0)
        sums.append(total)
    return sums


def stacked_rows(rows):
    shape = (8, LANES)
    index = lax.broadcasted_iota(jnp.int32, shape, 0)
    out = jnp.zeros(shape, F32)
    for at, row in rows.items():
        out = jnp.where(index == at, jnp.broadcast_to(row, shape), out)
    return out.astype(BF16)


def block_state(
    index,
    whole,
    gain,
    value_hbm,
    query_hbm,
    w_key,
    w_down,
    w_up,
    bias,
    seg_ids,
    taps_k,
    taps_v,
    pieces,
    tail,
    gained,
    row_scale,
    pre_q,
    pre_k,
    pre_v,
    cumulated,
    columns_out,
    own_rows,
    extended_k,
    extended_v,
    w_value,
    w_query,
    arrived,
):
    fetch_value = pltpu.make_async_copy(value_hbm, w_value, arrived.at[0])
    fetch_query = pltpu.make_async_copy(query_hbm, w_query, arrived.at[1])
    fetch_value.start()
    fetch_query.start()
    squares = jnp.zeros((BLOCK, CHUNK), F32)
    for f in range(WIDTH // CHUNK):
        lanes = slice(f * CHUNK, (f + 1) * CHUNK)
        activ = whole[f % 2, f // 2].astype(F32)
        squares = squares + activ * activ
        gained[:, lanes] = (activ * gain[:, lanes]).astype(BF16)
    scale = lax.rsqrt(jnp.sum(squares, axis=1, keepdims=True) / WIDTH + 1e-06)
    row_scale[...] = jnp.broadcast_to(scale, (BLOCK, CHUNK))
    rows = gained[...]
    rank_part = dot(rows, w_down[...], LAST) * scale

    at = index[0]
    own = seg_ids[pl.ds(at, 1), :].astype(F32)
    before = seg_ids[pl.ds(jnp.maximum(at - 1, 0), 1), :].astype(F32)
    before = jnp.where(at > 0, before, -1.0)
    following = seg_ids[pl.ds(jnp.minimum(at + 1, BLOCKS - 1), 1), :].astype(F32)
    own = jnp.broadcast_to(own, (8, BLOCK))
    before = jnp.broadcast_to(before, (8, BLOCK))
    lane = lax.broadcasted_iota(jnp.int32, (8, BLOCK), 1)
    parts = [own]
    for j in range(1, 4):
        parts.append(jnp.where(lane < j, pltpu.roll(before, j, 1), pltpu.roll(own, j, 1)))
    before = jnp.broadcast_to(before[:, BLOCK - 1 :], (8, BLOCK))
    last = jnp.broadcast_to(own[:, BLOCK - 1 :], (8, BLOCK))
    parts += [before, last]
    parts.append(jnp.zeros((BLOCK - 8 * len(parts), BLOCK), F32))
    columns = jnp.transpose(jnp.concatenate(parts, axis=0))
    columns_out[...] = columns
    own_rows[...] = own

    logits = bias[...]
    for part in thirds(rank_part):
        logits = logits + dot(part, w_up[...])
    log_decay = (jnp.minimum(logits, 0.0) - jnp.log(1.0 + jnp.exp(-jnp.abs(logits)))) / 16.0
    row_iota = lax.broadcasted_iota(jnp.int32, (BLOCK, BLOCK), 0)
    col_iota = lax.broadcasted_iota(jnp.int32, (BLOCK, BLOCK), 1)
    lower = jnp.where(row_iota >= col_iota, 1.0, 0.0).astype(BF16)
    cum = dot(
        jnp.concatenate([lower] * 3, axis=1), jnp.concatenate(thirds(log_decay), axis=0)
    )
    cumulated[...] = cum

    of_keys = dot(rows, w_key[...]) * scale
    fetch_value.wait()
    of_values = dot(rows, w_value[...]) * scale
    pre_k[...] = of_keys
    pre_v[...] = of_values
    sums_k = conv(of_keys, None, taps_k, extended_k, columns)
    sums_v = conv(of_values, None, taps_v, extended_v, columns)
    next_k = onward(of_keys, taps_k, own, following)
    next_v = onward(of_values, taps_v, own, following)
    final = cum[BLOCK - 1 :, :]
    factors = jnp.where(columns[:, 0:1] == columns[:, 40:41], jnp.exp(final - cum), 0.0)
    later = lax.broadcasted_iota(jnp.int32, (BLOCK, HEAD_K), 0) >= 3
    pushed = jnp.where(later, silu(sums_k) * factors, 0.0)
    state = dot(silu(sums_v).astype(BF16), pushed.astype(BF16), FIRST)
    keep = jnp.where(before[0:1, 0:1] == last[0:1, 0:1], jnp.exp(final), 0.0)
    high, low = halves(keep)
    lane = lax.broadcasted_iota(jnp.int32, (1, LANES), 1)
    mixed_v = []
    for upper in range(2):
        mine = (lane >= LANES // 2) == (upper == 1)
        mixed_v.append(
            [
                jnp.where(mine, sums_v[t : t + 1, :], pltpu.roll(next_v[t], LANES // 2, 1))
                for t in range(3)
            ]
        )
    for h in range(2):
        lanes = slice(h * LANES, (h + 1) * LANES)
        rows_b = {0: high.astype(F32)[:, lanes], 1: low.astype(F32)[:, lanes]}
        for t in range(3):
            rows_b[2 + t] = sums_k[t : t + 1, lanes]
            rows_b[5 + t] = next_k[t][:, lanes]
        tile_b = stacked_rows(rows_b)
        for upper in range(2):
            rows_c = {2 + t: factors[t : t + 1, lanes] for t in range(3)}
            rows_c.update({5 + t: mixed_v[upper][t] for t in range(3)})
            tile_c = stacked_rows(rows_c)
            for j in range(8):
                g = 8 * upper + j
                p = h * BLOCKS // 2 + g
                pieces[p, 0:PIECE, :] = state[g * PIECE : (g + 1) * PIECE, lanes].astype(BF16)
                pieces[p, PIECE : PIECE + 8, :] = tile_b
                pieces[p, PIECE + 8 :, :] = tile_c
    fetch_query.wait()
    of_queries = dot(rows, w_query[...]) * scale
    pre_q[...] = of_queries
    tail[:, :HEAD_K] = of_queries[BLOCK - 8 :, :]
    tail[:, HEAD_K : 2 * HEAD_K] = of_keys[BLOCK - 8 :, :]
    tail[:, 2 * HEAD_K :] = of_values[BLOCK - 8 :, :]


def output_gate(gained, row_scale, w_gate, head_gain, left, gate):
    del left
    gate[...] = silu(dot(gained[...], w_gate[...]) * row_scale[...]) * head_gain[...]


def block_attention(
    pre_q,
    pre_k,
    pre_v,
    edge,
    taps_q,
    taps_k,
    taps_v,
    cumulated,
    columns,
    own_rows,
    left,
    intra,
    reach,
    extended,
    extended_v,
):
    del left
    edges = edge[...]
    queries = silu(conv(pre_q[...], edges[:, :HEAD_K], taps_q, extended.at[0], columns))
    queries = queries * HEAD_K ** (-0.5)
    keys = silu(
        conv(pre_k[...], edges[:, HEAD_K : 2 * HEAD_K], taps_k, extended.at[1], columns)
    )
    values = silu(conv(pre_v[...], edges[:, 2 * HEAD_K :], taps_v, extended_v, columns))
    cum, seg = cumulated[...], columns[:, 0:1]
    row_iota = lax.broadcasted_iota(jnp.int32, (BLOCK, BLOCK), 0)
    col_iota = lax.broadcasted_iota(jnp.int32, (BLOCK, BLOCK), 1)
    reach[...] = jnp.where(seg == columns[:, 32:33], queries * jnp.exp(cum), 0.0)
    weights = jnp.zeros((BLOCK, BLOCK), F32)
    for half in (8, 16, 32, 64):
        anchors = [
            jnp.broadcast_to(cum[b + half - 1 : b + half, :], (2 * half, HEAD_K))
            for b in range(0, BLOCK, 2 * half)
        ]
        anchor = jnp.concatenate(anchors, axis=0) if len(anchors) > 1 else anchors[0]
        factor = jnp.exp(-jnp.abs(cum - anchor))
        part = dot((queries * factor).astype(BF16), (keys * factor).astype(BF16), LAST)
        inside = (
            (row_iota // (2 * half) == col_iota // (2 * half))
            & (row_iota % (2 * half) >= half)
            & (col_iota % (2 * half) < half)
        )
        weights = jnp.where(inside, part, weights)
    groups = (BLOCK // 8, 8, HEAD_K)
    cum_g, keys_g = cum.reshape(groups), keys.reshape(groups)
    queries_g = queries.reshape(groups)
    for by in range(8):
        if by:
            spread = jnp.minimum(cum_g - pltpu.roll(cum_g, by, 1), 0.0)
            product = queries_g * pltpu.roll(keys_g, by, 1) * jnp.exp(spread)
        else:
            product = queries_g * keys_g
        sums = jnp.sum(product.reshape(BLOCK, HEAD_K), axis=1, keepdims=True)
        inside = (row_iota - col_iota == by) & (row_iota % 8 >= by)
        weights = jnp.where(inside, sums, weights)
    visible = (seg == own_rows[0:1, :]) & (row_iota >= col_iota)
    weights = jnp.where(visible, weights, 0.0)
    intra[...] = dot(weights.astype(BF16), values.astype(BF16))


def scan_blocks(index, pieces, states, left):
    owner = (index[0] % ROWS_Y) * ROWS_X + index[0] // ROWS_Y
    first = (owner % (BLOCKS // 2)) * PIECE
    order = [(block % ROWS_Y) * ROWS_X + block // ROWS_Y for block in range(BLOCKS)]
    shape = (BLOCKS, 8, LANES)
    tiles_b = jnp.stack([pieces[at, PIECE : PIECE + 8, :].astype(F32) for at in order])
    tiles_c = jnp.stack([pieces[at, PIECE + 8 :, :].astype(F32) for at in order])
    nothing = jnp.zeros((1, 8, LANES), F32)
    back_b = jnp.concatenate([nothing, tiles_b[:-1]], axis=0)
    back_c = jnp.concatenate([nothing, tiles_c[:-1]], axis=0)
    pushed = silu(tiles_b + pltpu.roll(back_b, 5, 1)) * tiles_c
    values = pltpu.roll(silu(tiles_c + pltpu.roll(back_c, LANES // 2, 2)), 5, 1)
    row = lax.broadcasted_iota(jnp.int32, shape, 1)
    values = jnp.where((row >= 2) & (row < 5), values, 0.0)
    rows = BLOCKS * 8
    lane = lax.broadcasted_iota(jnp.int32, (PIECE, LANES), 1)
    chosen = lane == lax.broadcasted_iota(jnp.int32, (PIECE, LANES), 0) + first
    chosen = jnp.where(chosen, 1.0, 0.0).astype(BF16)
    mine = dot(chosen, values.reshape(rows, LANES).astype(BF16), LAST)
    same = lax.broadcasted_iota(jnp.int32, (rows, rows), 0) // 8
    same = same == lax.broadcasted_iota(jnp.int32, (rows, rows), 1) // 8
    spread = jnp.where(same, jnp.concatenate([mine] * BLOCKS, axis=0), 0.0)
    added = dot(spread.astype(BF16), pushed.reshape(rows, LANES).astype(BF16))
    state = jnp.zeros((PIECE, LANES), F32)
    for block, at in enumerate(order):
        states[at] = state.astype(BF16)
        decay = tiles_b[block, 0:1, :] + tiles_b[block, 1:2, :]
        own = pieces[at, 0:PIECE, :].astype(F32) + added[block * 8 : block * 8 + 8, :]
        state = state * decay + own
    left[...] = state


def attend(index, intra, reach, incoming, gate, w_out, kept, kept_squares, sent):
    high, low = halves(reach[...])
    state = jnp.concatenate([incoming[0], incoming[1]], axis=1)
    attended = intra[...] + dot(high, state, LAST) + dot(low, state, LAST)
    ones = jnp.ones((8, CHUNK), BF16)
    squares = sum(dot(ones, part, LAST) for part in thirds(attended * attended))
    terms = dot((attended * gate[...]).astype(BF16), w_out[...])
    first = index[0] == 0
    for j in range(8):
        even = terms[:, (2 * j) * CHUNK : (2 * j + 1) * CHUNK]
        odd = terms[:, (2 * j + 1) * CHUNK : (2 * j + 2) * CHUNK]
        kept[j] = jnp.where(first, even, odd)
        sent[j * BLOCK : (j + 1) * BLOCK, :] = jnp.where(first, odd, even).astype(BF16)
    kept_squares[...] = squares
    sent[8 * BLOCK :, :] = pair_rows(squares[0:1, :])


def pair_sum(index, kept, kept_squares, both, sent):
    received = both.at[1 - index[0]]
    other = received[8 * BLOCK :, :].astype(F32)
    squares = pair_rows(kept_squares[0:1, :] + other[0:1, :] + other[1:2, :])
    for j in range(8):
        terms = kept[j] + received[j * BLOCK : (j + 1) * BLOCK, :].astype(F32)
        sent[j, 0:BLOCK, :] = terms.astype(BF16)
        sent[j, BLOCK:, :] = squares


def finish(received, hidden, mixed):
    parts = []
    for r in range(4):
        pair = received[2 * r, BLOCK:, :].astype(F32) + received[2 * r + 1, BLOCK:, :].astype(F32)
        squares = pair[0:1, :] + pair[1:2, :]
        scale = lax.rsqrt(squares / HEAD_V + 1e-05)
        parts.append(jnp.broadcast_to(scale, (8, BLOCK)))
    parts.append(jnp.zeros((BLOCK - 8 * len(parts), BLOCK), F32))
    columns = jnp.transpose(jnp.concatenate(parts, axis=0))
    total = hidden[...].astype(F32)
    for r in range(4):
        terms = received[2 * r, 0:BLOCK, :].astype(F32)
        terms = terms + received[2 * r + 1, 0:BLOCK, :].astype(F32)
        total = total + columns[:, 8 * r : 8 * r + 1] * terms
    mixed[...] = total.astype(BF16)


def shards(
    hidden_in,
    seg_ids,
    norm_gain,
    w_query,
    w_key,
    w_value,
    w_gate,
    w_decay_down,
    w_decay_up,
    decay_bias,
    conv_query,
    conv_key,
    conv_value,
    head_gain,
    w_out,
):
    block = lax.axis_index("x") * ROWS_Y + lax.axis_index("y")
    block_at = jnp.reshape(block, (1,)).astype(jnp.int32)
    core_at = jnp.reshape(lax.axis_index("core"), (1,)).astype(jnp.int32)

    needed = (
        hidden_in,
        norm_gain.reshape(1, WIDTH),
        w_decay_down.T,
        w_decay_up,
        decay_bias.reshape(1, HEAD_K),
        seg_ids.reshape(BLOCKS, BLOCK),
        conv_query,
        conv_key,
        conv_value,
    )
    hidden, gain, down, up, bias, segs, taps_q, taps_k, taps_v, copies = local_call(
        fetch_and_spread,
        [*((a.shape, a.dtype) for a in needed), ((8, BLOCK, CHUNK), BF16)],
        block_at,
        core_at,
        *needed,
        scratch=[pltpu.SemaphoreType.DMA((len(needed),))],
        scalars=2,
        anywhere=range(2, 2 + len(needed)),
    )
    of_core = lax.all_to_all(copies, CHIPS, 0, 0)
    whole = lax.all_gather(of_core, "core", axis=0)
    pieces, tail, gained, row_scale, pre_q, pre_k, pre_v, cumulated, columns, own_rows = local_call(
        block_state,
        [
            ((BLOCKS, PIECE + 16, LANES), BF16),
            ((8, 2 * HEAD_K + CHUNK), F32),
            ((BLOCK, WIDTH), BF16),
            ((BLOCK, CHUNK), F32),
            ((BLOCK, HEAD_K), F32),
            ((BLOCK, HEAD_K), F32),
            ((BLOCK, CHUNK), F32),
            ((BLOCK, HEAD_K), F32),
            ((BLOCK, BLOCK), F32),
            ((8, BLOCK), F32),
        ],
        block_at,
        whole,
        gain,
        w_value,
        w_query,
        w_key,
        down,
        up,
        bias,
        segs,
        taps_k,
        taps_v,
        scratch=[
            pltpu.VMEM((BLOCK + 8, HEAD_K), F32),
            pltpu.VMEM((BLOCK + 8, CHUNK), F32),
            pltpu.VMEM((WIDTH, CHUNK), BF16),
            pltpu.VMEM((WIDTH, HEAD_K), BF16),
            pltpu.SemaphoreType.DMA((2,)),
        ],
        scalars=1,
        anywhere=(3, 4),
    )
    edge = lax.ppermute(tail, SEQ, [(i, i + 1) for i in range(BLOCKS - 1)])
    owned = lax.all_to_all(pieces, GRID, 0, 0)
    states, left = local_call(
        scan_blocks,
        [((BLOCKS, PIECE, LANES), BF16), ((PIECE, LANES), F32)],
        block_at,
        owned,
        scalars=1,
    )
    incoming = lax.all_to_all(states, GRID, 0, 0).reshape(2, CHUNK, LANES)
    (gate,) = local_call(
        output_gate,
        [((BLOCK, CHUNK), F32)],
        gained,
        row_scale,
        w_gate,
        head_gain.reshape(1, CHUNK),
        left,
    )
    intra, reach = local_call(
        block_attention,
        [((BLOCK, CHUNK), F32), ((BLOCK, HEAD_K), F32)],
        pre_q,
        pre_k,
        pre_v,
        edge,
        taps_q,
        taps_k,
        taps_v,
        cumulated,
        columns,
        own_rows,
        left,
        scratch=[
            pltpu.VMEM((2, BLOCK + 8, HEAD_K), F32),
            pltpu.VMEM((BLOCK + 8, CHUNK), F32),
        ],
    )
    mine, my_squares, sent = local_call(
        attend,
        [((8, BLOCK, CHUNK), F32), ((8, BLOCK), F32), ((8 * BLOCK + 8, CHUNK), BF16)],
        core_at,
        intra,
        reach,
        incoming,
        gate,
        w_out,
        scalars=1,
    )
    both = lax.all_gather(sent, "core", axis=0)
    (pairs,) = local_call(
        pair_sum, [((8, BLOCK + 8, CHUNK), BF16)], core_at, mine, my_squares, both, scalars=1
    )
    arrived = lax.all_to_all(pairs, CHIPS, 0, 0)
    (mixed,) = local_call(
        finish, [((BLOCK, CHUNK), BF16)], arrived, hidden, last=True
    )
    return mixed


def solution(mesh):
    finer = Mesh(mesh.devices.reshape(ROWS_X, ROWS_Y, 4, 2, 2), ("x", "y", "row", "zhi", "core"))
    part = ("row", "zhi", "core")
    return jax.shard_map(
        shards,
        mesh=finer,
        in_specs=(
            P(SEQ, part),
            P(),
            P(),
            P(None, "row"),
            P(None, "row"),
            P(None, part),
            P(None, part),
            P(),
            P(None, "row"),
            P("row"),
            P(None, "row"),
            P(None, "row"),
            P(None, part),
            P(("zhi", "core")),
            P(part, None),
        ),
        out_specs=P(SEQ, part),
        check_vma=False,
    )
```

```python
import jax
import jax.numpy as jnp
from jax import lax
from jax.experimental import pallas as pl
from jax.experimental.pallas import tpu as pltpu
from jax.sharding import Mesh, PartitionSpec as P

F32 = jnp.float32
BF16 = jnp.bfloat16
HIGHEST = lax.Precision.HIGHEST
HEAD_V = 512
WIDTH = 2048
BLOCK = 128
HEAD_K = 256
CHUNK = 128
LAST = (((1,), (1,)), ((), ()))
FIRST = (((0,), (0,)), ((), ()))

SEQ = ("x", "y")
GRID = ("y", "x")
CHIPS = ("row", "zhi")
ROWS_X, ROWS_Y = 4, 8
LANES = 128
BLOCKS = ROWS_X * ROWS_Y
PIECE = 2 * CHUNK // BLOCKS


def local_call(kernel, outs, *args, scratch=(), scalars=0, plain=(), anywhere=(), last=False):
    elsewhere = (*range(scalars), *plain, *anywhere)
    vmem = pl.BlockSpec(memory_space=pltpu.VMEM)
    smem = pl.BlockSpec(memory_space=pltpu.SMEM)
    args = [
        pltpu.with_memory_space_constraint(a, pltpu.HBM if i in anywhere else pltpu.VMEM)
        if i in anywhere or i not in elsewhere
        else a
        for i, a in enumerate(args)
    ]
    return pl.pallas_call(
        kernel,
        out_shape=[jax.ShapeDtypeStruct(s, t) if last else pltpu.VMEM(s, t) for s, t in outs],
        in_specs=[
            smem if i < scalars else pl.BlockSpec(memory_space=pltpu.HBM) if i in anywhere else vmem
            for i in range(len(args))
        ],
        out_specs=[vmem] * len(outs),
        scratch_shapes=list(scratch),
        name=kernel.__name__,
        compiler_params=pltpu.CompilerParams(vmem_limit_bytes=16 << 20),
    )(*args)


def dot(a, b, dims=(((1,), (0,)), ((), ())), precision=None):
    return lax.dot_general(a, b, dims, precision=precision, preferred_element_type=F32)


def halves(value):
    high = value.astype(BF16)
    return high, (value - high.astype(F32)).astype(BF16)


def pair_rows(value):
    high, low = halves(value)
    shape = (8, value.shape[1])
    index = lax.broadcasted_iota(jnp.int32, shape, 0)
    both = jnp.where(
        index == 0,
        jnp.broadcast_to(high.astype(F32), shape),
        jnp.where(index == 1, jnp.broadcast_to(low.astype(F32), shape), 0.0),
    )
    return both.astype(BF16)


def silu(value):
    return value * jax.nn.sigmoid(value)


def fetch_and_spread(index, core, *refs):
    del index, core
    *refs, copies, arrived = refs
    count = len(refs) // 2
    fetches = [
        pltpu.make_async_copy(refs[i], refs[count + i], arrived.at[i]) for i in range(count)
    ]
    for fetch in fetches:
        fetch.start()
    fetches[0].wait()
    for j in range(8):
        copies[j] = refs[count][...]
    for fetch in fetches[1:]:
        fetch.wait()


def conv(pre, edge, taps, extended, columns):
    extended[0:8, :] = jnp.zeros((8, pre.shape[1]), F32) if edge is None else edge
    extended[8:, :] = pre
    seg = columns[:, 0:1]
    total = taps[0:1, :] * pre
    for j in range(1, 4):
        same = columns[:, 8 * j : 8 * j + 1] == seg
        total = total + jnp.where(
            same, taps[j : j + 1, :] * extended[8 - j : 8 - j + BLOCK, :], 0.0
        )
    return total


def onward(pre, taps, own, following):
    sums = []
    for t in range(3):
        total = jnp.zeros((1, pre.shape[1]), F32)
        for j in range(t + 1, 4):
            at = BLOCK + t - j
            same = following[0:1, t : t + 1] == own[0:1, at : at + 1]
            total = total + jnp.where(same, taps[j : j + 1, :] * pre[at : at + 1, :], 0.0)
        sums.append(total)
    return sums


def stacked_rows(rows):
    shape = (8, LANES)
    index = lax.broadcasted_iota(jnp.int32, shape, 0)
    out = jnp.zeros(shape, F32)
    for at, row in rows.items():
        out = jnp.where(index == at, jnp.broadcast_to(row, shape), out)
    return out.astype(BF16)


def block_state(
    index,
    whole,
    gain,
    value_hbm,
    query_hbm,
    w_key,
    w_down,
    w_up,
    bias,
    seg_ids,
    taps_k,
    taps_v,
    pieces,
    tail,
    gained,
    row_scale,
    pre_q,
    pre_k,
    pre_v,
    cumulated,
    columns_out,
    own_rows,
    extended_k,
    extended_v,
    w_value,
    w_query,
    arrived,
):
    fetch_value = pltpu.make_async_copy(value_hbm, w_value, arrived.at[0])
    fetch_query = pltpu.make_async_copy(query_hbm, w_query, arrived.at[1])
    fetch_value.start()
    fetch_query.start()
    squares = jnp.zeros((BLOCK, CHUNK), F32)
    for f in range(WIDTH // CHUNK):
        lanes = slice(f * CHUNK, (f + 1) * CHUNK)
        activ = whole[f % 2, f // 2].astype(F32)
        squares = squares + activ * activ
        gained[:, lanes] = (activ * gain[:, lanes]).astype(BF16)
    scale = lax.rsqrt(jnp.sum(squares, axis=1, keepdims=True) / WIDTH + 1e-06)
    row_scale[...] = jnp.broadcast_to(scale, (BLOCK, CHUNK))
    rows = gained[...]
    rank_part = dot(rows, w_down[...], LAST) * scale

    at = index[0]
    own = seg_ids[pl.ds(at, 1), :].astype(F32)
    before = seg_ids[pl.ds(jnp.maximum(at - 1, 0), 1), :].astype(F32)
    before = jnp.where(at > 0, before, -1.0)
    following = seg_ids[pl.ds(jnp.minimum(at + 1, BLOCKS - 1), 1), :].astype(F32)
    own = jnp.broadcast_to(own, (8, BLOCK))
    before = jnp.broadcast_to(before, (8, BLOCK))
    lane = lax.broadcasted_iota(jnp.int32, (8, BLOCK), 1)
    parts = [own]
    for j in range(1, 4):
        parts.append(jnp.where(lane < j, pltpu.roll(before, j, 1), pltpu.roll(own, j, 1)))
    before = jnp.broadcast_to(before[:, BLOCK - 1 :], (8, BLOCK))
    last = jnp.broadcast_to(own[:, BLOCK - 1 :], (8, BLOCK))
    parts += [before, last]
    parts.append(jnp.zeros((BLOCK - 8 * len(parts), BLOCK), F32))
    columns = jnp.transpose(jnp.concatenate(parts, axis=0))
    columns_out[...] = columns
    own_rows[...] = own

    logits = dot(rank_part, w_up[...].astype(F32), precision=HIGHEST) + bias[...]
    log_decay = (jnp.minimum(logits, 0.0) - jnp.log(1.0 + jnp.exp(-jnp.abs(logits)))) / 16.0
    row_iota = lax.broadcasted_iota(jnp.int32, (BLOCK, BLOCK), 0)
    col_iota = lax.broadcasted_iota(jnp.int32, (BLOCK, BLOCK), 1)
    lower = jnp.where(row_iota >= col_iota, 1.0, 0.0).astype(F32)
    cum = dot(lower, log_decay, precision=HIGHEST)
    cumulated[...] = cum

    of_keys = dot(rows, w_key[...]) * scale
    fetch_value.wait()
    of_values = dot(rows, w_value[...]) * scale
    pre_k[...] = of_keys
    pre_v[...] = of_values
    sums_k = conv(of_keys, None, taps_k, extended_k, columns)
    sums_v = conv(of_values, None, taps_v, extended_v, columns)
    next_k = onward(of_keys, taps_k, own, following)
    next_v = onward(of_values, taps_v, own, following)
    final = cum[BLOCK - 1 :, :]
    factors = jnp.where(columns[:, 0:1] == columns[:, 40:41], jnp.exp(final - cum), 0.0)
    later = lax.broadcasted_iota(jnp.int32, (BLOCK, HEAD_K), 0) >= 3
    pushed = jnp.where(later, silu(sums_k) * factors, 0.0)
    state = dot(silu(sums_v).astype(BF16), pushed.astype(BF16), FIRST)
    keep = jnp.where(before[0:1, 0:1] == last[0:1, 0:1], jnp.exp(final), 0.0)
    high, low = halves(keep)
    lane = lax.broadcasted_iota(jnp.int32, (1, LANES), 1)
    mixed_v = []
    for upper in range(2):
        mine = (lane >= LANES // 2) == (upper == 1)
        mixed_v.append(
            [
                jnp.where(mine, sums_v[t : t + 1, :], pltpu.roll(next_v[t], LANES // 2, 1))
                for t in range(3)
            ]
        )
    for h in range(2):
        lanes = slice(h * LANES, (h + 1) * LANES)
        rows_b = {0: high.astype(F32)[:, lanes], 1: low.astype(F32)[:, lanes]}
        for t in range(3):
            rows_b[2 + t] = sums_k[t : t + 1, lanes]
            rows_b[5 + t] = next_k[t][:, lanes]
        tile_b = stacked_rows(rows_b)
        for upper in range(2):
            rows_c = {2 + t: factors[t : t + 1, lanes] for t in range(3)}
            rows_c.update({5 + t: mixed_v[upper][t] for t in range(3)})
            tile_c = stacked_rows(rows_c)
            for j in range(8):
                g = 8 * upper + j
                p = h * BLOCKS // 2 + g
                pieces[p, 0:PIECE, :] = state[g * PIECE : (g + 1) * PIECE, lanes].astype(BF16)
                pieces[p, PIECE : PIECE + 8, :] = tile_b
                pieces[p, PIECE + 8 :, :] = tile_c
    fetch_query.wait()
    of_queries = dot(rows, w_query[...]) * scale
    pre_q[...] = of_queries
    tail[:, :HEAD_K] = of_queries[BLOCK - 8 :, :].astype(BF16)
    tail[:, HEAD_K : 2 * HEAD_K] = of_keys[BLOCK - 8 :, :].astype(BF16)
    tail[:, 2 * HEAD_K :] = of_values[BLOCK - 8 :, :].astype(BF16)


HALVES = (8, 16, 32, 64)
GROUPS = (BLOCK // 8, 8, HEAD_K)


def ahead(gained, row_scale, w_gate, head_gain, cumulated, left, gate, factors):
    del left
    cum = cumulated[...]
    for i, half in enumerate(HALVES):
        anchors = [
            jnp.broadcast_to(cum[b + half - 1 : b + half, :], (2 * half, HEAD_K))
            for b in range(0, BLOCK, 2 * half)
        ]
        anchor = jnp.concatenate(anchors, axis=0) if len(anchors) > 1 else anchors[0]
        factors[i] = jnp.exp(-jnp.abs(cum - anchor))
    cum_g = cum.reshape(GROUPS)
    for by in range(1, 8):
        spread = jnp.minimum(cum_g - pltpu.roll(cum_g, by, 1), 0.0)
        factors[3 + by] = jnp.exp(spread).reshape(BLOCK, HEAD_K)
    factors[11] = jnp.exp(cum)
    gate[...] = silu(dot(gained[...], w_gate[...]) * row_scale[...]) * head_gain[...]


def block_attention(
    pre_q,
    pre_k,
    pre_v,
    edge,
    taps_q,
    taps_k,
    taps_v,
    factors,
    columns,
    own_rows,
    left,
    intra,
    reach,
    extended,
    extended_v,
):
    del left
    edges = edge[...].astype(F32)
    queries = silu(conv(pre_q[...], edges[:, :HEAD_K], taps_q, extended.at[0], columns))
    queries = queries * HEAD_K ** (-0.5)
    keys = silu(
        conv(pre_k[...], edges[:, HEAD_K : 2 * HEAD_K], taps_k, extended.at[1], columns)
    )
    values = silu(conv(pre_v[...], edges[:, 2 * HEAD_K :], taps_v, extended_v, columns))
    seg = columns[:, 0:1]
    row_iota = lax.broadcasted_iota(jnp.int32, (BLOCK, BLOCK), 0)
    col_iota = lax.broadcasted_iota(jnp.int32, (BLOCK, BLOCK), 1)
    reach[...] = jnp.where(seg == columns[:, 32:33], queries * factors[11], 0.0)
    weights = jnp.zeros((BLOCK, BLOCK), F32)
    for i, half in enumerate(HALVES):
        factor = factors[i]
        part = dot((queries * factor).astype(BF16), (keys * factor).astype(BF16), LAST)
        inside = (
            (row_iota // (2 * half) == col_iota // (2 * half))
            & (row_iota % (2 * half) >= half)
            & (col_iota % (2 * half) < half)
        )
        weights = jnp.where(inside, part, weights)
    keys_g, queries_g = keys.reshape(GROUPS), queries.reshape(GROUPS)
    for by in range(8):
        if by:
            product = queries_g * pltpu.roll(keys_g, by, 1) * factors[3 + by].reshape(GROUPS)
        else:
            product = queries_g * keys_g
        sums = jnp.sum(product.reshape(BLOCK, HEAD_K), axis=1, keepdims=True)
        inside = (row_iota - col_iota == by) & (row_iota % 8 >= by)
        weights = jnp.where(inside, sums, weights)
    visible = (seg == own_rows[0:1, :]) & (row_iota >= col_iota)
    weights = jnp.where(visible, weights, 0.0)
    intra[...] = dot(weights.astype(BF16), values.astype(BF16))


def scan_blocks(index, pieces, states, left):
    owner = (index[0] % ROWS_Y) * ROWS_X + index[0] // ROWS_Y
    first = (owner % (BLOCKS // 2)) * PIECE
    order = [(block % ROWS_Y) * ROWS_X + block // ROWS_Y for block in range(BLOCKS)]
    shape = (BLOCKS, 8, LANES)
    tiles_b = jnp.stack([pieces[at, PIECE : PIECE + 8, :].astype(F32) for at in order])
    tiles_c = jnp.stack([pieces[at, PIECE + 8 :, :].astype(F32) for at in order])
    nothing = jnp.zeros((1, 8, LANES), F32)
    back_b = jnp.concatenate([nothing, tiles_b[:-1]], axis=0)
    back_c = jnp.concatenate([nothing, tiles_c[:-1]], axis=0)
    pushed = silu(tiles_b + pltpu.roll(back_b, 5, 1)) * tiles_c
    values = pltpu.roll(silu(tiles_c + pltpu.roll(back_c, LANES // 2, 2)), 5, 1)
    row = lax.broadcasted_iota(jnp.int32, shape, 1)
    values = jnp.where((row >= 2) & (row < 5), values, 0.0)
    rows = BLOCKS * 8
    lane = lax.broadcasted_iota(jnp.int32, (PIECE, LANES), 1)
    chosen = lane == lax.broadcasted_iota(jnp.int32, (PIECE, LANES), 0) + first
    chosen = jnp.where(chosen, 1.0, 0.0).astype(BF16)
    mine = dot(chosen, values.reshape(rows, LANES).astype(BF16), LAST)
    same = lax.broadcasted_iota(jnp.int32, (rows, rows), 0) // 8
    same = same == lax.broadcasted_iota(jnp.int32, (rows, rows), 1) // 8
    spread = jnp.where(same, jnp.concatenate([mine] * BLOCKS, axis=0), 0.0)
    added = dot(spread.astype(BF16), pushed.reshape(rows, LANES).astype(BF16))
    state = jnp.zeros((PIECE, LANES), F32)
    for block, at in enumerate(order):
        states[at] = state.astype(BF16)
        decay = tiles_b[block, 0:1, :] + tiles_b[block, 1:2, :]
        own = pieces[at, 0:PIECE, :].astype(F32) + added[block * 8 : block * 8 + 8, :]
        state = state * decay + own
    left[...] = state


def attend(index, intra, reach, incoming, gate, w_out, kept, kept_squares, sent):
    high, low = halves(reach[...])
    state = jnp.concatenate([incoming[0], incoming[1]], axis=1)
    attended = intra[...] + dot(high, state, LAST) + dot(low, state, LAST)
    squares = dot(jnp.ones((8, CHUNK), F32), attended * attended, LAST, precision=HIGHEST)
    terms = dot((attended * gate[...]).astype(BF16), w_out[...])
    first = index[0] == 0
    for j in range(8):
        even = terms[:, (2 * j) * CHUNK : (2 * j + 1) * CHUNK]
        odd = terms[:, (2 * j + 1) * CHUNK : (2 * j + 2) * CHUNK]
        kept[j] = jnp.where(first, even, odd)
        sent[j * BLOCK : (j + 1) * BLOCK, :] = jnp.where(first, odd, even).astype(BF16)
    kept_squares[...] = squares
    sent[8 * BLOCK :, :] = pair_rows(squares[0:1, :])


def pair_sum(index, kept, kept_squares, both, sent):
    received = both.at[1 - index[0]]
    other = received[8 * BLOCK :, :].astype(F32)
    squares = pair_rows(kept_squares[0:1, :] + other[0:1, :] + other[1:2, :])
    for j in range(8):
        terms = kept[j] + received[j * BLOCK : (j + 1) * BLOCK, :].astype(F32)
        sent[j, 0:BLOCK, :] = terms.astype(BF16)
        sent[j, BLOCK:, :] = squares


def finish(received, hidden, mixed):
    parts = []
    for r in range(4):
        pair = received[2 * r, BLOCK:, :].astype(F32) + received[2 * r + 1, BLOCK:, :].astype(F32)
        squares = pair[0:1, :] + pair[1:2, :]
        scale = lax.rsqrt(squares / HEAD_V + 1e-05)
        parts.append(jnp.broadcast_to(scale, (8, BLOCK)))
    parts.append(jnp.zeros((BLOCK - 8 * len(parts), BLOCK), F32))
    columns = jnp.transpose(jnp.concatenate(parts, axis=0))
    total = hidden[...].astype(F32)
    for r in range(4):
        terms = received[2 * r, 0:BLOCK, :].astype(F32)
        terms = terms + received[2 * r + 1, 0:BLOCK, :].astype(F32)
        total = total + columns[:, 8 * r : 8 * r + 1] * terms
    mixed[...] = total.astype(BF16)


def shards(
    hidden_in,
    seg_ids,
    norm_gain,
    w_query,
    w_key,
    w_value,
    w_gate,
    w_decay_down,
    w_decay_up,
    decay_bias,
    conv_query,
    conv_key,
    conv_value,
    head_gain,
    w_out,
):
    block = lax.axis_index("x") * ROWS_Y + lax.axis_index("y")
    block_at = jnp.reshape(block, (1,)).astype(jnp.int32)
    core_at = jnp.reshape(lax.axis_index("core"), (1,)).astype(jnp.int32)

    needed = (
        hidden_in,
        norm_gain.reshape(1, WIDTH),
        w_decay_down.T,
        w_decay_up,
        decay_bias.reshape(1, HEAD_K),
        seg_ids.reshape(BLOCKS, BLOCK),
        conv_query,
        conv_key,
        conv_value,
    )
    hidden, gain, down, up, bias, segs, taps_q, taps_k, taps_v, copies = local_call(
        fetch_and_spread,
        [*((a.shape, a.dtype) for a in needed), ((8, BLOCK, CHUNK), BF16)],
        block_at,
        core_at,
        *needed,
        scratch=[pltpu.SemaphoreType.DMA((len(needed),))],
        scalars=2,
        anywhere=range(2, 2 + len(needed)),
    )
    of_core = lax.all_to_all(copies, CHIPS, 0, 0)
    whole = lax.all_gather(of_core, "core", axis=0)
    pieces, tail, gained, row_scale, pre_q, pre_k, pre_v, cumulated, columns, own_rows = local_call(
        block_state,
        [
            ((BLOCKS, PIECE + 16, LANES), BF16),
            ((8, 2 * HEAD_K + CHUNK), BF16),
            ((BLOCK, WIDTH), BF16),
            ((BLOCK, CHUNK), F32),
            ((BLOCK, HEAD_K), F32),
            ((BLOCK, HEAD_K), F32),
            ((BLOCK, CHUNK), F32),
            ((BLOCK, HEAD_K), F32),
            ((BLOCK, BLOCK), F32),
            ((8, BLOCK), F32),
        ],
        block_at,
        whole,
        gain,
        w_value,
        w_query,
        w_key,
        down,
        up,
        bias,
        segs,
        taps_k,
        taps_v,
        scratch=[
            pltpu.VMEM((BLOCK + 8, HEAD_K), F32),
            pltpu.VMEM((BLOCK + 8, CHUNK), F32),
            pltpu.VMEM((WIDTH, CHUNK), BF16),
            pltpu.VMEM((WIDTH, HEAD_K), BF16),
            pltpu.SemaphoreType.DMA((2,)),
        ],
        scalars=1,
        anywhere=(3, 4),
    )
    edge = lax.ppermute(tail, SEQ, [(i, i + 1) for i in range(BLOCKS - 1)])
    owned = lax.all_to_all(pieces, GRID, 0, 0)
    states, left = local_call(
        scan_blocks,
        [((BLOCKS, PIECE, LANES), BF16), ((PIECE, LANES), F32)],
        block_at,
        owned,
        scalars=1,
    )
    incoming = lax.all_to_all(states, GRID, 0, 0).reshape(2, CHUNK, LANES)
    gate, factors = local_call(
        ahead,
        [((BLOCK, CHUNK), F32), ((12, BLOCK, HEAD_K), F32)],
        gained,
        row_scale,
        w_gate,
        head_gain.reshape(1, CHUNK),
        cumulated,
        left,
    )
    intra, reach = local_call(
        block_attention,
        [((BLOCK, CHUNK), F32), ((BLOCK, HEAD_K), F32)],
        pre_q,
        pre_k,
        pre_v,
        edge,
        taps_q,
        taps_k,
        taps_v,
        factors,
        columns,
        own_rows,
        left,
        scratch=[
            pltpu.VMEM((2, BLOCK + 8, HEAD_K), F32),
            pltpu.VMEM((BLOCK + 8, CHUNK), F32),
        ],
    )
    mine, my_squares, sent = local_call(
        attend,
        [((8, BLOCK, CHUNK), F32), ((8, BLOCK), F32), ((8 * BLOCK + 8, CHUNK), BF16)],
        core_at,
        intra,
        reach,
        incoming,
        gate,
        w_out,
        scalars=1,
    )
    both = lax.all_gather(sent, "core", axis=0)
    (pairs,) = local_call(
        pair_sum, [((8, BLOCK + 8, CHUNK), BF16)], core_at, mine, my_squares, both, scalars=1
    )
    arrived = lax.all_to_all(pairs, CHIPS, 0, 0)
    (mixed,) = local_call(
        finish, [((BLOCK, CHUNK), BF16)], arrived, hidden, last=True
    )
    return mixed


def solution(mesh):
    finer = Mesh(mesh.devices.reshape(ROWS_X, ROWS_Y, 4, 2, 2), ("x", "y", "row", "zhi", "core"))
    part = ("row", "zhi", "core")
    return jax.shard_map(
        shards,
        mesh=finer,
        in_specs=(
            P(SEQ, part),
            P(),
            P(),
            P(None, "row"),
            P(None, "row"),
            P(None, part),
            P(None, part),
            P(),
            P(None, "row"),
            P("row"),
            P(None, "row"),
            P(None, "row"),
            P(None, part),
            P(("zhi", "core")),
            P(part, None),
        ),
        out_specs=P(SEQ, part),
        check_vma=False,
    )
```
